32 devices in a mesh: seq: 4 (over x, core), dp: 8 (over z, y).
Axes of the slice: x: 2, y: 2, z: 4, core: 2. Of those that a mesh axis runs over, the one named last changes fastest.
Arguments:
- x_in: bfloat16 [8, 1536, 1024], P('dp', 'seq'), may hold values from -6 to 6
- cu_seqlens: int32 [8, 4], P('dp'), may hold values from 0 to 1536, as said below
- positions: int32 [8, 1536], P('dp', 'seq'), may hold values from 0 to 1535, as said below
- cotangent: bfloat16 [8, 1536, 1024], P('dp', 'seq'), may hold values from -6 to 6
- w_in: bfloat16 [1024, 3072], P('dp'), may hold values from -0.1875 to 0.1875
- conv_w: bfloat16 [3, 1024], P(None, 'dp'), may hold values from -3 to 3
- w_out: bfloat16 [1024, 1024], P('dp'), may hold values from -0.1875 to 0.1875
- w_gate1: bfloat16 [1024, 4608], P('dp'), may hold values from -0.1875 to 0.1875
- w_up1: bfloat16 [1024, 4608], P('dp'), may hold values from -0.1875 to 0.1875
- w_down1: bfloat16 [1024, 4608], P('dp'), may hold values from -0.09375 to 0.09375
- g_mix1: bfloat16 [1024], P('dp'), may hold values from 0.25 to 1.75
- g_ffn1: bfloat16 [1024], P('dp'), may hold values from 0.25 to 1.75
- w_q: bfloat16 [1024, 1024], P('dp'), may hold values from -0.1875 to 0.1875
- key_projection_weight: bfloat16 [1024, 512], P('dp'), may hold values from -0.1875 to 0.1875
- value_projection_weight: bfloat16 [1024, 512], P('dp'), may hold values from -0.1875 to 0.1875
- w_o: bfloat16 [1024, 1024], P('dp'), may hold values from -0.75 to 0.75
- g_q: bfloat16 [64], P('dp'), may hold values from 0.25 to 1.75
- g_k: bfloat16 [64], P('dp'), may hold values from 0.25 to 1.75
- w_gate2: bfloat16 [1024, 4608], P('dp'), may hold values from -0.1875 to 0.1875
- w_up2: bfloat16 [1024, 4608], P('dp'), may hold values from -0.1875 to 0.1875
- w_down2: bfloat16 [1024, 4608], P('dp'), may hold values from -0.09375 to 0.09375
- g_attn2: bfloat16 [1024], P('dp'), may hold values from 0.25 to 1.75
- g_ffn2: bfloat16 [1024], P('dp'), may hold values from 0.25 to 1.75
Outputs:
- out: bfloat16 [8, 1536, 1024], P('dp', 'seq')
- d_x: float32 [8, 1536, 1024], P('dp', 'seq')
- d_w_in: float32 [1024, 3072], P('dp')
- d_conv_w: float32 [3, 1024], P(None, 'dp')
- d_w_out: float32 [1024, 1024], P('dp')
- d_w_gate1: float32 [1024, 4608], P('dp')
- d_w_up1: float32 [1024, 4608], P('dp')
- d_w_down1: float32 [1024, 4608], P('dp')
- d_g_mix1: float32 [1024], P('dp')
- d_g_ffn1: float32 [1024], P('dp')
- d_w_q: float32 [1024, 1024], P('dp')
- d_w_k: float32 [1024, 512], P('dp')
- d_w_v: float32 [1024, 512], P('dp')
- d_w_o: float32 [1024, 1024], P('dp')
- d_g_q: float32 [64], P('dp')
- d_g_k: float32 [64], P('dp')
- d_w_gate2: float32 [1024, 4608], P('dp')
- d_w_up2: float32 [1024, 4608], P('dp')
- d_w_down2: float32 [1024, 4608], P('dp')
- d_g_attn2: float32 [1024], P('dp')
- d_g_ffn2: float32 [1024], P('dp')
The draws below stay inside these ranges and needn't reach their ends.
Inputs may be any that keep to these rules, and one draw needn't show every extreme that they name: Row r holds n documents, 1 <= n <= 3; document j is tokens cu_seqlens[r, j] to cu_seqlens[r, j + 1] - 1 for j < n; cu_seqlens[r, 0] is 0, cu_seqlens[r, n] is 1536, later entries are 0; each document has 512 tokens or more. Some row holds 3 documents and some row one. positions[r, t] is t minus the first token of t's document.
All inputs are finite; a program needn't handle non-finite values.
Results may differ from the reference program's by a relative error of at most 0.03.
Values may be sent and summed in bfloat16 or wider, within the bound.
No kernel may reach another device: no remote copies, remote signals or barrier semaphores. Data moves between devices by JAX's collectives and lax.ppermute only.
A program may use at most 640 MiB of HBM per device.

```python
import jax
import jax.numpy as jnp
from jax import lax

MODEL_WIDTH = 1024
FF = 4608
HQ = 16
KEY_VALUE_HEADS = 8
HEAD_SIZE = 64
KERNEL = 3
ROW_LEN = 1536
DOC_MIN = 512
ROWS = 8
DOCS_MAX = 3


def layout(key):
    base = jax.random.fold_in(key, 7)
    count_key, pick_key, cut_key = jax.random.split(base, 3)
    counts = jax.random.randint(count_key, (ROWS,), 1, DOCS_MAX + 1)
    order = jax.random.permutation(pick_key, ROWS)
    counts = counts.at[order[0]].set(DOCS_MAX).at[order[1]].set(1)
    spare = ROW_LEN - counts * DOC_MIN
    cuts = jax.random.randint(cut_key, (ROWS, DOCS_MAX - 1), 0, spare[:, None] + 1)
    slots = jnp.arange(DOCS_MAX - 1)
    cuts = jnp.where(slots[None, :] < counts[:, None] - 1, cuts, spare[:, None])
    cuts = jnp.sort(cuts, axis=-1)
    later = jnp.arange(1, DOCS_MAX + 1)
    inner = later[None, :] * DOC_MIN + jnp.pad(cuts, ((0, 0), (0, 1)))
    ending = jnp.where(later[None, :] == counts[:, None], ROW_LEN, 0)
    bounds = jnp.where(later[None, :] < counts[:, None], inner, ending)
    starts = jnp.zeros((ROWS, 1), jnp.int32)
    return (jnp.concatenate([starts, bounds.astype(jnp.int32)], axis=1), counts.astype(jnp.int32))


def draw_cu_seqlens(key, part):
    bounds, counts = layout(key)
    return bounds


def draw_positions(key, part):
    bounds, counts = layout(key)
    places = jnp.arange(ROW_LEN, dtype=jnp.int32)
    later = jnp.arange(DOCS_MAX + 1, dtype=jnp.int32)
    valid = later[None, :] < counts[:, None]
    reached = valid[:, None, :] & (bounds[:, None, :] <= places[None, :, None])
    first = jnp.max(jnp.where(reached, bounds[:, None, :], 0), -1)
    return (places[None, :] - first).astype(jnp.int32)


def with_spikes(drawn, stream_key, source, target, shards_of, factor):
    owner, partner = [(jnp.arange(drawn.shape[axis_at]) // (drawn.shape[axis_at] // shards_of)).reshape([-1 if axis == axis_at else 1 for axis in range(drawn.ndim)]) for axis_at in (source, target)]
    chosen = jax.random.permutation(stream_key, shards_of)[partner]
    strong = (owner == chosen) | (owner == (partner + shards_of // 2) % shards_of)
    return jnp.where(strong, factor * drawn, drawn)


def steps_of(stream_key, dims, shards, least, high):
    def one(axis_at, shards_of):
        steps = jax.random.uniform(jax.random.fold_in(jax.random.fold_in(stream_key, 6), axis_at), (shards_of,), jnp.float32, least / len(shards), high / len(shards))
        return jnp.repeat(jnp.exp(steps), dims[axis_at] // shards_of).reshape((-1,) + (1,) * (len(dims) - axis_at - 1))

    level = one(*shards[0])
    for cut in shards[1:]:
        level = level * one(*cut)
    return level


def bell_draw(rng, shape, deviation, bound, cuts=(), kind=jnp.bfloat16):
    drawn = jax.random.normal(rng, shape, jnp.float32) * deviation
    if len(cuts) > 0:
        drawn = steps_of(rng, shape, cuts, -0.22, 0.18) * drawn
    return jnp.clip(drawn, min=-bound, max=bound).astype(kind)


def noise_with(stream_key, shape, deviation, most, cuts, heavy, held_as=jnp.bfloat16):
    result = deviation * jax.random.normal(stream_key, shape, jnp.float32)
    if cuts:
        result = result * steps_of(stream_key, shape, cuts, -0.22, 0.18)
    return jnp.clip(with_spikes(result, jax.random.fold_in(stream_key, 3), *heavy), -most, most).astype(held_as)


def setup_inputs(seed: int = 0) -> dict:
    streams_of = jax.random.split(jax.random.key(seed), 24)
    return {
        "x_in": noise_with(streams_of[0], (ROWS, ROW_LEN, MODEL_WIDTH), 1.0, 6.0, ((0, 8), (1, 4)), (0, 2, 8, 2.0)),
        "cu_seqlens": draw_cu_seqlens(jax.random.fold_in(streams_of[23], 71), 0),
        "positions": draw_positions(jax.random.fold_in(streams_of[23], 71), 0),
        "cotangent": noise_with(streams_of[3], (ROWS, ROW_LEN, MODEL_WIDTH), 1.0, 6.0, ((0, 8), (1, 4)), (0, 2, 8, 2.0)),
        "w_in": bell_draw(streams_of[4], (MODEL_WIDTH, 3 * MODEL_WIDTH), MODEL_WIDTH ** -0.5, 0.1875, ((0, 8),)),
        "conv_w": bell_draw(streams_of[5], (KERNEL, MODEL_WIDTH), 0.6, 3.0, ((1, 8),)),
        "w_out": bell_draw(streams_of[6], (MODEL_WIDTH, MODEL_WIDTH), MODEL_WIDTH ** -0.5, 0.1875, ((0, 8),)),
        "w_gate1": bell_draw(streams_of[7], (MODEL_WIDTH, FF), MODEL_WIDTH ** -0.5, 0.1875, ((0, 8),)),
        "w_up1": bell_draw(streams_of[8], (MODEL_WIDTH, FF), MODEL_WIDTH ** -0.5, 0.1875, ((0, 8),)),
        "w_down1": bell_draw(streams_of[9], (MODEL_WIDTH, FF), FF ** -0.5, 0.09375, ((0, 8),)),
        "g_mix1": jnp.clip(1.0 + 0.15 * jax.random.normal(streams_of[10], (MODEL_WIDTH,), jnp.float32), 0.25, 1.75).astype(jnp.bfloat16),
        "g_ffn1": jnp.clip(1.0 + 0.15 * jax.random.normal(streams_of[11], (MODEL_WIDTH,), jnp.float32), 0.25, 1.75).astype(jnp.bfloat16),
        "w_q": bell_draw(streams_of[12], (MODEL_WIDTH, HQ * HEAD_SIZE), MODEL_WIDTH ** -0.5, 0.1875, ((0, 8),)),
        "key_projection_weight": bell_draw(streams_of[13], (MODEL_WIDTH, KEY_VALUE_HEADS * HEAD_SIZE), MODEL_WIDTH ** -0.5, 0.1875, ((0, 8),)),
        "value_projection_weight": bell_draw(streams_of[14], (MODEL_WIDTH, KEY_VALUE_HEADS * HEAD_SIZE), MODEL_WIDTH ** -0.5, 0.1875, ((0, 8),)),
        "w_o": bell_draw(streams_of[15], (HQ * HEAD_SIZE, MODEL_WIDTH), (HQ * HEAD_SIZE // 16) ** -0.5, 0.75, ((0, 8),)),
        "g_q": jnp.clip(1.0 + 0.15 * jax.random.normal(streams_of[16], (HEAD_SIZE,), jnp.float32), 0.25, 1.75).astype(jnp.bfloat16),
        "g_k": jnp.clip(1.0 + 0.15 * jax.random.normal(streams_of[17], (HEAD_SIZE,), jnp.float32), 0.25, 1.75).astype(jnp.bfloat16),
        "w_gate2": bell_draw(streams_of[18], (MODEL_WIDTH, FF), MODEL_WIDTH ** -0.5, 0.1875, ((0, 8),)),
        "w_up2": bell_draw(streams_of[19], (MODEL_WIDTH, FF), MODEL_WIDTH ** -0.5, 0.1875, ((0, 8),)),
        "w_down2": bell_draw(streams_of[20], (MODEL_WIDTH, FF), FF ** -0.5, 0.09375, ((0, 8),)),
        "g_attn2": jnp.clip(1.0 + 0.15 * jax.random.normal(streams_of[21], (MODEL_WIDTH,), jnp.float32), 0.25, 1.75).astype(jnp.bfloat16),
        "g_ffn2": jnp.clip(1.0 + 0.15 * jax.random.normal(streams_of[22], (MODEL_WIDTH,), jnp.float32), 0.25, 1.75).astype(jnp.bfloat16),
    }


EPS = 1e-05
THETA = 1000000.0
NEG = -1e+30

@jax.custom_vjp
def low(v):
    return lax.optimization_barrier(v.astype(jnp.bfloat16)).astype(jnp.float32)

@jax.custom_vjp
def low_back(v):
    return v

def low_keep(v):
    return (low(v), None)

def low_pass(kept, grad):
    return (grad,)

def back_keep(v):
    return (v, None)

def back_low(kept, grad):
    return (low(grad),)
low.defvjp(low_keep, low_pass)
low_back.defvjp(back_keep, back_low)

def matmul(left, right):
    return jnp.dot(left, right, precision=lax.Precision.HIGHEST)

def root_norm(value, gain):
    return value * lax.rsqrt(lax.optimization_barrier(jnp.mean(value * value, -1, keepdims=True)) + EPS) * gain

def doc_index(bounds, places):
    later = bounds[1:]
    passed = (later[None, :] <= places[:, None]) & (later[None, :] > 0)
    return lax.optimization_barrier(jnp.sum(passed.astype(jnp.int32), -1))

def rope_tables(places, head):
    half = head // 2
    freqs = THETA ** (-(2.0 * jnp.arange(half, dtype=jnp.float32)) / head)
    angles = places.astype(jnp.float32)[..., None] * freqs
    angles = jnp.concatenate([angles, angles], -1)
    return (jnp.cos(angles), jnp.sin(angles))

def rotate_half(value):
    half = value.shape[-1] // 2
    return jnp.concatenate([-value[..., half:], value[..., :half]], -1)

def rope_apply(value, cosine, sine):
    return value * cosine + rotate_half(value) * sine

def feed_forward(hidden, gain, w_gate, w_up, w_down):
    normed = low(root_norm(hidden, gain))
    gate = low_back(matmul(normed, w_gate))
    upper = low_back(matmul(normed, w_up))
    act = low(gate * jax.nn.sigmoid(gate) * upper)
    return low_back(jnp.dot(act, w_down.T, precision=lax.Precision.HIGHEST))

def forward_row(x_row, weights, bounds, places):
    w_in, conv_w, w_out, w_gate1, w_up1, w_down1, g_mix1, g_ffn1, w_q, key_projection_weight, value_projection_weight, w_o, g_q, g_k, w_gate2, w_up2, w_down2, g_attn2, g_ffn2 = weights
    length = x_row.shape[0]
    width = w_out.shape[0]
    head = g_q.shape[0]
    tokens_at = jnp.arange(length, dtype=jnp.int32)
    docs = doc_index(bounds, tokens_at)
    normed_mix = low(root_norm(x_row, g_mix1))
    projected = low_back(matmul(normed_mix, w_in))
    b_part = projected[:, :width]
    c_part = projected[:, width:2 * width]
    x_part = projected[:, 2 * width:]
    product = low_back(low(b_part * x_part))
    conv_out = conv_w[0] * product
    for tap in range(1, conv_w.shape[0]):
        shifted = jnp.pad(product, ((tap, 0), (0, 0)))[:length]
        before = jnp.pad(docs, (tap, 0))[:length]
        conv_out = conv_out + conv_w[tap] * shifted * (before == docs).astype(jnp.float32)[:, None]
    gated = low(c_part * conv_out)
    hidden_one = x_row + low_back(matmul(gated, w_out))
    hidden_two = hidden_one + feed_forward(hidden_one, g_ffn1, w_gate1, w_up1, w_down1)
    attn_in = low(root_norm(hidden_two, g_attn2))
    heads_q = w_q.shape[1] // head
    heads_kv = key_projection_weight.shape[1] // head
    query = low_back(matmul(attn_in, w_q)).reshape(length, heads_q, head)
    keys = low_back(matmul(attn_in, key_projection_weight)).reshape(length, heads_kv, head)
    values = low(low_back(matmul(attn_in, value_projection_weight))).reshape(length, heads_kv, head)
    cosine, sine = rope_tables(places, head)
    cosine = cosine[:, None, :]
    sine = sine[:, None, :]
    query = low_back(low(rope_apply(root_norm(query, g_q), cosine, sine)))
    keys = low_back(low(rope_apply(root_norm(keys, g_k), cosine, sine)))
    group = heads_q // heads_kv
    keys_wide = jnp.repeat(keys, group, axis=1)
    values_wide = jnp.repeat(values, group, axis=1)
    scores = low_back(jnp.einsum('qhd,khd->hqk', query, keys_wide, precision=lax.Precision.HIGHEST) * head ** (-0.5))
    allowed = (docs[:, None] == docs[None, :]) & (tokens_at[None, :] <= tokens_at[:, None])
    scores = jnp.where(allowed[None], scores, NEG)
    probs = low(jax.nn.softmax(scores, axis=-1))
    attended = jnp.einsum('hqk,khd->qhd', probs, values_wide, precision=lax.Precision.HIGHEST)
    attended = low_back(low(attended)).reshape(length, heads_q * head)
    hidden_three = hidden_two + low_back(matmul(attended, w_o))
    return hidden_three + feed_forward(hidden_three, g_ffn2, w_gate2, w_up2, w_down2)

def add_pair(first, second):
    return first + second

def reference(x_in, cu_seqlens, positions, cotangent, w_in, conv_w, w_out, w_gate1, w_up1, w_down1, g_mix1, g_ffn1, w_q, key_projection_weight, value_projection_weight, w_o, g_q, g_k, w_gate2, w_up2, w_down2, g_attn2, g_ffn2):
    weights = tuple((item.astype(jnp.float32) for item in (w_in, conv_w, w_out, w_gate1, w_up1, w_down1, g_mix1, g_ffn1, w_q, key_projection_weight, value_projection_weight, w_o, g_q, g_k, w_gate2, w_up2, w_down2, g_attn2, g_ffn2)))

    def one_row(totals, row):
        x_row, bounds, places, grad_row = row

        def apply(x_value, weight_values):
            return forward_row(x_value, weight_values, bounds, places)
        out_row, pullback = jax.vjp(apply, x_row.astype(jnp.float32), weights)
        grad_x, grad_weights = pullback(grad_row.astype(jnp.float32))
        totals = jax.tree.map(add_pair, totals, grad_weights)
        return (totals, (out_row.astype(jnp.bfloat16), grad_x))
    start_totals = jax.tree.map(jnp.zeros_like, weights)
    totals, (out, grad_x) = lax.scan(one_row, start_totals, (x_in, cu_seqlens, positions, cotangent))
    return (out, grad_x, totals[0], totals[1], totals[2], totals[3], totals[4], totals[5], totals[6], totals[7], totals[8], totals[9], totals[10], totals[11], totals[12], totals[13], totals[14], totals[15], totals[16], totals[17], totals[18])
```

```python
import jax
import jax.numpy as jnp
from jax import lax
from jax.experimental import pallas as pl
from jax.experimental.pallas import tpu as pltpu
from jax.sharding import PartitionSpec as P

EPS = 1e-05
THETA = 1000000.0
NEG = -1e30
F32 = jnp.float32
BF16 = jnp.bfloat16
TILE = 256
LANES = 128
VMEM_LIMIT = 56 << 20


def left_dot(left, right):
    return lax.dot_general(left, right, (((0,), (0,)), ((), ())), preferred_element_type=F32)


def right_dot(left, right):
    return lax.dot_general(left, right, (((1,), (1,)), ((), ())), preferred_element_type=F32)


def plain_dot(left, right):
    return jnp.dot(left, right, preferred_element_type=F32)


def unit_scale(value):
    scale = lax.rsqrt(jnp.mean(value * value, -1, keepdims=True) + EPS)
    return (value * scale, scale)


def norm_back(grad_out, gain, unit, scale):
    weighted = grad_out * gain
    grad_in = scale * (weighted - unit * jnp.mean(weighted * unit, -1, keepdims=True))
    gain_grad = jnp.sum((grad_out * unit).reshape(-1, unit.shape[-1]), 0)
    return (grad_in, gain_grad)


def doc_index(bounds, places):
    later = bounds[1:]
    passed = (later <= places[..., None]) & (later > 0)
    return jnp.sum(passed.astype(jnp.int32), -1)


def doc_starts(bounds, places):
    return jnp.max(jnp.where(bounds <= places[..., None], bounds, 0), -1)


def rope_tables(places, head):
    half = head // 2
    freqs = THETA ** (-(2.0 * jnp.arange(half, dtype=F32)) / head)
    angles = places.astype(F32)[:, None] * freqs
    cosine = jnp.cos(angles)
    sine = jnp.sin(angles)
    return (
        jnp.concatenate([cosine] * 4, 1),
        jnp.concatenate([-sine, sine, -sine, sine], 1),
    )


def seq_bits():
    size = lax.axis_size("seq")
    bits = []
    bit = 1
    while bit < size:
        bits.append(bit)
        bit = bit * 2
    return bits


def swap_seq(array, bit):
    size = lax.axis_size("seq")
    return lax.ppermute(array, "seq", [(i, i ^ bit) for i in range(size)])


def seq_gather(block):
    have = {0: block}
    for bit in reversed(seq_bits()):
        for place in sorted(have):
            have[place | bit] = swap_seq(have[place], bit)
    return jnp.concatenate([have[place] for place in sorted(have)], 0)


def seq_scatter(partial):
    size = lax.axis_size("seq")
    length = partial.shape[0] // size
    have = {place: partial[place * length : (place + 1) * length] for place in range(size)}
    for bit in seq_bits():
        for place in sorted(have, reverse=True):
            if place & bit:
                got = swap_seq(have.pop(place).astype(BF16), bit).astype(F32)
                have[place ^ bit] = have[place ^ bit] + got
    return have[0]


def flip_blocks(array):
    place = lax.axis_index("seq")
    for bit in seq_bits():
        shape = array.shape
        split = array.reshape((shape[0] // (2 * bit), 2, bit) + shape[1:])
        turned = jnp.concatenate([split[:, 1:], split[:, :1]], 1)
        array = jnp.where((place & bit) > 0, turned, split).reshape(shape)
    return array


def half_lanes(shape):
    return lax.broadcasted_iota(jnp.int32, shape, 1) < LANES // 2


def head_mean(value):
    row = lax.broadcasted_iota(jnp.int32, (LANES, LANES), 0) < LANES // 2
    column = half_lanes((LANES, LANES))
    ones = jnp.where(row == column, 2.0 / LANES, 0.0).astype(BF16)
    high = value.astype(BF16)
    low = (value - high.astype(F32)).astype(BF16)
    return plain_dot(high, ones) + plain_dot(low, ones)


def swap_quarters(value):
    quarter = LANES // 4
    lane = lax.broadcasted_iota(jnp.int32, value.shape, 1)
    first = (lane // quarter) % 2 == 0
    return jnp.where(
        first, pltpu.roll(value, LANES - quarter, 1), pltpu.roll(value, quarter, 1)
    )


def head_unit(value):
    scale = lax.rsqrt(head_mean(value * value) + EPS)
    return (value * scale, scale)


def pad_pair(value, second):
    lower = half_lanes(value.shape)
    if second:
        high = jnp.where(lower, 0.0, value)
        return (pltpu.roll(high, LANES // 2, 1), high)
    low = jnp.where(lower, value, 0.0)
    return (low, pltpu.roll(low, LANES // 2, 1))


def load_heads(raw_ref, cos_ref, sin_ref, gains_ref, source, target, length, pairs):
    rows = pl.ds(source, length)
    cosine = cos_ref[pl.ds(target, length), :]
    sine = sin_ref[pl.ds(target, length), :]
    groups = raw_ref.shape[1] // LANES

    def turned(group, gain):
        value = head_unit(raw_ref[rows, group * LANES : (group + 1) * LANES])[0] * gain
        return value * cosine + swap_quarters(value) * sine

    scale = (LANES // 2) ** (-0.5)
    queries = [(turned(g, gains_ref[0:1, :]) * scale).astype(BF16) for g in range(pairs)]
    keys = []
    values = []
    cached = {}
    for g in range(pairs):
        place = pairs * LANES + g * (LANES // 2)
        group, second = divmod(place, LANES)
        if group not in cached:
            cached[group] = turned(group, gains_ref[1:2, :]).astype(BF16).astype(F32)
        keys.append([k.astype(BF16) for k in pad_pair(cached[group], second > 0)])
        place = place + pairs * (LANES // 2)
        group, second = divmod(place, LANES)
        value = raw_ref[rows, group * LANES : (group + 1) * LANES]
        values.append([v.astype(BF16) for v in pad_pair(value, second > 0)])
    return (queries, keys, values)


def allowed_tile(start_ref, first_key, first_query):
    query = first_query + lax.broadcasted_iota(jnp.int32, (1, TILE), 1)
    start = start_ref[0:1, pl.ds(first_query, TILE)]
    key = first_key + lax.broadcasted_iota(jnp.int32, (TILE, TILE), 0)
    return (key >= start) & (key <= query)


def attention_forward_kernel(
    place_ref, raw_ref, cos_ref, sin_ref, start_ref, gains_ref,
    out_ref, wide_ref, total_ref, query_ref, key_ref, value_ref,
    *, length, pairs,
):
    full = raw_ref.shape[0]
    count = full // length
    place = place_ref[0]

    def prepare(block, _):
        target = pl.multiple_of(block * length, 8)
        source = pl.multiple_of((block ^ place) * length, 8)
        queries, keys, values = load_heads(
            raw_ref, cos_ref, sin_ref, gains_ref, source, target, length, pairs
        )
        for g in range(pairs):
            query_ref[g, pl.ds(target, length), :] = queries[g]
            for h in range(2):
                key_ref[2 * g + h, pl.ds(target, length), :] = keys[g][h]
                value_ref[2 * g + h, pl.ds(target, length), :] = values[g][h]
        return 0

    lax.fori_loop(0, count, prepare, 0)
    half = LANES // 2

    def query_tile(i, _):
        first_query = pl.multiple_of(i * TILE, TILE)

        def key_tile(j, carry):
            first_key = pl.multiple_of(j * TILE, TILE)
            allowed = allowed_tile(start_ref, first_key, first_query)
            sums, outs = carry
            new_sums = []
            new_outs = []
            for g in range(pairs):
                query = query_ref[g, pl.ds(first_query, TILE), :]
                total = outs[g]
                for h in range(2):
                    key = key_ref[2 * g + h, pl.ds(first_key, TILE), :]
                    value = value_ref[2 * g + h, pl.ds(first_key, TILE), :]
                    weight = jnp.where(allowed, jnp.exp(right_dot(key, query)), 0.0)
                    new_sums.append(sums[2 * g + h] + jnp.sum(weight, 0, keepdims=True))
                    total = total + lax.dot_general(
                        value, weight.astype(BF16), (((0,), (0,)), ((), ())),
                        preferred_element_type=F32,
                    )
                new_outs.append(total)
            return (new_sums, new_outs)

        carry = (
            [jnp.zeros((1, TILE), F32) for _ in range(2 * pairs)],
            [jnp.zeros((LANES, TILE), F32) for _ in range(pairs)],
        )
        sums, outs = lax.fori_loop(0, i + 1, key_tile, carry)
        columns = pl.ds(first_query, TILE)
        for g in range(pairs):
            scaled = jnp.concatenate(
                [outs[g][h * half : (h + 1) * half] / sums[2 * g + h] for h in range(2)], 0
            )
            for h in range(2):
                total_ref[2 * g + h : 2 * g + h + 1, columns] = sums[2 * g + h]
            wide_ref[g * LANES : (g + 1) * LANES, columns] = scaled
            query_ref[g, columns, :] = scaled.T.astype(BF16)
        return 0

    lax.fori_loop(0, full // TILE, query_tile, 0)

    def finish(block, _):
        source = pl.multiple_of(block * length, 8)
        target = pl.multiple_of((block ^ place) * length, 8)
        for g in range(pairs):
            out_ref[pl.ds(target, length), g * LANES : (g + 1) * LANES] = query_ref[
                g, pl.ds(source, length), :
            ]
        return 0

    lax.fori_loop(0, count, finish, 0)


def attention_backward_kernel(
    place_ref, raw_ref, cos_ref, sin_ref, start_ref, gains_ref, wide_ref, total_ref, grad_ref,
    out_ref, gain_grad_ref,
    query_ref, key_ref, value_ref, hold_ref, dq_ref, dk_ref, dv_ref,
    *, length, pairs,
):
    full = raw_ref.shape[0]
    count = full // length
    place = place_ref[0]
    half = LANES // 2

    def prepare(block, _):
        target = pl.multiple_of(block * length, 8)
        source = pl.multiple_of((block ^ place) * length, 8)
        queries, keys, values = load_heads(
            raw_ref, cos_ref, sin_ref, gains_ref, source, target, length, pairs
        )
        rows = pl.ds(target, length)
        for g in range(pairs):
            query_ref[g, rows, :] = queries[g]
            hold_ref[g, rows, :] = grad_ref[
                pl.ds(source, length), g * LANES : (g + 1) * LANES
            ]
            dk_ref[g, rows, :] = jnp.zeros((length, LANES), F32)
            dv_ref[g, rows, :] = jnp.zeros((length, LANES), F32)
            for h in range(2):
                key_ref[2 * g + h, rows, :] = keys[g][h]
                value_ref[2 * g + h, rows, :] = values[g][h]
        return 0

    lax.fori_loop(0, count, prepare, 0)
    lower = half_lanes((TILE, LANES))

    def query_tile(i, _):
        first_query = pl.multiple_of(i * TILE, TILE)
        columns = pl.ds(first_query, TILE)
        inverse = [1.0 / total_ref[n : n + 1, columns] for n in range(2 * pairs)]
        inner = []
        for g in range(pairs):
            grad = hold_ref[g, columns, :].astype(F32).T
            both = grad * wide_ref[g * LANES : (g + 1) * LANES, columns]
            for h in range(2):
                inner.append(jnp.sum(both[h * half : (h + 1) * half], 0, keepdims=True))

        def key_tile(j, outs):
            first_key = pl.multiple_of(j * TILE, TILE)
            rows = pl.ds(first_key, TILE)
            allowed = allowed_tile(start_ref, first_key, first_query)
            new_outs = []
            for g in range(pairs):
                query = query_ref[g, columns, :]
                grad = hold_ref[g, columns, :]
                zero = jnp.zeros_like(query)
                total = outs[g]
                d_key = dk_ref[g, rows, :]
                d_value = dv_ref[g, rows, :]
                for h in range(2):
                    keep = lower if h == 0 else jnp.logical_not(lower)
                    key = key_ref[2 * g + h, rows, :]
                    value = value_ref[2 * g + h, rows, :]
                    weight = jnp.exp(right_dot(key, query)) * inverse[2 * g + h]
                    weight = jnp.where(allowed, weight, 0.0)
                    d_weight = right_dot(value, grad)
                    d_score = (weight * (d_weight - inner[2 * g + h])).astype(BF16)
                    d_value = d_value + plain_dot(
                        weight.astype(BF16), jnp.where(keep, grad, zero)
                    )
                    d_key = d_key + plain_dot(d_score, jnp.where(keep, query, zero))
                    total = total + lax.dot_general(
                        key, d_score, (((0,), (0,)), ((), ())), preferred_element_type=F32
                    )
                dk_ref[g, rows, :] = d_key
                dv_ref[g, rows, :] = d_value
                new_outs.append(total)
            return new_outs

        outs = lax.fori_loop(
            0, i + 1, key_tile, [jnp.zeros((LANES, TILE), F32) for _ in range(pairs)]
        )
        for g in range(pairs):
            dq_ref[g, columns, :] = outs[g].T
        return 0

    lax.fori_loop(0, full // TILE, query_tile, 0)
    scale = half ** (-0.5)

    def finish(block, carry):
        source = pl.multiple_of(block * length, 8)
        target = pl.multiple_of((block ^ place) * length, 8)
        rows = pl.ds(source, length)
        cosine = cos_ref[rows, :]
        sine = sin_ref[rows, :]
        low = half_lanes((length, LANES))

        def back(grad, group, gain):
            grad = grad.astype(BF16).astype(F32)
            unit, inverse = head_unit(
                raw_ref[pl.ds(target, length), group * LANES : (group + 1) * LANES]
            )
            d_rot = grad * cosine + swap_quarters(grad * sine)
            weighted = d_rot * gain
            d_raw = inverse * (weighted - unit * head_mean(weighted * unit))
            return (d_raw, d_rot * unit)

        query_gain, key_gain = carry
        for g in range(pairs):
            d_raw, terms = back(dq_ref[g, rows, :] * scale, g, gains_ref[0:1, :])
            query_gain = query_gain + jnp.sum(terms, 0, keepdims=True)
            out_ref[pl.ds(target, length), g * LANES : (g + 1) * LANES] = d_raw.astype(BF16)
        groups = {}
        for kind, held in ((0, dk_ref), (1, dv_ref)):
            for g in range(pairs):
                place_of = pairs * LANES + kind * pairs * half + g * half
                group, second = divmod(place_of, LANES)
                value = held[g, rows, :]
                value = value + pltpu.roll(value, half, 1)
                groups.setdefault(group, {})[second // half] = (kind, value)
        for group, parts in groups.items():
            merged = jnp.where(low, parts[0][1], parts[1][1])
            is_key = [parts[n][0] == 0 for n in range(2)]
            result = merged
            if any(is_key):
                d_raw, terms = back(merged, group, gains_ref[1:2, :])
                if not is_key[1]:
                    d_raw = jnp.where(low, d_raw, merged)
                    terms = jnp.where(low, terms, 0.0)
                result = d_raw
                key_gain = key_gain + jnp.sum(terms, 0, keepdims=True)
            out_ref[pl.ds(target, length), group * LANES : (group + 1) * LANES] = result.astype(
                BF16
            )
        return (query_gain, key_gain)

    zero = jnp.zeros((1, LANES), F32)
    query_gain, key_gain = lax.fori_loop(0, count, finish, (zero, zero))
    gain_grad_ref[0:1, :] = query_gain
    gain_grad_ref[1:2, :] = key_gain


def whole(count):
    return [pl.BlockSpec(memory_space=pltpu.VMEM)] * count


def attention_forward(place, raw, cosine, sine, start, gains, length):
    full, columns = raw.shape
    pairs = columns // (2 * LANES)
    return pl.pallas_call(
        lambda *refs: attention_forward_kernel(*refs, length=length, pairs=pairs),
        in_specs=[pl.BlockSpec(memory_space=pltpu.SMEM)] + whole(5),
        out_specs=tuple(whole(3)),
        out_shape=(
            jax.ShapeDtypeStruct((full, pairs * LANES), BF16),
            jax.ShapeDtypeStruct((pairs * LANES, full), F32),
            jax.ShapeDtypeStruct((8, full), F32),
        ),
        scratch_shapes=[
            pltpu.VMEM((pairs, full, LANES), BF16),
            pltpu.VMEM((2 * pairs, full, LANES), BF16),
            pltpu.VMEM((2 * pairs, full, LANES), BF16),
        ],
        compiler_params=pltpu.CompilerParams(vmem_limit_bytes=VMEM_LIMIT),
        name="attention_forward",
    )(place, raw, cosine, sine, start, gains)


def attention_backward(place, raw, cosine, sine, start, gains, wide, totals, grads, length):
    full, columns = raw.shape
    pairs = columns // (2 * LANES)
    return pl.pallas_call(
        lambda *refs: attention_backward_kernel(*refs, length=length, pairs=pairs),
        in_specs=[pl.BlockSpec(memory_space=pltpu.SMEM)] + whole(8),
        out_specs=tuple(whole(2)),
        out_shape=(
            jax.ShapeDtypeStruct((full, columns), BF16),
            jax.ShapeDtypeStruct((2, LANES), F32),
        ),
        scratch_shapes=[
            pltpu.VMEM((pairs, full, LANES), BF16),
            pltpu.VMEM((2 * pairs, full, LANES), BF16),
            pltpu.VMEM((2 * pairs, full, LANES), BF16),
            pltpu.VMEM((pairs, full, LANES), BF16),
            pltpu.VMEM((pairs, full, LANES), F32),
            pltpu.VMEM((pairs, full, LANES), F32),
            pltpu.VMEM((pairs, full, LANES), F32),
        ],
        compiler_params=pltpu.CompilerParams(vmem_limit_bytes=VMEM_LIMIT),
        name="attention_backward",
    )(place, raw, cosine, sine, start, gains, wide, totals, grads)

def column_block(weight, parts):
    size = lax.axis_size("seq")
    place = lax.axis_index("seq")
    rows, columns = weight.shape
    block = columns // parts // size
    split = weight.reshape(rows, parts, size * block)
    return lax.dynamic_slice_in_dim(split, place * block, block, 2).reshape(rows, parts * block)


def deal_pairs():
    size = lax.axis_size("seq")
    count = lax.axis_size("dp")
    pairs = []
    for place in range(size):
        for owner in range(count):
            source = (owner % size) * count + place * (count // size) + owner // size
            pairs.append((source, place * count + owner))
    return pairs


def deal_rows(weight):
    size = lax.axis_size("seq")
    place = lax.axis_index("seq")
    piece = weight.shape[0] // size
    part = lax.dynamic_slice_in_dim(weight, place * piece, piece, 0)
    return lax.ppermute(part, ("seq", "dp"), deal_pairs())


def undeal_rows(part):
    return lax.ppermute(part, ("seq", "dp"), [(b, a) for a, b in deal_pairs()])


def dp_gather(block):
    return lax.all_gather(block, "dp", axis=0, tiled=True)


def dp_scatter(grads):
    return lax.psum_scatter(grads, "dp", scatter_dimension=0, tiled=True)


def share(owned):
    size = lax.axis_size("seq")
    place = lax.axis_index("seq")
    everywhere = seq_gather(owned).reshape((size,) + owned.shape)
    return [lax.dynamic_index_in_dim(everywhere, place ^ i, 0, False) for i in range(size)]


def split_columns(blocks, parts):
    results = []
    offset = 0
    for split, columns in parts:
        pieces = []
        for number in range(split):
            start = offset + number * columns
            pieces = pieces + [block[:, start : start + columns] for block in blocks]
        results.append(jnp.concatenate(pieces, 1).astype(F32))
        offset = offset + split * columns
    return (results, [block[:, offset:] for block in blocks])


def ffn_gate(normed, weights):
    hidden = weights.shape[1] // 3
    both = plain_dot(normed, weights[:, : 2 * hidden])
    gate = both[:, :hidden]
    upper = both[:, hidden:]
    sigma = jax.nn.sigmoid(gate)
    act = (gate * sigma * upper).astype(BF16)
    return (gate, upper, act)


def ffn_back(grad_all, kept, normed_all, weights):
    gate, upper, act = kept
    hidden = weights.shape[1] // 3
    sigma = jax.nn.sigmoid(gate)
    d_down = left_dot(grad_all, act)
    d_act = plain_dot(grad_all, weights[:, 2 * hidden :])
    d_gate = (d_act * upper * sigma * (1.0 + gate * (1.0 - sigma))).astype(BF16)
    d_up = (d_act * gate * sigma).astype(BF16)
    d_both = jnp.concatenate([d_gate, d_up], 1)
    d_gate_up = left_dot(normed_all, d_both)
    partial = right_dot(d_both, weights[:, : 2 * hidden])
    grads = jnp.concatenate([d_gate_up.astype(BF16), d_down.astype(BF16)], 1)
    return (seq_scatter(partial), grads)


def local(
    x_in,
    cu_seqlens,
    positions,
    cotangent,
    w_in,
    conv_w,
    w_out,
    w_gate1,
    w_up1,
    w_down1,
    g_mix1,
    g_ffn1,
    w_q,
    key_projection_weight,
    value_projection_weight,
    w_o,
    g_q,
    g_k,
    w_gate2,
    w_up2,
    w_down2,
    g_attn2,
    g_ffn2,
):
    rows, length, width = x_in.shape
    assert rows == 1
    seq_count = lax.axis_size("seq")
    dp_count = lax.axis_size("dp")
    seq_place = lax.axis_index("seq")
    full = length * seq_count
    channels = width // seq_count
    slots = width // dp_count
    head = g_q.shape[0] * dp_count
    taps = conv_w.shape[0]
    reach = taps - 1

    x_all = seq_gather(x_in.reshape(length, width)).astype(F32)
    head_gains = jnp.pad(jnp.stack([g_q, g_k], 1), ((0, slots - head // dp_count), (0, 0)))
    small = jnp.concatenate(
        [conv_w.T, jnp.stack([g_mix1, g_ffn1, g_attn2, g_ffn2], 1), head_gains], 1
    )
    small = jnp.pad(small, ((0, 0), (0, 128 - small.shape[1])))
    dealt = deal_rows(jnp.stack([w_out, w_o], 1))
    out_piece = dealt[:, 0].reshape(slots, -1)
    o_piece = dealt[:, 1].reshape(slots, -1)
    mix_all = dp_gather(jnp.concatenate([column_block(w_in, 3), small, out_piece], 1))
    ffn_one = dp_gather(
        jnp.concatenate([column_block(w, 1) for w in (w_gate1, w_up1, w_down1)], 1)
    )
    attn_all = dp_gather(
        jnp.concatenate(
            [
                column_block(w_q, 1),
                column_block(key_projection_weight, 1),
                column_block(value_projection_weight, 1),
                o_piece,
            ],
            1,
        )
    )
    ffn_two = dp_gather(
        jnp.concatenate([column_block(w, 1) for w in (w_gate2, w_up2, w_down2)], 1)
    )
    in_block = mix_all[:, : 3 * channels]
    out_block = mix_all[:, 3 * channels + 128 :].reshape(channels, width)
    qkv_width = attn_all.shape[1] - channels
    qkv_block = attn_all[:, :qkv_width]
    o_block = attn_all[:, qkv_width:].reshape(channels, width)
    small_all = mix_all[:, 3 * channels : 3 * channels + 128].astype(F32).T
    kernel = lax.dynamic_slice_in_dim(small_all[:taps], seq_place * channels, channels, 1)
    gain_mix, gain_ffn_one, gain_attn, gain_ffn_two = (small_all[taps + i] for i in range(4))
    head_gains = small_all[taps + 4 : taps + 6].reshape(2, dp_count, slots)
    head_gains = jnp.tile(head_gains[:, :, : head // dp_count].reshape(2, head), (1, 2))

    bounds = cu_seqlens[0]
    turn = seq_place ^ jnp.arange(seq_count, dtype=jnp.int32)
    places = turn[:, None] * length + jnp.arange(length, dtype=jnp.int32)[None, :]
    docs_here = doc_index(bounds, places)
    masks = [
        (doc_index(bounds, places - tap) == docs_here).astype(F32)[..., None]
        for tap in range(1, reach + 1)
    ]

    order = jnp.arange(full, dtype=jnp.int32)
    starts = doc_starts(bounds, order)
    cosine, sine = rope_tables(order - starts, head)
    starts = starts[None, :]
    place = seq_place.reshape(1).astype(jnp.int32)

    x_flat = x_in.reshape(length, width).astype(F32)
    unit_one, scale_one = unit_scale(x_flat)
    normed_one = (unit_scale(x_all)[0] * gain_mix).astype(BF16)
    projected = plain_dot(normed_one, in_block).reshape(seq_count, length, 3 * channels)
    part_b = projected[..., :channels]
    part_c = projected[..., channels : 2 * channels]
    part_x = projected[..., 2 * channels :]
    product = (part_b * part_x).astype(BF16)
    tails = flip_blocks(product[:, length - reach :])
    before = flip_blocks(jnp.concatenate([jnp.zeros_like(tails[:1]), tails[:-1]], 0))
    extended = jnp.concatenate([before, product], 1).astype(F32)
    conv_out = kernel[0] * extended[:, reach:]
    for tap in range(1, reach + 1):
        conv_out = (
            conv_out
            + kernel[tap] * extended[:, reach - tap : reach - tap + length] * masks[tap - 1]
        )
    gated = (part_c * conv_out).astype(BF16).reshape(full, channels)
    hidden_one = x_flat + seq_scatter(plain_dot(gated, out_block))

    unit_two, scale_two = unit_scale(hidden_one)
    normed_two = seq_gather((unit_two * gain_ffn_one).astype(BF16))
    keep_one = ffn_gate(normed_two, ffn_one)
    hidden = ffn_one.shape[1] // 3
    hidden_two = hidden_one + seq_scatter(right_dot(keep_one[2], ffn_one[:, 2 * hidden :]))

    unit_three, scale_three = unit_scale(hidden_two)
    normed_three = seq_gather((unit_three * gain_attn).astype(BF16))
    raw = plain_dot(normed_three, qkv_block)
    kv_width = (qkv_width - channels) // 2
    attended_low, wide, totals = attention_forward(
        place, raw, cosine, sine, starts, head_gains, length
    )
    hidden_three = hidden_two + seq_scatter(plain_dot(attended_low, o_block))

    unit_four, scale_four = unit_scale(hidden_three)
    normed_four = seq_gather((unit_four * gain_ffn_two).astype(BF16))
    keep_two = ffn_gate(normed_four, ffn_two)
    hidden_four = hidden_three + seq_scatter(right_dot(keep_two[2], ffn_two[:, 2 * hidden :]))
    out = hidden_four.astype(BF16).reshape(rows, length, width)

    cotangent_all = seq_gather(cotangent.reshape(length, width))
    grad_four = cotangent.reshape(length, width).astype(F32)
    d_ffn_in, grads_two = ffn_back(cotangent_all, keep_two, normed_four, ffn_two)
    owned_two = dp_scatter(grads_two)
    d_hidden, d_gain_ffn_two = norm_back(d_ffn_in, gain_ffn_two, unit_four, scale_four)
    grad_three = grad_four + d_hidden

    grad_attn = seq_gather(grad_three.astype(BF16))
    d_w_o = left_dot(attended_low, grad_attn)
    d_attended = right_dot(grad_attn, o_block).astype(BF16)
    d_raw, d_head_gains = attention_backward(
        place, raw, cosine, sine, starts, head_gains, wide, totals, d_attended, length
    )
    d_head_gains = d_head_gains[:, :head] + d_head_gains[:, head:]
    d_qkv = left_dot(normed_three, d_raw)
    d_attn_in = seq_scatter(right_dot(d_raw, qkv_block))
    grads_attn = jnp.concatenate(
        [d_qkv.astype(BF16), d_w_o.astype(BF16).reshape(width, channels)], 1
    )
    owned_attn = dp_scatter(grads_attn)
    d_attn_h, d_gain_attn = norm_back(d_attn_in, gain_attn, unit_three, scale_three)
    grad_two = grad_three + d_attn_h

    grad_two_all = seq_gather(grad_two.astype(BF16))
    grad_two_all, owned_two = lax.optimization_barrier((grad_two_all, owned_two))
    d_ffn_in_one, grads_one = ffn_back(grad_two_all, keep_one, normed_two, ffn_one)
    d_hidden_one, d_gain_ffn_one = norm_back(d_ffn_in_one, gain_ffn_one, unit_two, scale_two)
    grad_one = grad_two + d_hidden_one

    grad_mix = seq_gather(grad_one.astype(BF16))
    grad_mix, owned_attn, grads_one = lax.optimization_barrier((grad_mix, owned_attn, grads_one))
    owned_one = dp_scatter(grads_one)
    d_w_out = left_dot(gated, grad_mix)
    d_gated = right_dot(grad_mix, out_block).reshape(seq_count, length, channels)
    d_part_c = d_gated * conv_out
    d_conv = d_gated * part_c
    sent = [d_conv * masks[tap - 1] for tap in range(1, reach + 1)]
    kernel_grads = [jnp.sum((d_conv * extended[:, reach:]).reshape(-1, channels), 0)]
    for tap in range(1, reach + 1):
        piece = extended[:, reach - tap : reach - tap + length]
        kernel_grads.append(jnp.sum((sent[tap - 1] * piece).reshape(-1, channels), 0))
    d_product_sum = kernel[0] * d_conv
    for tap in range(1, reach + 1):
        heads = flip_blocks(sent[tap - 1][:, :tap])
        after = flip_blocks(jnp.concatenate([heads[1:], jnp.zeros_like(heads[:1])], 0))
        moved = jnp.concatenate([sent[tap - 1][:, tap:], after], 1)
        d_product_sum = d_product_sum + kernel[tap] * moved
    d_product = lax.optimization_barrier(d_product_sum.astype(BF16)).astype(F32)
    d_projected = jnp.concatenate([d_product * part_x, d_part_c, d_product * part_b], -1)
    d_projected = d_projected.astype(BF16).reshape(full, 3 * channels)
    d_w_in = left_dot(normed_one, d_projected)
    d_normed = seq_scatter(right_dot(d_projected, in_block))
    d_x_part, d_gain_mix = norm_back(d_normed, gain_mix, unit_one, scale_one)
    d_x = (grad_one + d_x_part).reshape(rows, length, width)

    kernel_wide = lax.dynamic_update_slice_in_dim(
        jnp.zeros((taps, width), F32), jnp.stack(kernel_grads), seq_place * channels, 1
    )
    head_wide = jnp.pad(
        d_head_gains.reshape(2, dp_count, -1),
        ((0, 0), (0, 0), (0, slots - head // dp_count)),
    ).reshape(2, width)
    vectors = jnp.concatenate(
        [
            jnp.stack([d_gain_mix, d_gain_ffn_one, d_gain_attn, d_gain_ffn_two]),
            kernel_wide,
            head_wide,
        ],
        0,
    )
    vector_columns = jnp.pad(vectors.T, ((0, 0), (0, 128 - vectors.shape[0])))
    grads_mix = jnp.concatenate(
        [
            d_w_in.astype(BF16),
            vector_columns.astype(BF16),
            d_w_out.astype(BF16).reshape(width, channels),
        ],
        1,
    )
    grads_mix, owned_one = lax.optimization_barrier((grads_mix, owned_one))
    owned_mix = dp_scatter(grads_mix)

    def redeal(owned):
        block = owned[:, owned.shape[1] - channels :].reshape(-1, width)
        back = undeal_rows(block).reshape(slots, channels)
        return jnp.concatenate([owned[:, : owned.shape[1] - channels], back], 1)

    (d_wgate_two, d_wup_two, d_down_two), _ = split_columns(share(owned_two), [(1, hidden)] * 3)
    shared_one = share(jnp.concatenate([owned_one, redeal(owned_attn)], 1))
    one, rest_attn = split_columns(
        shared_one, [(1, hidden)] * 3 + [(1, channels), (1, kv_width), (1, kv_width)]
    )
    d_wgate_one, d_wup_one, d_down_one, d_w_q, d_w_k, d_w_v = one
    (d_w_in_full,), rest_mix = split_columns(share(redeal(owned_mix)), [(3, channels)])
    d_w_o_full = jnp.concatenate([b.reshape(-1, width) for b in rest_attn], 0).astype(F32)
    d_w_out_full = jnp.concatenate([b[:, 128:].reshape(-1, width) for b in rest_mix], 0)
    d_w_out_full = d_w_out_full.astype(F32)
    sums = sum(b[:, :128].astype(F32) for b in rest_mix).T
    small_head = head // dp_count
    return (
        out,
        d_x,
        d_w_in_full,
        sums[4 : 4 + taps],
        d_w_out_full,
        d_wgate_one,
        d_wup_one,
        d_down_one,
        sums[0],
        sums[1],
        d_w_q,
        d_w_k,
        d_w_v,
        d_w_o_full,
        sums[4 + taps, :small_head],
        sums[5 + taps, :small_head],
        d_wgate_two,
        d_wup_two,
        d_down_two,
        sums[2],
        sums[3],
    )


def solution(mesh):
    matrix = P("dp", None)
    vector = P("dp")
    tokens = P("dp", "seq", None)
    kernel = P(None, "dp")
    in_specs = (
        (tokens, matrix, P("dp", "seq"), tokens, matrix, kernel)
        + (matrix,) * 4
        + (vector,) * 2
        + (matrix,) * 4
        + (vector,) * 2
        + (matrix,) * 3
        + (vector,) * 2
    )
    out_specs = (
        (tokens, tokens, matrix, kernel)
        + (matrix,) * 4
        + (vector,) * 2
        + (matrix,) * 4
        + (vector,) * 2
        + (matrix,) * 3
        + (vector,) * 2
    )
    return jax.shard_map(local, mesh=mesh, in_specs=in_specs, out_specs=out_specs, check_vma=False)
```

```python
import jax
import jax.numpy as jnp
from jax import lax
from jax.experimental import pallas as pl
from jax.experimental.pallas import tpu as pltpu
from jax.sharding import PartitionSpec as P

EPS = 1e-05
THETA = 1000000.0
NEG = -1e30
F32 = jnp.float32
BF16 = jnp.bfloat16
TILE = 256
LANES = 128
VMEM_LIMIT = 48 << 20


def left_dot(left, right):
    return lax.dot_general(left, right, (((0,), (0,)), ((), ())), preferred_element_type=F32)


def right_dot(left, right):
    return lax.dot_general(left, right, (((1,), (1,)), ((), ())), preferred_element_type=F32)


def plain_dot(left, right):
    return jnp.dot(left, right, preferred_element_type=F32)


def unit_scale(value):
    scale = lax.rsqrt(jnp.mean(value * value, -1, keepdims=True) + EPS)
    return (value * scale, scale)


def norm_back(grad_out, gain, unit, scale):
    weighted = grad_out * gain
    grad_in = scale * (weighted - unit * jnp.mean(weighted * unit, -1, keepdims=True))
    gain_grad = jnp.sum((grad_out * unit).reshape(-1, unit.shape[-1]), 0)
    return (grad_in, gain_grad)


def doc_index(bounds, places):
    later = bounds[1:]
    passed = (later <= places[..., None]) & (later > 0)
    return jnp.sum(passed.astype(jnp.int32), -1)


def doc_starts(bounds, places):
    return jnp.max(jnp.where(bounds <= places[..., None], bounds, 0), -1)


def rope_tables(places, head):
    half = head // 2
    freqs = THETA ** (-(2.0 * jnp.arange(half, dtype=F32)) / head)
    angles = places.astype(F32)[:, None] * freqs
    cosine = jnp.cos(angles)
    sine = jnp.sin(angles)
    return (
        jnp.concatenate([cosine] * 4, 1),
        jnp.concatenate([-sine, sine, -sine, sine], 1),
    )


def seq_bits():
    size = lax.axis_size("seq")
    bits = []
    bit = 1
    while bit < size:
        bits.append(bit)
        bit = bit * 2
    return bits


def swap_seq(array, bit):
    size = lax.axis_size("seq")
    return lax.ppermute(array, "seq", [(i, i ^ bit) for i in range(size)])


def tie(*values):
    return lax.optimization_barrier(values)


def near_blocks(block):
    have = {0: block}
    for bit in reversed(seq_bits()[:-1]):
        for place in sorted(have):
            have[place | bit] = swap_seq(have[place], bit)
    return [have[place] for place in sorted(have)]


def near_half(block):
    return jnp.concatenate(near_blocks(block), 0)


def far_half(block):
    return swap_seq(block, seq_bits()[-1])


def near_sum(half):
    size = lax.axis_size("seq") // 2
    length = half.shape[0] // size
    have = {place: half[place * length : (place + 1) * length] for place in range(size)}
    for bit in seq_bits()[:-1]:
        for place in sorted(have, reverse=True):
            if place & bit:
                got = swap_seq(have.pop(place).astype(BF16), bit).astype(F32)
                have[place ^ bit] = have[place ^ bit].astype(F32) + got
    return have[0].astype(F32)


def seq_scatter(near, far, *work):
    sent = far_half(near_sum(far).astype(BF16))
    kept = near_sum(near)
    sent, kept, *work = tie(sent, kept, *work)
    total = kept + sent.astype(F32)
    return (total, *work) if work else total


def flip_blocks(array):
    place = lax.axis_index("seq")
    for bit in seq_bits():
        shape = array.shape
        split = array.reshape((shape[0] // (2 * bit), 2, bit) + shape[1:])
        turned = jnp.concatenate([split[:, 1:], split[:, :1]], 1)
        array = jnp.where((place & bit) > 0, turned, split).reshape(shape)
    return array


def half_lanes(shape):
    return lax.broadcasted_iota(jnp.int32, shape, 1) < LANES // 2


def head_mean(value):
    row = lax.broadcasted_iota(jnp.int32, (LANES, LANES), 0) < LANES // 2
    column = half_lanes((LANES, LANES))
    ones = jnp.where(row == column, 2.0 / LANES, 0.0).astype(BF16)
    high = value.astype(BF16)
    low = (value - high.astype(F32)).astype(BF16)
    return plain_dot(high, ones) + plain_dot(low, ones)


def swap_quarters(value):
    quarter = LANES // 4
    lane = lax.broadcasted_iota(jnp.int32, value.shape, 1)
    first = (lane // quarter) % 2 == 0
    return jnp.where(
        first, pltpu.roll(value, LANES - quarter, 1), pltpu.roll(value, quarter, 1)
    )


def head_unit(value):
    scale = lax.rsqrt(head_mean(value * value) + EPS)
    return (value * scale, scale)


def pad_pair(value, second):
    lower = half_lanes(value.shape)
    if second:
        high = jnp.where(lower, 0.0, value)
        return (pltpu.roll(high, LANES // 2, 1), high)
    low = jnp.where(lower, value, 0.0)
    return (low, pltpu.roll(low, LANES // 2, 1))


def load_heads(raw_ref, cos_ref, sin_ref, gains_ref, source, target, length, pairs):
    rows = pl.ds(source, length)
    cosine = cos_ref[pl.ds(target, length), :]
    sine = sin_ref[pl.ds(target, length), :]
    groups = raw_ref.shape[1] // LANES

    def turned(group, gain):
        value = head_unit(raw_ref[rows, group * LANES : (group + 1) * LANES])[0] * gain
        return value * cosine + swap_quarters(value) * sine

    scale = (LANES // 2) ** (-0.5)
    queries = [(turned(g, gains_ref[0:1, :]) * scale).astype(BF16) for g in range(pairs)]
    keys = []
    values = []
    cached = {}
    for g in range(pairs):
        place = pairs * LANES + g * (LANES // 2)
        group, second = divmod(place, LANES)
        if group not in cached:
            cached[group] = turned(group, gains_ref[1:2, :]).astype(BF16).astype(F32)
        keys.append([k.astype(BF16) for k in pad_pair(cached[group], second > 0)])
        place = place + pairs * (LANES // 2)
        group, second = divmod(place, LANES)
        value = raw_ref[rows, group * LANES : (group + 1) * LANES]
        values.append([v.astype(BF16) for v in pad_pair(value, second > 0)])
    return (queries, keys, values)


def allowed_tile(start_ref, first_key, first_query):
    query = first_query + lax.broadcasted_iota(jnp.int32, (1, TILE), 1)
    start = start_ref[0:1, pl.ds(first_query, TILE)]
    key = first_key + lax.broadcasted_iota(jnp.int32, (TILE, TILE), 0)
    return (key >= start) & (key <= query)


def attention_forward_kernel(
    place_ref, raw_ref, cos_ref, sin_ref, start_ref, gains_ref,
    out_ref, wide_ref, total_ref, query_ref, key_ref, value_ref,
    *, length, pairs,
):
    full = raw_ref.shape[0]
    count = full // length
    place = place_ref[0]

    def prepare(block, _):
        target = pl.multiple_of(block * length, 8)
        source = pl.multiple_of((block ^ place) * length, 8)
        queries, keys, values = load_heads(
            raw_ref, cos_ref, sin_ref, gains_ref, source, target, length, pairs
        )
        for g in range(pairs):
            query_ref[g, pl.ds(target, length), :] = queries[g]
            for h in range(2):
                key_ref[2 * g + h, pl.ds(target, length), :] = keys[g][h]
                value_ref[2 * g + h, pl.ds(target, length), :] = values[g][h]
        return 0

    lax.fori_loop(0, count, prepare, 0)
    half = LANES // 2

    def query_tile(i, _):
        first_query = pl.multiple_of(i * TILE, TILE)

        def key_tile(j, carry):
            first_key = pl.multiple_of(j * TILE, TILE)
            allowed = allowed_tile(start_ref, first_key, first_query)
            sums, outs = carry
            new_sums = []
            new_outs = []
            for g in range(pairs):
                query = query_ref[g, pl.ds(first_query, TILE), :]
                total = outs[g]
                for h in range(2):
                    key = key_ref[2 * g + h, pl.ds(first_key, TILE), :]
                    value = value_ref[2 * g + h, pl.ds(first_key, TILE), :]
                    weight = jnp.where(allowed, jnp.exp(right_dot(key, query)), 0.0)
                    new_sums.append(sums[2 * g + h] + jnp.sum(weight, 0, keepdims=True))
                    total = total + lax.dot_general(
                        value, weight.astype(BF16), (((0,), (0,)), ((), ())),
                        preferred_element_type=F32,
                    )
                new_outs.append(total)
            return (new_sums, new_outs)

        carry = (
            [jnp.zeros((1, TILE), F32) for _ in range(2 * pairs)],
            [jnp.zeros((LANES, TILE), F32) for _ in range(pairs)],
        )
        sums, outs = lax.fori_loop(0, i + 1, key_tile, carry)
        columns = pl.ds(first_query, TILE)
        for g in range(pairs):
            scaled = jnp.concatenate(
                [outs[g][h * half : (h + 1) * half] / sums[2 * g + h] for h in range(2)], 0
            )
            for h in range(2):
                total_ref[2 * g + h : 2 * g + h + 1, columns] = sums[2 * g + h]
            wide_ref[g * LANES : (g + 1) * LANES, columns] = scaled
            query_ref[g, columns, :] = scaled.T.astype(BF16)
        return 0

    lax.fori_loop(0, full // TILE, query_tile, 0)

    def finish(block, _):
        source = pl.multiple_of(block * length, 8)
        target = pl.multiple_of((block ^ place) * length, 8)
        for g in range(pairs):
            out_ref[pl.ds(target, length), g * LANES : (g + 1) * LANES] = query_ref[
                g, pl.ds(source, length), :
            ]
        return 0

    lax.fori_loop(0, count, finish, 0)


def attention_backward_kernel(
    place_ref, raw_ref, cos_ref, sin_ref, start_ref, gains_ref, wide_ref, total_ref, grad_ref,
    out_ref, gain_grad_ref,
    query_ref, key_ref, value_ref, hold_ref, dq_ref, dk_ref, dv_ref,
    *, length, pairs,
):
    full = raw_ref.shape[0]
    count = full // length
    place = place_ref[0]
    half = LANES // 2

    def prepare(block, _):
        target = pl.multiple_of(block * length, 8)
        source = pl.multiple_of((block ^ place) * length, 8)
        queries, keys, values = load_heads(
            raw_ref, cos_ref, sin_ref, gains_ref, source, target, length, pairs
        )
        rows = pl.ds(target, length)
        for g in range(pairs):
            query_ref[g, rows, :] = queries[g]
            hold_ref[g, rows, :] = grad_ref[
                pl.ds(source, length), g * LANES : (g + 1) * LANES
            ]
            dk_ref[g, rows, :] = jnp.zeros((length, LANES), F32)
            dv_ref[g, rows, :] = jnp.zeros((length, LANES), F32)
            for h in range(2):
                key_ref[2 * g + h, rows, :] = keys[g][h]
                value_ref[2 * g + h, rows, :] = values[g][h]
        return 0

    lax.fori_loop(0, count, prepare, 0)
    lower = half_lanes((TILE, LANES))

    def query_tile(i, _):
        first_query = pl.multiple_of(i * TILE, TILE)
        columns = pl.ds(first_query, TILE)
        inverse = [1.0 / total_ref[n : n + 1, columns] for n in range(2 * pairs)]
        inner = []
        for g in range(pairs):
            grad = hold_ref[g, columns, :].astype(F32).T
            both = grad * wide_ref[g * LANES : (g + 1) * LANES, columns]
            for h in range(2):
                inner.append(jnp.sum(both[h * half : (h + 1) * half], 0, keepdims=True))

        def key_tile(j, outs):
            first_key = pl.multiple_of(j * TILE, TILE)
            rows = pl.ds(first_key, TILE)
            allowed = allowed_tile(start_ref, first_key, first_query)
            new_outs = []
            for g in range(pairs):
                query = query_ref[g, columns, :]
                grad = hold_ref[g, columns, :]
                zero = jnp.zeros_like(query)
                total = outs[g]
                d_key = dk_ref[g, rows, :]
                d_value = dv_ref[g, rows, :]
                for h in range(2):
                    keep = lower if h == 0 else jnp.logical_not(lower)
                    key = key_ref[2 * g + h, rows, :]
                    value = value_ref[2 * g + h, rows, :]
                    weight = jnp.exp(right_dot(key, query)) * inverse[2 * g + h]
                    weight = jnp.where(allowed, weight, 0.0)
                    d_weight = right_dot(value, grad)
                    d_score = (weight * (d_weight - inner[2 * g + h])).astype(BF16)
                    d_value = d_value + plain_dot(
                        weight.astype(BF16), jnp.where(keep, grad, zero)
                    )
                    d_key = d_key + plain_dot(d_score, jnp.where(keep, query, zero))
                    total = total + lax.dot_general(
                        key, d_score, (((0,), (0,)), ((), ())), preferred_element_type=F32
                    )
                dk_ref[g, rows, :] = d_key
                dv_ref[g, rows, :] = d_value
                new_outs.append(total)
            return new_outs

        outs = lax.fori_loop(
            0, i + 1, key_tile, [jnp.zeros((LANES, TILE), F32) for _ in range(pairs)]
        )
        for g in range(pairs):
            dq_ref[g, columns, :] = outs[g].T
        return 0

    lax.fori_loop(0, full // TILE, query_tile, 0)
    scale = half ** (-0.5)

    def finish(block, carry):
        source = pl.multiple_of(block * length, 8)
        target = pl.multiple_of((block ^ place) * length, 8)
        rows = pl.ds(source, length)
        cosine = cos_ref[rows, :]
        sine = sin_ref[rows, :]
        low = half_lanes((length, LANES))

        def back(grad, group, gain):
            grad = grad.astype(BF16).astype(F32)
            unit, inverse = head_unit(
                raw_ref[pl.ds(target, length), group * LANES : (group + 1) * LANES]
            )
            d_rot = grad * cosine + swap_quarters(grad * sine)
            weighted = d_rot * gain
            d_raw = inverse * (weighted - unit * head_mean(weighted * unit))
            return (d_raw, d_rot * unit)

        query_gain, key_gain = carry
        for g in range(pairs):
            d_raw, terms = back(dq_ref[g, rows, :] * scale, g, gains_ref[0:1, :])
            query_gain = query_gain + jnp.sum(terms, 0, keepdims=True)
            out_ref[pl.ds(target, length), g * LANES : (g + 1) * LANES] = d_raw.astype(BF16)
        groups = {}
        for kind, held in ((0, dk_ref), (1, dv_ref)):
            for g in range(pairs):
                place_of = pairs * LANES + kind * pairs * half + g * half
                group, second = divmod(place_of, LANES)
                value = held[g, rows, :]
                value = value + pltpu.roll(value, half, 1)
                groups.setdefault(group, {})[second // half] = (kind, value)
        for group, parts in groups.items():
            merged = jnp.where(low, parts[0][1], parts[1][1])
            is_key = [parts[n][0] == 0 for n in range(2)]
            result = merged
            if any(is_key):
                d_raw, terms = back(merged, group, gains_ref[1:2, :])
                if not is_key[1]:
                    d_raw = jnp.where(low, d_raw, merged)
                    terms = jnp.where(low, terms, 0.0)
                result = d_raw
                key_gain = key_gain + jnp.sum(terms, 0, keepdims=True)
            out_ref[pl.ds(target, length), group * LANES : (group + 1) * LANES] = result.astype(
                BF16
            )
        return (query_gain, key_gain)

    zero = jnp.zeros((1, LANES), F32)
    query_gain, key_gain = lax.fori_loop(0, count, finish, (zero, zero))
    gain_grad_ref[0:1, :] = query_gain
    gain_grad_ref[1:2, :] = key_gain


def whole(count):
    return [pl.BlockSpec(memory_space=pltpu.VMEM)] * count


def attention_forward(place, raw, cosine, sine, start, gains, length):
    full, columns = raw.shape
    pairs = columns // (2 * LANES)
    return pl.pallas_call(
        lambda *refs: attention_forward_kernel(*refs, length=length, pairs=pairs),
        in_specs=[pl.BlockSpec(memory_space=pltpu.SMEM)] + whole(5),
        out_specs=tuple(whole(3)),
        out_shape=(
            jax.ShapeDtypeStruct((full, pairs * LANES), BF16),
            jax.ShapeDtypeStruct((pairs * LANES, full), F32),
            jax.ShapeDtypeStruct((8, full), F32),
        ),
        scratch_shapes=[
            pltpu.VMEM((pairs, full, LANES), BF16),
            pltpu.VMEM((2 * pairs, full, LANES), BF16),
            pltpu.VMEM((2 * pairs, full, LANES), BF16),
        ],
        compiler_params=pltpu.CompilerParams(vmem_limit_bytes=VMEM_LIMIT),
        cost_estimate=pl.CostEstimate(flops=20_000_000_000, transcendentals=6000000, bytes_accessed=20000000),
        name="attention_forward",
    )(place, raw, cosine, sine, start, gains)


def attention_backward(place, raw, cosine, sine, start, gains, wide, totals, grads, length):
    full, columns = raw.shape
    pairs = columns // (2 * LANES)
    return pl.pallas_call(
        lambda *refs: attention_backward_kernel(*refs, length=length, pairs=pairs),
        in_specs=[pl.BlockSpec(memory_space=pltpu.SMEM)] + whole(8),
        out_specs=tuple(whole(2)),
        out_shape=(
            jax.ShapeDtypeStruct((full, columns), BF16),
            jax.ShapeDtypeStruct((2, LANES), F32),
        ),
        scratch_shapes=[
            pltpu.VMEM((pairs, full, LANES), BF16),
            pltpu.VMEM((2 * pairs, full, LANES), BF16),
            pltpu.VMEM((2 * pairs, full, LANES), BF16),
            pltpu.VMEM((pairs, full, LANES), BF16),
            pltpu.VMEM((pairs, full, LANES), F32),
            pltpu.VMEM((pairs, full, LANES), F32),
            pltpu.VMEM((pairs, full, LANES), F32),
        ],
        compiler_params=pltpu.CompilerParams(vmem_limit_bytes=VMEM_LIMIT),
        cost_estimate=pl.CostEstimate(flops=20_000_000_000, transcendentals=6000000, bytes_accessed=20000000),
        name="attention_backward",
    )(place, raw, cosine, sine, start, gains, wide, totals, grads)

def column_block(weight, parts):
    size = lax.axis_size("seq")
    place = lax.axis_index("seq")
    rows, columns = weight.shape
    block = columns // parts // size
    split = weight.reshape(rows, parts, size * block)
    return lax.dynamic_slice_in_dim(split, place * block, block, 2).reshape(rows, parts * block)


def deal_pairs():
    size = lax.axis_size("seq")
    count = lax.axis_size("dp")
    pairs = []
    for place in range(size):
        for owner in range(count):
            source = (owner % size) * count + place * (count // size) + owner // size
            pairs.append((source, place * count + owner))
    return pairs


def deal_rows(weight):
    size = lax.axis_size("seq")
    place = lax.axis_index("seq")
    piece = weight.shape[0] // size
    part = lax.dynamic_slice_in_dim(weight, place * piece, piece, 0)
    return lax.ppermute(part, ("seq", "dp"), deal_pairs())


def undeal_rows(part):
    return lax.ppermute(part, ("seq", "dp"), [(b, a) for a, b in deal_pairs()])


def dp_gather(block):
    return lax.all_gather(block, "dp", axis=0, tiled=True)


def dp_scatter(grads):
    return lax.psum_scatter(grads, "dp", scatter_dimension=0, tiled=True)


def swap_dp(array, bit):
    size = lax.axis_size("dp")
    return lax.ppermute(array, "dp", [(i, i ^ bit) for i in range(size)])


def dp_gather_small(block, later):
    size = lax.axis_size("dp")
    if size != 8:
        return (dp_gather(block), later)
    place = lax.axis_index("dp")
    rows = block.shape[0]
    have = {0: block}
    for far in (2, 4, 6):
        have[far] = swap_dp(block, far)
    have[2], later = tie(have[2], later)
    for far in (0, 2, 4, 6):
        have[far ^ 1] = swap_dp(have[far], 1)
    result = jnp.zeros((size * rows, block.shape[1]), block.dtype)
    for turn in range(size):
        result = lax.dynamic_update_slice_in_dim(result, have[turn], (place ^ turn) * rows, 0)
    return (result, later)


def dp_scatter_small(grads):
    size = lax.axis_size("dp")
    if size != 8:
        return dp_scatter(grads)
    place = lax.axis_index("dp")
    rows = grads.shape[0] // size

    def part(turn):
        return lax.dynamic_slice_in_dim(grads, (place ^ turn) * rows, rows, 0)

    sums = {}
    for far in (4, 6, 2, 0):
        sums[far] = part(far).astype(F32) + swap_dp(part(far ^ 1), 1).astype(F32)
    total = sums[0]
    for far in (4, 6, 2):
        total = total + swap_dp(sums[far].astype(BF16), far).astype(F32)
    return total.astype(BF16)


def share(owned):
    size = lax.axis_size("seq")
    place = lax.axis_index("seq")
    everywhere = jnp.stack(near_blocks(owned) + near_blocks(far_half(owned)), 0)
    return [lax.dynamic_index_in_dim(everywhere, place ^ i, 0, False) for i in range(size)]


def split_columns(blocks, parts):
    results = []
    offset = 0
    for split, columns in parts:
        pieces = []
        for number in range(split):
            start = offset + number * columns
            pieces = pieces + [block[:, start : start + columns] for block in blocks]
        results.append(jnp.concatenate(pieces, 1).astype(F32))
        offset = offset + split * columns
    return (results, [block[:, offset:] for block in blocks])


def gate_terms(normed, w_gate, w_up):
    gate = plain_dot(normed, w_gate)
    upper = plain_dot(normed, w_up)
    sigma = jax.nn.sigmoid(gate)
    swish = gate * sigma
    return (upper * (sigma + swish * (1.0 - sigma)), swish, swish * upper)


def ffn_forward_kernel(normed_ref, gate_ref, up_ref, down_ref, *rest):
    kept_ref, partial_ref = rest[-2:]
    hidden = gate_ref.shape[1]
    slope, swish, act = gate_terms(normed_ref[...], gate_ref[...], up_ref[...])
    act = act.astype(BF16)
    kept_ref[:, :hidden] = slope.astype(BF16)
    kept_ref[:, hidden : 2 * hidden] = swish.astype(BF16)
    kept_ref[:, 2 * hidden :] = act
    partial_ref[...] = right_dot(act, down_ref[...]).astype(BF16)


def ffn_turn_kernel(normed_ref, grad_ref, gate_ref, up_ref, down_ref, *rest):
    kept_ref, partial_ref = rest[-2:]
    hidden = gate_ref.shape[1]
    slope, swish, act = gate_terms(normed_ref[...], gate_ref[...], up_ref[...])
    d_act = plain_dot(grad_ref[...], down_ref[...])
    d_gate = (d_act * slope).astype(BF16)
    d_up = (d_act * swish).astype(BF16)
    kept_ref[:, :hidden] = d_gate
    kept_ref[:, hidden : 2 * hidden] = d_up
    kept_ref[:, 2 * hidden :] = act.astype(BF16)
    partial = right_dot(d_gate, gate_ref[...]) + right_dot(d_up, up_ref[...])
    partial_ref[...] = partial.astype(BF16)


def ffn_backward_kernel(grad_ref, terms_ref, gate_ref, up_ref, down_ref, *rest):
    kept_ref, partial_ref = rest[-2:]
    hidden = gate_ref.shape[1]
    d_act = plain_dot(grad_ref[...], down_ref[...])
    d_gate = (d_act * terms_ref[:, :hidden].astype(F32)).astype(BF16)
    d_up = (d_act * terms_ref[:, hidden:].astype(F32)).astype(BF16)
    kept_ref[:, :hidden] = d_gate
    kept_ref[:, hidden:] = d_up
    partial = right_dot(d_gate, gate_ref[...]) + right_dot(d_up, up_ref[...])
    partial_ref[...] = partial.astype(BF16)


def ffn_call(kernel, name, tokens, terms, weights, hidden, length, first, full, kept_width, kept):
    width = weights.shape[0]
    count = tokens[0].shape[0] // length
    in_specs = [pl.BlockSpec((length, width), lambda i: (i, 0)) for _ in tokens]
    operands = list(tokens)
    if terms is not None:
        in_specs.append(pl.BlockSpec((length, 2 * hidden), lambda i: (i + first, 0)))
        operands.append(terms)
    for place in range(3):
        in_specs.append(
            pl.BlockSpec(
                (width, hidden), lambda i, place=place: (0, place), pipeline_mode=pl.Buffered(1)
            )
        )
        operands.append(weights)
    aliases = {}
    if kept is not None:
        aliases = {len(operands): 0}
        in_specs.append(pl.BlockSpec(memory_space=pl.ANY))
        operands.append(kept)
    return pl.pallas_call(
        kernel,
        grid=(count,),
        in_specs=in_specs,
        out_specs=(
            pl.BlockSpec((length, kept_width), lambda i: (i + first, 0)),
            pl.BlockSpec((length, width), lambda i: (i, 0)),
        ),
        out_shape=(
            jax.ShapeDtypeStruct((full, kept_width), BF16),
            jax.ShapeDtypeStruct((count * length, width), BF16),
        ),
        input_output_aliases=aliases,
        compiler_params=pltpu.CompilerParams(vmem_limit_bytes=VMEM_LIMIT),
        cost_estimate=pl.CostEstimate(flops=6_000_000_000, transcendentals=1000000, bytes_accessed=20000000),
        name=name,
    )(*operands)


def split_weights(weights, hidden):
    return [weights[:, n * hidden : (n + 1) * hidden] for n in range(3)]


def halves_of(array):
    half = array.shape[0] // 2
    return (array[:half], array[half:])


def first_block(number, full, length):
    return number * (full // length // 2)


def place_rows(kept, part, number):
    if kept is None:
        kept = jnp.zeros((2 * part.shape[0], part.shape[1]), part.dtype)
    return lax.dynamic_update_slice_in_dim(kept, part, number * part.shape[0], 0)


def ffn_forward(normed, weights, hidden, length, number, kept):
    full = 2 * normed.shape[0]
    if hidden % LANES:
        w_gate, w_up, w_down = split_weights(weights, hidden)
        terms = jnp.concatenate(gate_terms(normed, w_gate, w_up), 1).astype(BF16)
        partial = right_dot(terms[:, 2 * hidden :], w_down).astype(BF16)
        return (place_rows(kept, terms, number), partial)
    return ffn_call(
        ffn_forward_kernel, "ffn_forward", [normed], None, weights, hidden, length,
        first_block(number, full, length), full, 3 * hidden, kept,
    )


def ffn_turn(normed, grads, weights, hidden, length, number, kept):
    full = 2 * normed.shape[0]
    if hidden % LANES:
        w_gate, w_up, w_down = split_weights(weights, hidden)
        slope, swish, act = gate_terms(normed, w_gate, w_up)
        d_act = plain_dot(grads, w_down)
        part = jnp.concatenate([d_act * slope, d_act * swish, act], 1).astype(BF16)
        partial = right_dot(part[:, : 2 * hidden], weights[:, : 2 * hidden]).astype(BF16)
        return (place_rows(kept, part, number), partial)
    return ffn_call(
        ffn_turn_kernel, "ffn_turn", [normed, grads], None, weights, hidden, length,
        first_block(number, full, length), full, 3 * hidden, kept,
    )


def ffn_backward(grads, terms, weights, hidden, length, number, kept):
    full = 2 * grads.shape[0]
    if hidden % LANES:
        w_gate, w_up, w_down = split_weights(weights, hidden)
        rows = slice(number * grads.shape[0], (number + 1) * grads.shape[0])
        d_act = plain_dot(grads, w_down)
        slope = terms[rows, :hidden].astype(F32)
        swish = terms[rows, hidden : 2 * hidden].astype(F32)
        part = jnp.concatenate([d_act * slope, d_act * swish], 1).astype(BF16)
        partial = right_dot(part, weights[:, : 2 * hidden]).astype(BF16)
        return (place_rows(kept, part, number), partial)
    return ffn_call(
        ffn_backward_kernel, "ffn_backward", [grads], terms, weights, hidden, length,
        first_block(number, full, length), full, 2 * hidden, kept,
    )


def local(
    x_in,
    cu_seqlens,
    positions,
    cotangent,
    w_in,
    conv_w,
    w_out,
    w_gate1,
    w_up1,
    w_down1,
    g_mix1,
    g_ffn1,
    w_q,
    key_projection_weight,
    value_projection_weight,
    w_o,
    g_q,
    g_k,
    w_gate2,
    w_up2,
    w_down2,
    g_attn2,
    g_ffn2,
):
    rows, length, width = x_in.shape
    assert rows == 1
    seq_count = lax.axis_size("seq")
    dp_count = lax.axis_size("dp")
    seq_place = lax.axis_index("seq")
    full = length * seq_count
    channels = width // seq_count
    slots = width // dp_count
    head = g_q.shape[0] * dp_count
    taps = conv_w.shape[0]
    reach = taps - 1

    x_far = far_half(x_in.reshape(length, width))
    cotangent_low, x_far = tie(cotangent.reshape(length, width), x_far)
    x_all = jnp.concatenate([near_half(x_in.reshape(length, width)), near_half(x_far)], 0)
    cotangent_halves = [near_half(cotangent_low), near_half(far_half(cotangent_low))]
    head_gains = jnp.pad(jnp.stack([g_q, g_k], 1), ((0, slots - head // dp_count), (0, 0)))
    small = jnp.concatenate(
        [conv_w.T, jnp.stack([g_mix1, g_ffn1, g_attn2, g_ffn2], 1), head_gains], 1
    )
    small = jnp.pad(small, ((0, 0), (0, 128 - small.shape[1])))
    dealt = deal_rows(jnp.stack([w_out, w_o], 1))
    out_piece = dealt[:, 0].reshape(slots, -1)
    o_piece = dealt[:, 1].reshape(slots, -1)
    ffn_columns = 3 * w_gate1.shape[1] // seq_count
    both = jnp.concatenate(
        [column_block(w, 1) for w in (w_gate1, w_up1, w_down1)]
        + [
            column_block(w_q, 1),
            column_block(key_projection_weight, 1),
            column_block(value_projection_weight, 1),
            o_piece,
        ],
        1,
    )
    mix_all, both = dp_gather_small(
        jnp.concatenate([column_block(w_in, 3), small, out_piece], 1), both
    )
    both = dp_gather(both)
    mix_all, *cotangent_halves = tie(mix_all, *cotangent_halves)
    ffn_one = both
    hidden = ffn_columns // 3
    attn_all = both[:, ffn_columns:]
    ffn_two = dp_gather(
        jnp.concatenate([column_block(w, 1) for w in (w_gate2, w_up2, w_down2)], 1)
    )
    in_block = mix_all[:, : 3 * channels]
    out_block = mix_all[:, 3 * channels + 128 :].reshape(channels, width)
    qkv_width = attn_all.shape[1] - channels
    qkv_block = attn_all[:, :qkv_width]
    o_block = attn_all[:, qkv_width:].reshape(channels, width)
    small_all = mix_all[:, 3 * channels : 3 * channels + 128].astype(F32).T
    kernel = lax.dynamic_slice_in_dim(small_all[:taps], seq_place * channels, channels, 1)
    gain_mix, gain_ffn_one, gain_attn, gain_ffn_two = (small_all[taps + i] for i in range(4))
    head_gains = small_all[taps + 4 : taps + 6].reshape(2, dp_count, slots)
    head_gains = jnp.tile(head_gains[:, :, : head // dp_count].reshape(2, head), (1, 2))

    bounds = cu_seqlens[0]
    turn = seq_place ^ jnp.arange(seq_count, dtype=jnp.int32)
    places = turn[:, None] * length + jnp.arange(length, dtype=jnp.int32)[None, :]
    docs_here = doc_index(bounds, places)
    masks = [
        (doc_index(bounds, places - tap) == docs_here).astype(F32)[..., None]
        for tap in range(1, reach + 1)
    ]

    order = jnp.arange(full, dtype=jnp.int32)
    starts = doc_starts(bounds, order)
    cosine, sine = rope_tables(order - starts, head)
    starts = starts[None, :]
    place = seq_place.reshape(1).astype(jnp.int32)

    x_flat = x_in.reshape(length, width).astype(F32)
    unit_one, scale_one = unit_scale(x_flat)
    normed_one = (unit_scale(x_all.astype(F32))[0] * gain_mix).astype(BF16)
    projected = plain_dot(normed_one, in_block).reshape(seq_count, length, 3 * channels)
    part_b = projected[..., :channels]
    part_c = projected[..., channels : 2 * channels]
    part_x = projected[..., 2 * channels :]
    product = (part_b * part_x).astype(BF16)
    tails = flip_blocks(product[:, length - reach :])
    before = flip_blocks(jnp.concatenate([jnp.zeros_like(tails[:1]), tails[:-1]], 0))
    extended = jnp.concatenate([before, product], 1).astype(F32)
    conv_out = kernel[0] * extended[:, reach:]
    for tap in range(1, reach + 1):
        conv_out = (
            conv_out
            + kernel[tap] * extended[:, reach - tap : reach - tap + length] * masks[tap - 1]
        )
    gated = (part_c * conv_out).astype(BF16).reshape(full, channels)
    hidden_one = x_flat + seq_scatter(*halves_of(plain_dot(gated, out_block)))

    unit_two, scale_two = unit_scale(hidden_one)
    near_two = (unit_two * gain_ffn_one).astype(BF16)
    far_two = far_half(near_two)
    near_two = near_half(near_two)
    terms_one, near_out = ffn_forward(near_two, ffn_one, hidden, length, 0, None)
    far_two, near_out = tie(far_two, near_out)
    far_two = near_half(far_two)
    terms_one, far_out = ffn_forward(far_two, ffn_one, hidden, length, 1, terms_one)
    hidden_two = hidden_one + seq_scatter(near_out, far_out)

    unit_three, scale_three = unit_scale(hidden_two)
    normed_three = (unit_three * gain_attn).astype(BF16)
    normed_three = jnp.concatenate(
        [near_half(normed_three), near_half(far_half(normed_three))], 0
    )
    raw = plain_dot(normed_three, qkv_block)
    kv_width = (qkv_width - channels) // 2
    attended_low, wide, totals = attention_forward(
        place, raw, cosine, sine, starts, head_gains, length
    )
    hidden_three = hidden_two + seq_scatter(*halves_of(plain_dot(attended_low, o_block)))

    unit_four, scale_four = unit_scale(hidden_three)
    near_four = (unit_four * gain_ffn_two).astype(BF16)
    far_four = far_half(near_four)
    near_four = near_half(near_four)
    kept_two, near_out = ffn_turn(near_four, cotangent_halves[0], ffn_two, hidden, length, 0, None)
    far_four, near_out = tie(far_four, near_out)
    far_four = near_half(far_four)
    kept_two, far_out = ffn_turn(far_four, cotangent_halves[1], ffn_two, hidden, length, 1, kept_two)

    grad_four = cotangent.reshape(length, width).astype(F32)
    kept_two, far_out = tie(kept_two, far_out)
    normed_four = jnp.concatenate([near_four, far_four], 0)
    d_gate_up = left_dot(normed_four, kept_two[:, : 2 * hidden]).astype(BF16)
    d_ffn_in, d_gate_up = seq_scatter(near_out, far_out, d_gate_up)
    d_hidden, d_gain_ffn_two = norm_back(d_ffn_in, gain_ffn_two, unit_four, scale_four)
    grad_three = grad_four + d_hidden

    grad_attn = grad_three.astype(BF16)
    far_attn = far_half(grad_attn)
    d_down = left_dot(jnp.concatenate(cotangent_halves, 0), kept_two[:, 2 * hidden :])
    grads_two = jnp.concatenate([d_gate_up, d_down.astype(BF16)], 1)
    far_attn, grads_two = tie(far_attn, grads_two)
    owned_two = dp_scatter(grads_two)
    grad_attn = jnp.concatenate([near_half(grad_attn), near_half(far_attn)], 0)
    d_w_o = left_dot(attended_low, grad_attn)
    d_attended = right_dot(grad_attn, o_block).astype(BF16)
    d_raw, d_head_gains = attention_backward(
        place, raw, cosine, sine, starts, head_gains, wide, totals, d_attended, length
    )
    d_head_gains = d_head_gains[:, :head] + d_head_gains[:, head:]
    partial_attn = right_dot(d_raw, qkv_block)
    d_raw, partial_attn = tie(d_raw, partial_attn)
    d_qkv = left_dot(normed_three, d_raw)
    grads_attn = jnp.concatenate(
        [d_qkv.astype(BF16), d_w_o.astype(BF16).reshape(width, channels)], 1
    )
    d_attn_in, grads_attn = seq_scatter(*halves_of(partial_attn), grads_attn)
    d_attn_h, d_gain_attn = norm_back(d_attn_in, gain_attn, unit_three, scale_three)
    grad_two = grad_three + d_attn_h

    owned_attn = dp_scatter_small(grads_attn)
    near_grad = grad_two.astype(BF16)
    far_grad = far_half(near_grad)
    near_grad = near_half(near_grad)
    kept_one, near_out = ffn_backward(near_grad, terms_one, ffn_one, hidden, length, 0, None)
    far_grad, near_out = tie(far_grad, near_out)
    far_grad = near_half(far_grad)
    kept_one, far_out = ffn_backward(far_grad, terms_one, ffn_one, hidden, length, 1, kept_one)
    kept_one, far_out = tie(kept_one, far_out)
    d_gate_up = left_dot(jnp.concatenate([near_two, far_two], 0), kept_one).astype(BF16)
    d_ffn_in_one, d_gate_up, owned_attn = seq_scatter(near_out, far_out, d_gate_up, owned_attn)
    d_hidden_one, d_gain_ffn_one = norm_back(d_ffn_in_one, gain_ffn_one, unit_two, scale_two)
    grad_one = grad_two + d_hidden_one

    grad_mix = grad_one.astype(BF16)
    far_mix = far_half(grad_mix)
    d_down = left_dot(
        jnp.concatenate([near_grad, far_grad], 0), terms_one[:, 2 * hidden :]
    ).astype(BF16)
    far_mix, grads_one = tie(far_mix, jnp.concatenate([d_gate_up, d_down], 1))
    owned_one = dp_scatter(grads_one)
    grad_mix = jnp.concatenate([near_half(grad_mix), near_half(far_mix)], 0)
    grad_mix, owned_two = tie(grad_mix, owned_two)
    d_w_out = left_dot(gated, grad_mix)
    d_gated = right_dot(grad_mix, out_block).reshape(seq_count, length, channels)
    d_part_c = d_gated * conv_out
    d_conv = d_gated * part_c
    sent = [d_conv * masks[tap - 1] for tap in range(1, reach + 1)]
    kernel_grads = [jnp.sum((d_conv * extended[:, reach:]).reshape(-1, channels), 0)]
    for tap in range(1, reach + 1):
        piece = extended[:, reach - tap : reach - tap + length]
        kernel_grads.append(jnp.sum((sent[tap - 1] * piece).reshape(-1, channels), 0))
    d_product_sum = kernel[0] * d_conv
    for tap in range(1, reach + 1):
        heads = flip_blocks(sent[tap - 1][:, :tap])
        after = flip_blocks(jnp.concatenate([heads[1:], jnp.zeros_like(heads[:1])], 0))
        moved = jnp.concatenate([sent[tap - 1][:, tap:], after], 1)
        d_product_sum = d_product_sum + kernel[tap] * moved
    d_product = lax.optimization_barrier(d_product_sum.astype(BF16)).astype(F32)
    d_projected = jnp.concatenate([d_product * part_x, d_part_c, d_product * part_b], -1)
    d_projected = d_projected.astype(BF16).reshape(full, 3 * channels)
    kept_two, d_projected = tie(kept_two, d_projected)
    ffn_out = right_dot(kept_two[:, 2 * hidden :], ffn_two[:, 2 * hidden :])
    hidden_four = hidden_three + seq_scatter(*halves_of(ffn_out))
    out = hidden_four.astype(BF16).reshape(rows, length, width)
    d_w_in = left_dot(normed_one, d_projected)
    d_normed = seq_scatter(*halves_of(right_dot(d_projected, in_block)))
    d_x_part, d_gain_mix = norm_back(d_normed, gain_mix, unit_one, scale_one)
    d_x = (grad_one + d_x_part).reshape(rows, length, width)

    kernel_wide = lax.dynamic_update_slice_in_dim(
        jnp.zeros((taps, width), F32), jnp.stack(kernel_grads), seq_place * channels, 1
    )
    head_wide = jnp.pad(
        d_head_gains.reshape(2, dp_count, -1),
        ((0, 0), (0, 0), (0, slots - head // dp_count)),
    ).reshape(2, width)
    vectors = jnp.concatenate(
        [
            jnp.stack([d_gain_mix, d_gain_ffn_one, d_gain_attn, d_gain_ffn_two]),
            kernel_wide,
            head_wide,
        ],
        0,
    )
    vector_columns = jnp.pad(vectors.T, ((0, 0), (0, 128 - vectors.shape[0])))
    grads_mix = jnp.concatenate(
        [
            d_w_in.astype(BF16),
            vector_columns.astype(BF16),
            d_w_out.astype(BF16).reshape(width, channels),
        ],
        1,
    )
    owned_mix = dp_scatter_small(grads_mix)

    def redeal(owned):
        block = owned[:, owned.shape[1] - channels :].reshape(-1, width)
        back = undeal_rows(block).reshape(slots, channels)
        return jnp.concatenate([owned[:, : owned.shape[1] - channels], back], 1)

    attn_cut = owned_attn.shape[1]
    shared_small = share(jnp.concatenate([redeal(owned_attn), redeal(owned_mix)], 1))
    (d_w_q, d_w_k, d_w_v), _ = split_columns(
        shared_small, [(1, channels), (1, kv_width), (1, kv_width)]
    )
    (d_w_in_full,), rest_mix = split_columns(
        [b[:, attn_cut:] for b in shared_small], [(3, channels)]
    )
    rest_attn = [b[:, attn_cut - channels : attn_cut] for b in shared_small]
    (d_wgate_two, d_wup_two, d_down_two), _ = split_columns(share(owned_two), [(1, hidden)] * 3)
    owned_one, d_wgate_two, d_wup_two, d_down_two, out = tie(
        owned_one, d_wgate_two, d_wup_two, d_down_two, out
    )
    (d_wgate_one, d_wup_one, d_down_one), _ = split_columns(share(owned_one), [(1, hidden)] * 3)
    d_w_o_full = jnp.concatenate([b.reshape(-1, width) for b in rest_attn], 0).astype(F32)
    d_w_out_full = jnp.concatenate([b[:, 128:].reshape(-1, width) for b in rest_mix], 0)
    d_w_out_full = d_w_out_full.astype(F32)
    sums = sum(b[:, :128].astype(F32) for b in rest_mix).T
    small_head = head // dp_count
    return (
        out,
        d_x,
        d_w_in_full,
        sums[4 : 4 + taps],
        d_w_out_full,
        d_wgate_one,
        d_wup_one,
        d_down_one,
        sums[0],
        sums[1],
        d_w_q,
        d_w_k,
        d_w_v,
        d_w_o_full,
        sums[4 + taps, :small_head],
        sums[5 + taps, :small_head],
        d_wgate_two,
        d_wup_two,
        d_down_two,
        sums[2],
        sums[3],
    )


def solution(mesh):
    matrix = P("dp", None)
    vector = P("dp")
    tokens = P("dp", "seq", None)
    kernel = P(None, "dp")
    in_specs = (
        (tokens, matrix, P("dp", "seq"), tokens, matrix, kernel)
        + (matrix,) * 4
        + (vector,) * 2
        + (matrix,) * 4
        + (vector,) * 2
        + (matrix,) * 3
        + (vector,) * 2
    )
    out_specs = (
        (tokens, tokens, matrix, kernel)
        + (matrix,) * 4
        + (vector,) * 2
        + (matrix,) * 4
        + (vector,) * 2
        + (matrix,) * 3
        + (vector,) * 2
    )
    return jax.shard_map(local, mesh=mesh, in_specs=in_specs, out_specs=out_specs, check_vma=False)
```

```python
import jax
import jax.numpy as jnp
from jax import lax
from jax.experimental import pallas as pl
from jax.experimental.pallas import tpu as pltpu
from jax.sharding import PartitionSpec as P

EPS = 1e-05
THETA = 1000000.0
NEG = -1e30
F32 = jnp.float32
BF16 = jnp.bfloat16
TILE = 256
LANES = 128
VMEM_LIMIT = 48 << 20


def left_dot(left, right):
    return lax.dot_general(left, right, (((0,), (0,)), ((), ())), preferred_element_type=F32)


def right_dot(left, right):
    return lax.dot_general(left, right, (((1,), (1,)), ((), ())), preferred_element_type=F32)


def plain_dot(left, right):
    return jnp.dot(left, right, preferred_element_type=F32)


def unit_scale(value):
    scale = lax.rsqrt(jnp.mean(value * value, -1, keepdims=True) + EPS)
    return (value * scale, scale)


def norm_back(grad_out, gain, unit, scale):
    weighted = grad_out * gain
    grad_in = scale * (weighted - unit * jnp.mean(weighted * unit, -1, keepdims=True))
    gain_grad = jnp.sum((grad_out * unit).reshape(-1, unit.shape[-1]), 0)
    return (grad_in, gain_grad)


def doc_index(bounds, places):
    later = bounds[1:]
    passed = (later <= places[..., None]) & (later > 0)
    return jnp.sum(passed.astype(jnp.int32), -1)


def doc_starts(bounds, places):
    return jnp.max(jnp.where(bounds <= places[..., None], bounds, 0), -1)


def rope_tables(places, head):
    half = head // 2
    freqs = THETA ** (-(2.0 * jnp.arange(half, dtype=F32)) / head)
    angles = places.astype(F32)[:, None] * freqs
    cosine = jnp.cos(angles)
    sine = jnp.sin(angles)
    return (
        jnp.concatenate([cosine] * 4, 1),
        jnp.concatenate([-sine, sine, -sine, sine], 1),
    )


def seq_bits():
    size = lax.axis_size("seq")
    bits = []
    bit = 1
    while bit < size:
        bits.append(bit)
        bit = bit * 2
    return bits


def swap_seq(array, bit):
    size = lax.axis_size("seq")
    return lax.ppermute(array, "seq", [(i, i ^ bit) for i in range(size)])


def tie(*values):
    return lax.optimization_barrier(values)


def near_blocks(block):
    have = {0: block}
    for bit in reversed(seq_bits()[:-1]):
        for place in sorted(have):
            have[place | bit] = swap_seq(have[place], bit)
    return [have[place] for place in sorted(have)]


def near_half(block):
    return jnp.concatenate(near_blocks(block), 0)


def far_half(block):
    return swap_seq(block, seq_bits()[-1])


def near_sum(half):
    size = lax.axis_size("seq") // 2
    length = half.shape[0] // size
    have = {place: half[place * length : (place + 1) * length] for place in range(size)}
    for bit in seq_bits()[:-1]:
        for place in sorted(have, reverse=True):
            if place & bit:
                got = swap_seq(have.pop(place).astype(BF16), bit).astype(F32)
                have[place ^ bit] = have[place ^ bit].astype(F32) + got
    return have[0].astype(F32)


def seq_scatter(near, far, *work):
    sent = far_half(near_sum(far).astype(BF16))
    kept = near_sum(near)
    sent, kept, *work = tie(sent, kept, *work)
    total = kept + sent.astype(F32)
    return (total, *work) if work else total


def flip_blocks(array):
    place = lax.axis_index("seq")
    for bit in seq_bits():
        shape = array.shape
        split = array.reshape((shape[0] // (2 * bit), 2, bit) + shape[1:])
        turned = jnp.concatenate([split[:, 1:], split[:, :1]], 1)
        array = jnp.where((place & bit) > 0, turned, split).reshape(shape)
    return array


def half_lanes(shape):
    return lax.broadcasted_iota(jnp.int32, shape, 1) < LANES // 2


def head_mean(value):
    row = lax.broadcasted_iota(jnp.int32, (LANES, LANES), 0) < LANES // 2
    column = half_lanes((LANES, LANES))
    ones = jnp.where(row == column, 2.0 / LANES, 0.0).astype(BF16)
    high = value.astype(BF16)
    low = (value - high.astype(F32)).astype(BF16)
    return plain_dot(high, ones) + plain_dot(low, ones)


def swap_quarters(value):
    quarter = LANES // 4
    lane = lax.broadcasted_iota(jnp.int32, value.shape, 1)
    first = (lane // quarter) % 2 == 0
    return jnp.where(
        first, pltpu.roll(value, LANES - quarter, 1), pltpu.roll(value, quarter, 1)
    )


def head_unit(value):
    scale = lax.rsqrt(head_mean(value * value) + EPS)
    return (value * scale, scale)


def pad_pair(value, second):
    lower = half_lanes(value.shape)
    if second:
        high = jnp.where(lower, 0.0, value)
        return (pltpu.roll(high, LANES // 2, 1), high)
    low = jnp.where(lower, value, 0.0)
    return (low, pltpu.roll(low, LANES // 2, 1))


def load_heads(raw_ref, cos_ref, sin_ref, gains_ref, rows, target, length, pairs):
    cosine = cos_ref[pl.ds(target, length), :]
    sine = sin_ref[pl.ds(target, length), :]
    groups = raw_ref.shape[1] // LANES

    def turned(group, gain):
        value = head_unit(raw_ref[rows, group * LANES : (group + 1) * LANES])[0] * gain
        return value * cosine + swap_quarters(value) * sine

    scale = (LANES // 2) ** (-0.5)
    queries = [(turned(g, gains_ref[0:1, :]) * scale).astype(BF16) for g in range(pairs)]
    keys = []
    values = []
    cached = {}
    for g in range(pairs):
        place = pairs * LANES + g * (LANES // 2)
        group, second = divmod(place, LANES)
        if group not in cached:
            cached[group] = turned(group, gains_ref[1:2, :]).astype(BF16).astype(F32)
        keys.append([k.astype(BF16) for k in pad_pair(cached[group], second > 0)])
        place = place + pairs * (LANES // 2)
        group, second = divmod(place, LANES)
        value = raw_ref[rows, group * LANES : (group + 1) * LANES]
        values.append([v.astype(BF16) for v in pad_pair(value, second > 0)])
    return (queries, keys, values)


def allowed_tile(start_ref, first_key, first_query):
    query = first_query + lax.broadcasted_iota(jnp.int32, (1, TILE), 1)
    start = start_ref[0:1, pl.ds(first_query, TILE)]
    key = first_key + lax.broadcasted_iota(jnp.int32, (TILE, TILE), 0)
    return (key >= start) & (key <= query)


def block_rows(block, count, length):
    half, offset = divmod(block, count // 2)
    return (half, slice(offset * length, (offset + 1) * length))


def attention_forward_kernel(place_ref, *refs, length, pairs, tokens):
    token_refs = refs[:tokens]
    (
        qkv_ref, o_ref, cos_ref, sin_ref, start_ref, gains_ref,
        raw_ref, out_ref, wide_ref, total_ref, near_out_ref, far_out_ref,
        query_ref, key_ref, value_ref,
    ) = refs[tokens:]
    full = raw_ref.shape[0]
    count = full // length
    place = place_ref[0]

    for block in range(count):
        target = pl.multiple_of((block ^ place) * length, 8)
        source = slice(block * length, (block + 1) * length)
        raw_ref[source, :] = plain_dot(token_refs[block][...], qkv_ref[...])
        queries, keys, values = load_heads(
            raw_ref, cos_ref, sin_ref, gains_ref, source, target, length, pairs
        )
        for g in range(pairs):
            query_ref[g, pl.ds(target, length), :] = queries[g]
            for h in range(2):
                key_ref[2 * g + h, pl.ds(target, length), :] = keys[g][h]
                value_ref[2 * g + h, pl.ds(target, length), :] = values[g][h]

    half = LANES // 2

    def query_tile(i, _):
        first_query = pl.multiple_of(i * TILE, TILE)

        def key_tile(j, carry):
            first_key = pl.multiple_of(j * TILE, TILE)
            allowed = allowed_tile(start_ref, first_key, first_query)
            sums, outs = carry
            new_sums = []
            new_outs = []
            for g in range(pairs):
                query = query_ref[g, pl.ds(first_query, TILE), :]
                total = outs[g]
                for h in range(2):
                    key = key_ref[2 * g + h, pl.ds(first_key, TILE), :]
                    value = value_ref[2 * g + h, pl.ds(first_key, TILE), :]
                    weight = jnp.where(allowed, jnp.exp(right_dot(key, query)), 0.0)
                    new_sums.append(sums[2 * g + h] + jnp.sum(weight, 0, keepdims=True))
                    total = total + lax.dot_general(
                        value, weight.astype(BF16), (((0,), (0,)), ((), ())),
                        preferred_element_type=F32,
                    )
                new_outs.append(total)
            return (new_sums, new_outs)

        carry = (
            [jnp.zeros((1, TILE), F32) for _ in range(2 * pairs)],
            [jnp.zeros((LANES, TILE), F32) for _ in range(pairs)],
        )
        sums, outs = lax.fori_loop(0, i + 1, key_tile, carry)
        columns = pl.ds(first_query, TILE)
        for g in range(pairs):
            scaled = jnp.concatenate(
                [outs[g][h * half : (h + 1) * half] / sums[2 * g + h] for h in range(2)], 0
            )
            for h in range(2):
                total_ref[2 * g + h : 2 * g + h + 1, columns] = sums[2 * g + h]
            wide_ref[g * LANES : (g + 1) * LANES, columns] = scaled
            query_ref[g, columns, :] = scaled.T.astype(BF16)
        return 0

    lax.fori_loop(0, full // TILE, query_tile, 0)

    for block in range(count):
        side, rows = block_rows(block, count, length)
        source = pl.multiple_of((block ^ place) * length, 8)
        target = slice(block * length, (block + 1) * length)
        for g in range(pairs):
            out_ref[target, g * LANES : (g + 1) * LANES] = query_ref[
                g, pl.ds(source, length), :
            ]
        partial = plain_dot(out_ref[target, :], o_ref[...])
        (near_out_ref, far_out_ref)[side][rows, :] = partial.astype(BF16)


def attention_backward_kernel(place_ref, *refs, length, pairs, tokens):
    token_refs = refs[:tokens]
    (
        qkv_ref, o_ref, cos_ref, sin_ref, start_ref, gains_ref, raw_ref, wide_ref, total_ref,
        out_ref, near_out_ref, far_out_ref, gain_grad_ref,
        query_ref, key_ref, value_ref, hold_ref, dq_ref, dk_ref, dv_ref,
    ) = refs[tokens:]
    full = raw_ref.shape[0]
    count = full // length
    place = place_ref[0]
    half = LANES // 2

    for block in range(count):
        target = pl.multiple_of((block ^ place) * length, 8)
        source = slice(block * length, (block + 1) * length)
        grads = right_dot(token_refs[block][...], o_ref[...]).astype(BF16)
        queries, keys, values = load_heads(
            raw_ref, cos_ref, sin_ref, gains_ref, source, target, length, pairs
        )
        rows = pl.ds(target, length)
        for g in range(pairs):
            query_ref[g, rows, :] = queries[g]
            hold_ref[g, rows, :] = grads[:, g * LANES : (g + 1) * LANES]
            dk_ref[g, rows, :] = jnp.zeros((length, LANES), F32)
            dv_ref[g, rows, :] = jnp.zeros((length, LANES), F32)
            for h in range(2):
                key_ref[2 * g + h, rows, :] = keys[g][h]
                value_ref[2 * g + h, rows, :] = values[g][h]

    lower = half_lanes((TILE, LANES))

    def query_tile(i, _):
        first_query = pl.multiple_of(i * TILE, TILE)
        columns = pl.ds(first_query, TILE)
        inverse = [1.0 / total_ref[n : n + 1, columns] for n in range(2 * pairs)]
        inner = []
        for g in range(pairs):
            grad = hold_ref[g, columns, :].astype(F32).T
            both = grad * wide_ref[g * LANES : (g + 1) * LANES, columns]
            for h in range(2):
                inner.append(jnp.sum(both[h * half : (h + 1) * half], 0, keepdims=True))

        def key_tile(j, outs):
            first_key = pl.multiple_of(j * TILE, TILE)
            rows = pl.ds(first_key, TILE)
            allowed = allowed_tile(start_ref, first_key, first_query)
            new_outs = []
            for g in range(pairs):
                query = query_ref[g, columns, :]
                grad = hold_ref[g, columns, :]
                zero = jnp.zeros_like(query)
                total = outs[g]
                d_key = dk_ref[g, rows, :]
                d_value = dv_ref[g, rows, :]
                for h in range(2):
                    keep = lower if h == 0 else jnp.logical_not(lower)
                    key = key_ref[2 * g + h, rows, :]
                    value = value_ref[2 * g + h, rows, :]
                    weight = jnp.exp(right_dot(key, query)) * inverse[2 * g + h]
                    weight = jnp.where(allowed, weight, 0.0)
                    d_weight = right_dot(value, grad)
                    d_score = (weight * (d_weight - inner[2 * g + h])).astype(BF16)
                    d_value = d_value + plain_dot(
                        weight.astype(BF16), jnp.where(keep, grad, zero)
                    )
                    d_key = d_key + plain_dot(d_score, jnp.where(keep, query, zero))
                    total = total + lax.dot_general(
                        key, d_score, (((0,), (0,)), ((), ())), preferred_element_type=F32
                    )
                dk_ref[g, rows, :] = d_key
                dv_ref[g, rows, :] = d_value
                new_outs.append(total)
            return new_outs

        outs = lax.fori_loop(
            0, i + 1, key_tile, [jnp.zeros((LANES, TILE), F32) for _ in range(pairs)]
        )
        for g in range(pairs):
            dq_ref[g, columns, :] = outs[g].T
        return 0

    lax.fori_loop(0, full // TILE, query_tile, 0)
    scale = half ** (-0.5)

    low = half_lanes((length, LANES))
    query_gain = jnp.zeros((1, LANES), F32)
    key_gain = jnp.zeros((1, LANES), F32)
    for block in range(count):
        side, side_rows = block_rows(block, count, length)
        rows = pl.ds(pl.multiple_of((block ^ place) * length, 8), length)
        target = slice(block * length, (block + 1) * length)
        cosine = cos_ref[rows, :]
        sine = sin_ref[rows, :]

        def back(grad, group, gain):
            grad = grad.astype(BF16).astype(F32)
            unit, inverse = head_unit(raw_ref[target, group * LANES : (group + 1) * LANES])
            d_rot = grad * cosine + swap_quarters(grad * sine)
            weighted = d_rot * gain
            d_raw = inverse * (weighted - unit * head_mean(weighted * unit))
            return (d_raw, d_rot * unit)

        for g in range(pairs):
            d_raw, terms = back(dq_ref[g, rows, :] * scale, g, gains_ref[0:1, :])
            query_gain = query_gain + jnp.sum(terms, 0, keepdims=True)
            out_ref[target, g * LANES : (g + 1) * LANES] = d_raw.astype(BF16)
        groups = {}
        for kind, held in ((0, dk_ref), (1, dv_ref)):
            for g in range(pairs):
                place_of = pairs * LANES + kind * pairs * half + g * half
                group, second = divmod(place_of, LANES)
                value = held[g, rows, :]
                value = value + pltpu.roll(value, half, 1)
                groups.setdefault(group, {})[second // half] = (kind, value)
        for group, parts in groups.items():
            merged = jnp.where(low, parts[0][1], parts[1][1])
            is_key = [parts[n][0] == 0 for n in range(2)]
            result = merged
            if any(is_key):
                d_raw, terms = back(merged, group, gains_ref[1:2, :])
                if not is_key[1]:
                    d_raw = jnp.where(low, d_raw, merged)
                    terms = jnp.where(low, terms, 0.0)
                result = d_raw
                key_gain = key_gain + jnp.sum(terms, 0, keepdims=True)
            out_ref[target, group * LANES : (group + 1) * LANES] = result.astype(BF16)
        partial = right_dot(out_ref[target, :], qkv_ref[...])
        (near_out_ref, far_out_ref)[side][side_rows, :] = partial.astype(BF16)
    gain_grad_ref[0:1, :] = query_gain
    gain_grad_ref[1:2, :] = key_gain


def whole(count):
    return [pl.BlockSpec(memory_space=pltpu.VMEM)] * count


def attention_forward(place, tokens, qkv, o, cosine, sine, start, gains):
    length = tokens[0].shape[0]
    full = len(tokens) * length
    width, columns = qkv.shape
    pairs = columns // (2 * LANES)
    return pl.pallas_call(
        lambda *refs: attention_forward_kernel(
            *refs, length=length, pairs=pairs, tokens=len(tokens)
        ),
        in_specs=[pl.BlockSpec(memory_space=pltpu.SMEM)] + whole(6 + len(tokens)),
        out_specs=tuple(whole(6)),
        out_shape=(
            jax.ShapeDtypeStruct((full, columns), F32),
            jax.ShapeDtypeStruct((full, pairs * LANES), BF16),
            jax.ShapeDtypeStruct((pairs * LANES, full), F32),
            jax.ShapeDtypeStruct((8, full), F32),
            jax.ShapeDtypeStruct((full // 2, width), BF16),
            jax.ShapeDtypeStruct((full // 2, width), BF16),
        ),
        scratch_shapes=[
            pltpu.VMEM((pairs, full, LANES), BF16),
            pltpu.VMEM((2 * pairs, full, LANES), BF16),
            pltpu.VMEM((2 * pairs, full, LANES), BF16),
        ],
        cost_estimate=pl.CostEstimate(
            flops=20_000_000_000, transcendentals=6_000_000, bytes_accessed=20_000_000
        ),
        compiler_params=pltpu.CompilerParams(vmem_limit_bytes=VMEM_LIMIT),
        name="attention_forward",
    )(place, *tokens, qkv, o, cosine, sine, start, gains)


def attention_backward(place, tokens, qkv, o, cosine, sine, start, gains, raw, wide, totals):
    length = tokens[0].shape[0]
    full = len(tokens) * length
    width, columns = qkv.shape
    pairs = columns // (2 * LANES)
    return pl.pallas_call(
        lambda *refs: attention_backward_kernel(
            *refs, length=length, pairs=pairs, tokens=len(tokens)
        ),
        in_specs=[pl.BlockSpec(memory_space=pltpu.SMEM)] + whole(9 + len(tokens)),
        out_specs=tuple(whole(4)),
        out_shape=(
            jax.ShapeDtypeStruct((full, columns), BF16),
            jax.ShapeDtypeStruct((full // 2, width), BF16),
            jax.ShapeDtypeStruct((full // 2, width), BF16),
            jax.ShapeDtypeStruct((2, LANES), F32),
        ),
        scratch_shapes=[
            pltpu.VMEM((pairs, full, LANES), BF16),
            pltpu.VMEM((2 * pairs, full, LANES), BF16),
            pltpu.VMEM((2 * pairs, full, LANES), BF16),
            pltpu.VMEM((pairs, full, LANES), BF16),
            pltpu.VMEM((pairs, full, LANES), F32),
            pltpu.VMEM((pairs, full, LANES), F32),
            pltpu.VMEM((pairs, full, LANES), F32),
        ],
        cost_estimate=pl.CostEstimate(
            flops=20_000_000_000, transcendentals=6_000_000, bytes_accessed=20_000_000
        ),
        compiler_params=pltpu.CompilerParams(vmem_limit_bytes=VMEM_LIMIT),
        name="attention_backward",
    )(place, *tokens, qkv, o, cosine, sine, start, gains, raw, wide, totals)


def column_block(weight, parts):
    size = lax.axis_size("seq")
    place = lax.axis_index("seq")
    rows, columns = weight.shape
    block = columns // parts // size
    split = weight.reshape(rows, parts, size * block)
    return lax.dynamic_slice_in_dim(split, place * block, block, 2).reshape(rows, parts * block)


def deal_pairs():
    size = lax.axis_size("seq")
    count = lax.axis_size("dp")
    pairs = []
    for place in range(size):
        for owner in range(count):
            source = (owner % size) * count + place * (count // size) + owner // size
            pairs.append((source, place * count + owner))
    return pairs


def deal_rows(weight):
    size = lax.axis_size("seq")
    place = lax.axis_index("seq")
    piece = weight.shape[0] // size
    part = lax.dynamic_slice_in_dim(weight, place * piece, piece, 0)
    return lax.ppermute(part, ("seq", "dp"), deal_pairs())


def pack_piece(piece, columns):
    count = piece.shape[1] // columns
    return jnp.concatenate(
        [piece[:, n * columns : (n + 1) * columns] for n in range(count)], 0
    )


def unpack_piece(block, width):
    count = width // block.shape[1]
    rows = block.shape[0] // count
    return jnp.concatenate([block[n * rows : (n + 1) * rows] for n in range(count)], 1)


def pack_rows(rows_block, parts):
    rows, width = rows_block.shape
    piece = rows // parts
    split = rows_block.reshape(parts, piece, width // rows, rows)
    return jnp.swapaxes(split, 1, 2).reshape(width, rows)


def unpack_rows(block, parts):
    width, rows = block.shape
    split = block.reshape(parts, width // rows, rows // parts, rows)
    return jnp.swapaxes(split, 1, 2).reshape(rows, width)


def undeal_rows(part):
    return lax.ppermute(part, ("seq", "dp"), [(b, a) for a, b in deal_pairs()])


def dp_gather(block):
    return lax.all_gather(block, "dp", axis=0, tiled=True)


def dp_scatter(grads):
    return lax.psum_scatter(grads, "dp", scatter_dimension=0, tiled=True)


def swap_dp(array, bit):
    size = lax.axis_size("dp")
    return lax.ppermute(array, "dp", [(i, i ^ bit) for i in range(size)])


def dp_bits():
    return [1, 2, 4] if lax.axis_size("dp") == 8 else []


def dp_gather_small(block, later):
    if not dp_bits():
        return (dp_gather(block), later)
    size = lax.axis_size("dp")
    place = lax.axis_index("dp")
    rows = block.shape[0]
    turns = [0]
    held = block
    for bit in reversed(dp_bits()):
        got = swap_dp(held, bit)
        if bit == dp_bits()[1]:
            got, later = tie(got, later)
        held = jnp.concatenate([held, got], 0)
        turns = turns + [turn | bit for turn in turns]
    result = jnp.zeros((size * rows, block.shape[1]), block.dtype)
    for number, turn in enumerate(turns):
        piece = held[number * rows : (number + 1) * rows]
        result = lax.dynamic_update_slice_in_dim(result, piece, (place ^ turn) * rows, 0)
    return (result, later)


def share(owned):
    return near_blocks(owned) + near_blocks(far_half(owned))


def assemble_kernel(place_ref, *refs, count, tasks):
    blocks = refs[:count]
    outs = refs[count:]
    place = place_ref[0]
    for turn in range(count):
        for target in range(count):

            @pl.when((place ^ turn) == target)
            def _():
                for (start, columns, split, by_rows), out_ref in zip(tasks, outs):
                    if by_rows:
                        rows = blocks[turn].shape[0] // count
                        for part in range(count):
                            out_ref[
                                target * rows : (target + 1) * rows,
                                part * columns : (part + 1) * columns,
                            ] = blocks[turn][
                                part * rows : (part + 1) * rows, start : start + columns
                            ].astype(F32)
                    else:
                        step = columns // split
                        for part in range(split):
                            first = (part * count + target) * step
                            out_ref[:, first : first + step] = blocks[turn][
                                :, start + part * step : start + (part + 1) * step
                            ].astype(F32)


def assemble(place, blocks, tasks):
    count = len(blocks)
    rows = blocks[0].shape[0]
    if all(columns // split % LANES == 0 for _, columns, split, _ in tasks):
        return pl.pallas_call(
            lambda *refs: assemble_kernel(*refs, count=count, tasks=tasks),
            in_specs=[pl.BlockSpec(memory_space=pltpu.SMEM)] + whole(count),
            out_specs=tuple(whole(len(tasks))),
            out_shape=tuple(
                jax.ShapeDtypeStruct((rows, count * columns), F32) for _, columns, _, _ in tasks
            ),
            compiler_params=pltpu.CompilerParams(vmem_limit_bytes=VMEM_LIMIT),
            name="assemble",
        )(place, *blocks)
    stacked = jnp.stack(blocks, 0)
    ordered = [
        lax.dynamic_index_in_dim(stacked, place[0] ^ i, 0, False) for i in range(count)
    ]
    results = []
    for start, columns, split, by_rows in tasks:
        parts = [block[:, start : start + columns] for block in ordered]
        if by_rows:
            joined = jnp.concatenate([unpack_piece(p, count * columns) for p in parts], 0)
        else:
            step = columns // split
            joined = jnp.concatenate(
                [p[:, n * step : (n + 1) * step] for n in range(split) for p in parts], 1
            )
        results.append(joined.astype(F32))
    return results


def gate_terms(normed, w_gate, w_up):
    gate = plain_dot(normed, w_gate)
    upper = plain_dot(normed, w_up)
    sigma = jax.nn.sigmoid(gate)
    swish = gate * sigma
    return (upper * (sigma + swish * (1.0 - sigma)), swish, swish * upper)


def block_here(refs):
    value = refs[0][...]
    for number, ref in enumerate(refs[1:]):
        value = jnp.where(pl.program_id(0) == number + 1, ref[...], value)
    return value


def ffn_forward_kernel(*refs, count):
    normed_refs = refs[:count]
    gate_ref, up_ref, down_ref = refs[count : count + 3]
    kept_ref, partial_ref = refs[-2:]
    hidden = gate_ref.shape[1]
    slope, swish, act = gate_terms(block_here(normed_refs), gate_ref[...], up_ref[...])
    act = act.astype(BF16)
    kept_ref[:, :hidden] = slope.astype(BF16)
    kept_ref[:, hidden : 2 * hidden] = swish.astype(BF16)
    kept_ref[:, 2 * hidden :] = act
    partial_ref[...] = right_dot(act, down_ref[...]).astype(BF16)


def ffn_turn_kernel(*refs, count):
    normed_refs = refs[:count]
    grad_refs = refs[count : 2 * count]
    gate_ref, up_ref, down_ref = refs[2 * count : 2 * count + 3]
    kept_ref, partial_ref = refs[-2:]
    hidden = gate_ref.shape[1]
    slope, swish, act = gate_terms(block_here(normed_refs), gate_ref[...], up_ref[...])
    d_act = plain_dot(block_here(grad_refs), down_ref[...])
    d_gate = (d_act * slope).astype(BF16)
    d_up = (d_act * swish).astype(BF16)
    kept_ref[:, :hidden] = d_gate
    kept_ref[:, hidden : 2 * hidden] = d_up
    kept_ref[:, 2 * hidden :] = act.astype(BF16)
    partial = right_dot(d_gate, gate_ref[...]) + right_dot(d_up, up_ref[...])
    partial_ref[...] = partial.astype(BF16)


def ffn_backward_kernel(*refs, count):
    grad_refs = refs[:count]
    terms_ref, gate_ref, up_ref, down_ref = refs[count : count + 4]
    kept_ref, partial_ref = refs[-2:]
    hidden = gate_ref.shape[1]
    d_act = plain_dot(block_here(grad_refs), down_ref[...])
    d_gate = (d_act * terms_ref[:, :hidden].astype(F32)).astype(BF16)
    d_up = (d_act * terms_ref[:, hidden:].astype(F32)).astype(BF16)
    kept_ref[:, :hidden] = d_gate
    kept_ref[:, hidden:] = d_up
    partial = right_dot(d_gate, gate_ref[...]) + right_dot(d_up, up_ref[...])
    partial_ref[...] = partial.astype(BF16)


def ffn_call(kernel, name, tokens, terms, weights, hidden, first, full, kept_width, kept):
    width = weights.shape[0]
    count = len(tokens[0])
    length = tokens[0][0].shape[0]
    operands = [block for blocks in tokens for block in blocks]
    in_specs = [
        pl.BlockSpec((length, width), lambda i: (0, 0), pipeline_mode=pl.Buffered(1))
        for _ in operands
    ]
    if terms is not None:
        in_specs.append(pl.BlockSpec((length, 2 * hidden), lambda i: (i + first, 0)))
        operands.append(terms)
    for place in range(3):
        in_specs.append(
            pl.BlockSpec(
                (width, hidden), lambda i, place=place: (0, place), pipeline_mode=pl.Buffered(1)
            )
        )
        operands.append(weights)
    aliases = {}
    if kept is not None:
        aliases = {len(operands): 0}
        in_specs.append(pl.BlockSpec(memory_space=pl.ANY))
        operands.append(kept)
    return pl.pallas_call(
        lambda *refs: kernel(*refs, count=count),
        grid=(count,),
        in_specs=in_specs,
        out_specs=(
            pl.BlockSpec((length, kept_width), lambda i: (i + first, 0)),
            pl.BlockSpec((length, width), lambda i: (i, 0)),
        ),
        out_shape=(
            jax.ShapeDtypeStruct((full, kept_width), BF16),
            jax.ShapeDtypeStruct((count * length, width), BF16),
        ),
        input_output_aliases=aliases,
        cost_estimate=pl.CostEstimate(
            flops=6_000_000_000, transcendentals=1_000_000, bytes_accessed=20_000_000
        ),
        compiler_params=pltpu.CompilerParams(vmem_limit_bytes=VMEM_LIMIT),
        name=name,
    )(*operands)


def split_weights(weights, hidden):
    return [weights[:, n * hidden : (n + 1) * hidden] for n in range(3)]


def halves_of(array):
    half = array.shape[0] // 2
    return (array[:half], array[half:])


def place_rows(kept, part, number):
    if kept is None:
        kept = jnp.zeros((2 * part.shape[0], part.shape[1]), part.dtype)
    return lax.dynamic_update_slice_in_dim(kept, part, number * part.shape[0], 0)


def ffn_forward(normed, weights, hidden):
    if hidden % LANES:
        w_gate, w_up, w_down = split_weights(weights, hidden)
        terms = gate_terms(jnp.concatenate(normed, 0), w_gate, w_up)
        terms = jnp.concatenate(terms, 1).astype(BF16)
        return (terms, right_dot(terms[:, 2 * hidden :], w_down).astype(BF16))
    return ffn_call(
        ffn_forward_kernel, "ffn_forward", [normed], None, weights, hidden,
        0, len(normed) * normed[0].shape[0], 3 * hidden, None,
    )


def ffn_turn(normed, grads, weights, hidden, number, kept):
    if hidden % LANES:
        w_gate, w_up, w_down = split_weights(weights, hidden)
        slope, swish, act = gate_terms(jnp.concatenate(normed, 0), w_gate, w_up)
        d_act = plain_dot(jnp.concatenate(grads, 0), w_down)
        part = jnp.concatenate([d_act * slope, d_act * swish, act], 1).astype(BF16)
        partial = right_dot(part[:, : 2 * hidden], weights[:, : 2 * hidden]).astype(BF16)
        return (place_rows(kept, part, number), partial)
    count = len(normed)
    return ffn_call(
        ffn_turn_kernel, "ffn_turn", [normed, grads], None, weights, hidden,
        number * count, 2 * count * normed[0].shape[0], 3 * hidden, kept,
    )


def ffn_backward(grads, terms, weights, hidden, number, kept):
    count = len(grads)
    length = grads[0].shape[0]
    if hidden % LANES:
        w_gate, w_up, w_down = split_weights(weights, hidden)
        rows = slice(number * count * length, (number + 1) * count * length)
        d_act = plain_dot(jnp.concatenate(grads, 0), w_down)
        slope = terms[rows, :hidden].astype(F32)
        swish = terms[rows, hidden : 2 * hidden].astype(F32)
        part = jnp.concatenate([d_act * slope, d_act * swish], 1).astype(BF16)
        partial = right_dot(part, weights[:, : 2 * hidden]).astype(BF16)
        return (place_rows(kept, part, number), partial)
    return ffn_call(
        ffn_backward_kernel, "ffn_backward", [grads], terms, weights, hidden,
        number * count, 2 * count * length, 2 * hidden, kept,
    )


def conv_forward_kernel(*refs, length, tokens, taps):
    place_ref, bounds_ref = refs[:2]
    token_refs = refs[2 : 2 + tokens]
    (
        in_ref, out_w_ref, tap_ref, gain_ref,
        normed_ref, projected_ref, gated_ref, near_out_ref, far_out_ref, product_ref,
    ) = refs[2 + tokens :]
    place = place_ref[0]
    channels = gated_ref.shape[1]
    product_ref[0:8, :] = jnp.zeros((8, channels), F32)
    for block in range(tokens):
        rows = slice(block * length, (block + 1) * length)
        value = token_refs[block][...].astype(F32)
        scale = lax.rsqrt(jnp.mean(value * value, -1, keepdims=True) + EPS)
        normed = (value * scale * gain_ref[...]).astype(BF16)
        normed_ref[rows, :] = normed
        projected = plain_dot(normed, in_ref[:, : 3 * channels])
        projected_ref[rows, :] = projected
        product = (projected[:, :channels] * projected[:, 2 * channels :]).astype(BF16)
        target = pl.multiple_of(8 + (block ^ place) * length, 8)
        product_ref[pl.ds(target, length), :] = product.astype(F32)
    for block in range(tokens):
        side, side_rows = block_rows(block, tokens, length)
        rows = slice(block * length, (block + 1) * length)
        first = pl.multiple_of((block ^ place) * length, 8)
        window = product_ref[pl.ds(first, length + 8), :]
        token = first + lax.broadcasted_iota(jnp.int32, (length, channels), 0)
        start = jnp.zeros((length, channels), jnp.int32)
        for number in range(1, bounds_ref.shape[0]):
            bound = bounds_ref[number]
            start = jnp.where(bound <= token, jnp.maximum(start, bound), start)
        conv = tap_ref[0:1, :] * window[8:, :]
        for tap in range(1, taps):
            moved = window[8 - tap : 8 - tap + length, :]
            moved = jnp.where(token - tap >= start, moved, 0.0)
            conv = conv + tap_ref[tap : tap + 1, :] * moved
        gated = (projected_ref[rows, channels : 2 * channels] * conv).astype(BF16)
        gated_ref[rows, :] = gated
        partial = plain_dot(gated, out_w_ref[...]).astype(BF16)
        (near_out_ref, far_out_ref)[side][side_rows, :] = partial


def conv_forward(place, bounds, tokens, in_weights, out_weights, kernel, gain):
    length, width = tokens[0].shape
    full = len(tokens) * length
    channels = out_weights.shape[0]
    taps = kernel.shape[0]
    scalar = pl.BlockSpec(memory_space=pltpu.SMEM)
    return pl.pallas_call(
        lambda *refs: conv_forward_kernel(*refs, length=length, tokens=len(tokens), taps=taps),
        in_specs=[scalar, scalar] + whole(len(tokens) + 4),
        out_specs=tuple(whole(5)),
        out_shape=(
            jax.ShapeDtypeStruct((full, width), BF16),
            jax.ShapeDtypeStruct((full, 3 * channels), F32),
            jax.ShapeDtypeStruct((full, channels), BF16),
            jax.ShapeDtypeStruct((full // 2, width), BF16),
            jax.ShapeDtypeStruct((full // 2, width), BF16),
        ),
        scratch_shapes=[pltpu.VMEM((full + 8, channels), F32)],
        cost_estimate=pl.CostEstimate(
            flops=4_000_000_000, transcendentals=2_000, bytes_accessed=20_000_000
        ),
        compiler_params=pltpu.CompilerParams(vmem_limit_bytes=VMEM_LIMIT),
        name="conv_forward",
    )(place, bounds, *tokens, in_weights, out_weights, kernel, gain)


def local(
    x_in,
    cu_seqlens,
    positions,
    cotangent,
    w_in,
    conv_w,
    w_out,
    w_gate1,
    w_up1,
    w_down1,
    g_mix1,
    g_ffn1,
    w_q,
    key_projection_weight,
    value_projection_weight,
    w_o,
    g_q,
    g_k,
    w_gate2,
    w_up2,
    w_down2,
    g_attn2,
    g_ffn2,
):
    rows, length, width = x_in.shape
    assert rows == 1
    seq_count = lax.axis_size("seq")
    dp_count = lax.axis_size("dp")
    seq_place = lax.axis_index("seq")
    full = length * seq_count
    channels = width // seq_count
    slots = width // dp_count
    head = g_q.shape[0] * dp_count
    taps = conv_w.shape[0]
    reach = taps - 1

    x_far = far_half(x_in.reshape(length, width))
    cotangent_low, x_far = tie(cotangent.reshape(length, width), x_far)
    x_blocks = near_blocks(x_in.reshape(length, width)) + near_blocks(x_far)
    cotangent_blocks = near_blocks(cotangent_low) + near_blocks(far_half(cotangent_low))
    head_gains = jnp.pad(jnp.stack([g_q, g_k], 1), ((0, slots - head // dp_count), (0, 0)))
    small = jnp.concatenate(
        [conv_w.T, jnp.stack([g_mix1, g_ffn1, g_attn2, g_ffn2], 1), head_gains], 1
    )
    small = jnp.pad(small, ((0, 0), (0, 128 - small.shape[1])))
    dealt = deal_rows(jnp.stack([w_out, w_o], 1))
    out_piece = pack_piece(dealt[:, 0], channels)
    o_piece = pack_piece(dealt[:, 1], channels)
    mix_block = jnp.concatenate([column_block(w_in, 3), small, out_piece], 1)
    mix_block, w_gate1, w_up1, w_down1, w_q, key_projection_weight, value_projection_weight = tie(
        mix_block, w_gate1, w_up1, w_down1, w_q, key_projection_weight, value_projection_weight
    )
    hidden = w_gate1.shape[1] // seq_count
    ffn_one = jnp.concatenate(
        [
            column_block(w, 1)
            for w in (
                w_gate1, w_up1, w_down1, w_q, key_projection_weight, value_projection_weight
            )
        ]
        + [o_piece],
        1,
    )
    mix_all, ffn_one = dp_gather_small(mix_block, ffn_one)
    ffn_one = dp_gather(ffn_one)
    attn_all = ffn_one[:, 3 * hidden :]
    ffn_two = dp_gather(
        jnp.concatenate([column_block(w, 1) for w in (w_gate2, w_up2, w_down2)], 1)
    )
    qkv_width = attn_all.shape[1] - channels
    qkv_block = attn_all[:, :qkv_width]
    o_block = unpack_rows(attn_all[:, qkv_width:], dp_count)
    bounds = cu_seqlens[0]
    turn = seq_place ^ jnp.arange(seq_count, dtype=jnp.int32)
    places = turn[:, None] * length + jnp.arange(length, dtype=jnp.int32)[None, :]
    docs_here = doc_index(bounds, places)
    masks = [
        (doc_index(bounds, places - tap) == docs_here).astype(F32)[..., None]
        for tap in range(1, reach + 1)
    ]

    order = jnp.arange(full, dtype=jnp.int32)
    starts = doc_starts(bounds, order)
    cosine, sine = rope_tables(order - starts, head)
    starts = starts[None, :]
    place = seq_place.reshape(1).astype(jnp.int32)
    mix_all, cosine, sine, starts, *cotangent_blocks = tie(
        mix_all, cosine, sine, starts, *cotangent_blocks
    )
    in_block = mix_all[:, : 3 * channels]
    out_block = unpack_rows(mix_all[:, 3 * channels + 128 :], dp_count)
    small_all = mix_all[:, 3 * channels : 3 * channels + 128].astype(F32).T
    kernel = lax.dynamic_slice_in_dim(small_all[:taps], seq_place * channels, channels, 1)
    gain_mix, gain_ffn_one, gain_attn, gain_ffn_two = (small_all[taps + i] for i in range(4))
    head_gains = small_all[taps + 4 : taps + 6].reshape(2, dp_count, slots)
    head_gains = jnp.tile(head_gains[:, :, : head // dp_count].reshape(2, head), (1, 2))

    x_flat = x_in.reshape(length, width).astype(F32)
    normed_one, projected, gated, near_out, far_out = conv_forward(
        place, bounds, x_blocks, mix_all, out_block, kernel, gain_mix[None, :]
    )
    hidden_one = x_flat + seq_scatter(near_out, far_out)

    unit_two, scale_two = unit_scale(hidden_one)
    near_two = (unit_two * gain_ffn_one).astype(BF16)
    far_two = far_half(near_two)
    blocks_two = near_blocks(near_two) + near_blocks(far_two)
    terms_one, partial_one = ffn_forward(blocks_two, ffn_one, hidden)
    hidden_two = hidden_one + seq_scatter(*halves_of(partial_one))

    unit_three, scale_three = unit_scale(hidden_two)
    near_three = (unit_three * gain_attn).astype(BF16)
    blocks_three = near_blocks(near_three) + near_blocks(far_half(near_three))
    kv_width = (qkv_width - channels) // 2
    raw, attended_low, wide, totals, near_out, far_out = attention_forward(
        place, blocks_three, qkv_block, o_block, cosine, sine, starts, head_gains
    )
    hidden_three = hidden_two + seq_scatter(near_out, far_out)

    unit_four, scale_four = unit_scale(hidden_three)
    near_four = (unit_four * gain_ffn_two).astype(BF16)
    far_four = far_half(near_four)
    near_four = near_blocks(near_four)
    half = len(near_four)
    kept_two, near_out = ffn_turn(
        near_four, cotangent_blocks[:half], ffn_two, hidden, 0, None
    )
    far_four, near_out = tie(far_four, near_out)
    far_four = near_blocks(far_four)
    kept_two, far_out = ffn_turn(
        far_four, cotangent_blocks[half:], ffn_two, hidden, 1, kept_two
    )

    grad_four = cotangent.reshape(length, width).astype(F32)
    kept_two, far_out = tie(kept_two, far_out)
    normed_four = jnp.concatenate(near_four + far_four, 0)
    d_gate_up = left_dot(normed_four, kept_two[:, : 2 * hidden]).astype(BF16)
    d_ffn_in, d_gate_up = seq_scatter(near_out, far_out, d_gate_up)
    d_hidden, d_gain_ffn_two = norm_back(d_ffn_in, gain_ffn_two, unit_four, scale_four)
    grad_three = grad_four + d_hidden

    grad_attn = grad_three.astype(BF16)
    far_attn = far_half(grad_attn)
    d_down = left_dot(jnp.concatenate(cotangent_blocks, 0), kept_two[:, 2 * hidden :])
    grads_two = jnp.concatenate([d_gate_up, d_down.astype(BF16)], 1)
    far_attn, grads_two = tie(far_attn, grads_two)
    owned_two = dp_scatter(grads_two)
    grad_blocks = near_blocks(grad_attn) + near_blocks(far_attn)
    d_raw, near_out, far_out, d_head_gains = attention_backward(
        place, grad_blocks, qkv_block, o_block, cosine, sine, starts, head_gains,
        raw, wide, totals,
    )
    d_head_gains = d_head_gains[:, :head] + d_head_gains[:, head:]
    d_qkv = left_dot(jnp.concatenate(blocks_three, 0), d_raw)
    d_w_o = left_dot(attended_low, jnp.concatenate(grad_blocks, 0))
    d_w_o = pack_rows(d_w_o.astype(BF16), dp_count)
    d_attn_in, *grads_attn = seq_scatter(near_out, far_out, d_qkv.astype(BF16), d_w_o)
    d_attn_h, d_gain_attn = norm_back(d_attn_in, gain_attn, unit_three, scale_three)
    grad_two = grad_three + d_attn_h

    near_grad = grad_two.astype(BF16)
    far_grad = far_half(near_grad)
    near_grad = near_blocks(near_grad)
    kept_one, near_out = ffn_backward(near_grad, terms_one, ffn_one, hidden, 0, None)
    far_grad, near_out = tie(far_grad, near_out)
    far_grad = near_blocks(far_grad)
    kept_one, far_out = ffn_backward(far_grad, terms_one, ffn_one, hidden, 1, kept_one)
    kept_one, far_out = tie(kept_one, far_out)
    d_gate_up = left_dot(jnp.concatenate(blocks_two, 0), kept_one).astype(BF16)
    d_down = left_dot(
        jnp.concatenate(near_grad + far_grad, 0), terms_one[:, 2 * hidden :]
    ).astype(BF16)
    owned_one = dp_scatter(jnp.concatenate([d_gate_up, *grads_attn], 1))
    d_ffn_in_one, d_down = seq_scatter(near_out, far_out, d_down)
    d_hidden_one, d_gain_ffn_one = norm_back(d_ffn_in_one, gain_ffn_one, unit_two, scale_two)
    grad_one = grad_two + d_hidden_one

    grad_mix = grad_one.astype(BF16)
    far_mix = far_half(grad_mix)
    far_mix, d_down = tie(far_mix, d_down)
    grad_mix = jnp.concatenate([near_half(grad_mix), near_half(far_mix)], 0)
    grad_mix, owned_two = tie(grad_mix, owned_two)
    projected = projected.reshape(seq_count, length, 3 * channels)
    part_b = projected[..., :channels]
    part_c = projected[..., channels : 2 * channels]
    part_x = projected[..., 2 * channels :]
    product = (part_b * part_x).astype(BF16)
    tails = flip_blocks(product[:, length - reach :])
    before = flip_blocks(jnp.concatenate([jnp.zeros_like(tails[:1]), tails[:-1]], 0))
    extended = jnp.concatenate([before, product], 1).astype(F32)
    conv_out = kernel[0] * extended[:, reach:]
    for tap in range(1, reach + 1):
        conv_out = (
            conv_out
            + kernel[tap] * extended[:, reach - tap : reach - tap + length] * masks[tap - 1]
        )
    d_w_out = left_dot(gated, grad_mix)
    d_gated = right_dot(grad_mix, out_block).reshape(seq_count, length, channels)
    d_part_c = d_gated * conv_out
    d_conv = d_gated * part_c
    sent = [d_conv * masks[tap - 1] for tap in range(1, reach + 1)]
    kernel_grads = [jnp.sum((d_conv * extended[:, reach:]).reshape(-1, channels), 0)]
    for tap in range(1, reach + 1):
        piece = extended[:, reach - tap : reach - tap + length]
        kernel_grads.append(jnp.sum((sent[tap - 1] * piece).reshape(-1, channels), 0))
    d_product_sum = kernel[0] * d_conv
    for tap in range(1, reach + 1):
        heads = flip_blocks(sent[tap - 1][:, :tap])
        after = flip_blocks(jnp.concatenate([heads[1:], jnp.zeros_like(heads[:1])], 0))
        moved = jnp.concatenate([sent[tap - 1][:, tap:], after], 1)
        d_product_sum = d_product_sum + kernel[tap] * moved
    d_product = lax.optimization_barrier(d_product_sum.astype(BF16)).astype(F32)
    d_projected = jnp.concatenate([d_product * part_x, d_part_c, d_product * part_b], -1)
    d_projected = d_projected.astype(BF16).reshape(full, 3 * channels)
    d_w_in = left_dot(normed_one, d_projected)
    d_normed = seq_scatter(*halves_of(right_dot(d_projected, in_block)))
    unit_one, scale_one = unit_scale(x_flat)
    d_x_part, d_gain_mix = norm_back(d_normed, gain_mix, unit_one, scale_one)
    d_x = (grad_one + d_x_part).reshape(rows, length, width)

    kernel_wide = lax.dynamic_update_slice_in_dim(
        jnp.zeros((taps, width), F32), jnp.stack(kernel_grads), seq_place * channels, 1
    )
    head_wide = jnp.pad(
        d_head_gains.reshape(2, dp_count, -1),
        ((0, 0), (0, 0), (0, slots - head // dp_count)),
    ).reshape(2, width)
    vectors = jnp.concatenate(
        [
            jnp.stack([d_gain_mix, d_gain_ffn_one, d_gain_attn, d_gain_ffn_two]),
            kernel_wide,
            head_wide,
        ],
        0,
    )
    vector_columns = jnp.pad(vectors.T, ((0, 0), (0, 128 - vectors.shape[0])))
    grads_mix = jnp.concatenate(
        [
            d_down,
            d_w_in.astype(BF16),
            vector_columns.astype(BF16),
            pack_rows(d_w_out.astype(BF16), dp_count),
        ],
        1,
    )
    grads_mix, owned_one = tie(grads_mix, owned_one)
    owned_mix = dp_scatter(grads_mix)

    def redeal(block):
        return pack_piece(undeal_rows(unpack_piece(block, width)), channels)

    owned_two, owned_one, kept_two = tie(owned_two, owned_one, kept_two)
    ffn_out = right_dot(kept_two[:, 2 * hidden :], ffn_two[:, 2 * hidden :])
    hidden_four = hidden_three + seq_scatter(*halves_of(ffn_out))
    out = hidden_four.astype(BF16).reshape(rows, length, width)
    d_wgate_two, d_wup_two, d_down_two = assemble(
        place, share(owned_two), [(n * hidden, hidden, 1, False) for n in range(3)]
    )
    tasks = [(n * hidden, hidden, 1, False) for n in range(2)]
    for columns in (channels, kv_width, kv_width):
        tasks.append((tasks[-1][0] + tasks[-1][1], columns, 1, False))
    d_wgate_one, d_wup_one, d_w_q, d_w_k, d_w_v = assemble(
        place, share(owned_one[:, :-channels]), tasks
    )
    (d_w_o_full,) = assemble(
        place, share(redeal(owned_one[:, -channels:])), [(0, channels, 1, True)]
    )
    owned_mix, out, d_x, d_wgate_two, d_wup_two, d_down_two, d_wgate_one, d_w_o_full = tie(
        owned_mix, out, d_x, d_wgate_two, d_wup_two, d_down_two, d_wgate_one, d_w_o_full
    )
    shared_mix = share(owned_mix[:, :-channels])
    shared_out = share(redeal(owned_mix[:, -channels:]))
    d_down_one, d_w_in_full = assemble(
        place, shared_mix, [(0, hidden, 1, False), (hidden, 3 * channels, 3, False)]
    )
    (d_w_out_full,) = assemble(place, shared_out, [(0, channels, 1, True)])
    vectors_all = [block[:, hidden + 3 * channels :] for block in shared_mix]
    sums = sum(block.astype(F32) for block in vectors_all).T
    small_head = head // dp_count
    return (
        out,
        d_x,
        d_w_in_full,
        sums[4 : 4 + taps],
        d_w_out_full,
        d_wgate_one,
        d_wup_one,
        d_down_one,
        sums[0],
        sums[1],
        d_w_q,
        d_w_k,
        d_w_v,
        d_w_o_full,
        sums[4 + taps, :small_head],
        sums[5 + taps, :small_head],
        d_wgate_two,
        d_wup_two,
        d_down_two,
        sums[2],
        sums[3],
    )


def solution(mesh):
    matrix = P("dp", None)
    vector = P("dp")
    tokens = P("dp", "seq", None)
    kernel = P(None, "dp")
    in_specs = (
        (tokens, matrix, P("dp", "seq"), tokens, matrix, kernel)
        + (matrix,) * 4
        + (vector,) * 2
        + (matrix,) * 4
        + (vector,) * 2
        + (matrix,) * 3
        + (vector,) * 2
    )
    out_specs = (
        (tokens, tokens, matrix, kernel)
        + (matrix,) * 4
        + (vector,) * 2
        + (matrix,) * 4
        + (vector,) * 2
        + (matrix,) * 3
        + (vector,) * 2
    )
    return jax.shard_map(local, mesh=mesh, in_specs=in_specs, out_specs=out_specs, check_vma=False)
```

```python
import jax
import jax.numpy as jnp
from jax import lax
from jax.experimental import pallas as pl
from jax.experimental.pallas import tpu as pltpu
from jax.sharding import PartitionSpec as P

EPS = 1e-05
THETA = 1000000.0
NEG = -1e30
F32 = jnp.float32
BF16 = jnp.bfloat16
TILE = 256
LANES = 128
VMEM_LIMIT = 48 << 20


def left_dot(left, right):
    return lax.dot_general(left, right, (((0,), (0,)), ((), ())), preferred_element_type=F32)


def right_dot(left, right):
    return lax.dot_general(left, right, (((1,), (1,)), ((), ())), preferred_element_type=F32)


def plain_dot(left, right):
    return jnp.dot(left, right, preferred_element_type=F32)


def unit_scale(value):
    scale = lax.rsqrt(jnp.mean(value * value, -1, keepdims=True) + EPS)
    return (value * scale, scale)


def norm_back(grad_out, gain, unit, scale):
    weighted = grad_out * gain
    grad_in = scale * (weighted - unit * jnp.mean(weighted * unit, -1, keepdims=True))
    gain_grad = jnp.sum((grad_out * unit).reshape(-1, unit.shape[-1]), 0)
    return (grad_in, gain_grad)


def doc_starts(bounds, places):
    return jnp.max(jnp.where(bounds <= places[..., None], bounds, 0), -1)


def rope_tables(places, head):
    half = head // 2
    freqs = THETA ** (-(2.0 * jnp.arange(half, dtype=F32)) / head)
    angles = places.astype(F32)[:, None] * freqs
    cosine = jnp.cos(angles)
    sine = jnp.sin(angles)
    return (
        jnp.concatenate([cosine] * 4, 1),
        jnp.concatenate([-sine, sine, -sine, sine], 1),
    )


def seq_bits():
    size = lax.axis_size("seq")
    bits = []
    bit = 1
    while bit < size:
        bits.append(bit)
        bit = bit * 2
    return bits


def swap_seq(array, bit):
    size = lax.axis_size("seq")
    return lax.ppermute(array, "seq", [(i, i ^ bit) for i in range(size)])


def tie(*values):
    return lax.optimization_barrier(values)


def near_blocks(block):
    have = {0: block}
    for bit in reversed(seq_bits()[:-1]):
        for place in sorted(have):
            have[place | bit] = swap_seq(have[place], bit)
    return [have[place] for place in sorted(have)]


def far_half(block):
    return swap_seq(block, seq_bits()[-1])


def near_sum(half):
    size = lax.axis_size("seq") // 2
    length = half.shape[0] // size
    have = {place: half[place * length : (place + 1) * length] for place in range(size)}
    for bit in seq_bits()[:-1]:
        for place in sorted(have, reverse=True):
            if place & bit:
                got = swap_seq(have.pop(place).astype(BF16), bit).astype(F32)
                have[place ^ bit] = have[place ^ bit].astype(F32) + got
    return have[0].astype(F32)


def seq_scatter(near, far, *work):
    sent = far_half(near_sum(far).astype(BF16))
    kept = near_sum(near)
    sent, kept, *work = tie(sent, kept, *work)
    total = kept + sent.astype(F32)
    return (total, *work) if work else total


def half_lanes(shape):
    return lax.broadcasted_iota(jnp.int32, shape, 1) < LANES // 2


def head_mean(value):
    row = lax.broadcasted_iota(jnp.int32, (LANES, LANES), 0) < LANES // 2
    column = half_lanes((LANES, LANES))
    ones = jnp.where(row == column, 2.0 / LANES, 0.0).astype(BF16)
    high = value.astype(BF16)
    low = (value - high.astype(F32)).astype(BF16)
    return plain_dot(high, ones) + plain_dot(low, ones)


def swap_quarters(value):
    quarter = LANES // 4
    lane = lax.broadcasted_iota(jnp.int32, value.shape, 1)
    first = (lane // quarter) % 2 == 0
    return jnp.where(
        first, pltpu.roll(value, LANES - quarter, 1), pltpu.roll(value, quarter, 1)
    )


def head_unit(value):
    scale = lax.rsqrt(head_mean(value * value) + EPS)
    return (value * scale, scale)


def pad_pair(value, second):
    lower = half_lanes(value.shape)
    if second:
        high = jnp.where(lower, 0.0, value)
        return (pltpu.roll(high, LANES // 2, 1), high)
    low = jnp.where(lower, value, 0.0)
    return (low, pltpu.roll(low, LANES // 2, 1))


def load_heads(raw_ref, cos_ref, sin_ref, gains_ref, rows, target, length, pairs):
    cosine = cos_ref[pl.ds(target, length), :]
    sine = sin_ref[pl.ds(target, length), :]
    groups = raw_ref.shape[1] // LANES

    def turned(group, gain):
        value = head_unit(raw_ref[rows, group * LANES : (group + 1) * LANES])[0] * gain
        return value * cosine + swap_quarters(value) * sine

    scale = (LANES // 2) ** (-0.5)
    queries = [(turned(g, gains_ref[0:1, :]) * scale).astype(BF16) for g in range(pairs)]
    keys = []
    values = []
    cached = {}
    for g in range(pairs):
        place = pairs * LANES + g * (LANES // 2)
        group, second = divmod(place, LANES)
        if group not in cached:
            cached[group] = turned(group, gains_ref[1:2, :]).astype(BF16).astype(F32)
        keys.append([k.astype(BF16) for k in pad_pair(cached[group], second > 0)])
        place = place + pairs * (LANES // 2)
        group, second = divmod(place, LANES)
        value = raw_ref[rows, group * LANES : (group + 1) * LANES]
        values.append([v.astype(BF16) for v in pad_pair(value, second > 0)])
    return (queries, keys, values)


def allowed_tile(start_ref, first_key, first_query):
    query = first_query + lax.broadcasted_iota(jnp.int32, (1, TILE), 1)
    start = start_ref[0:1, pl.ds(first_query, TILE)]
    key = first_key + lax.broadcasted_iota(jnp.int32, (TILE, TILE), 0)
    return (key >= start) & (key <= query)


def block_rows(block, count, length):
    half, offset = divmod(block, count // 2)
    return (half, slice(offset * length, (offset + 1) * length))


def attention_forward_kernel(place_ref, *refs, length, pairs, tokens):
    token_refs = refs[:tokens]
    (
        qkv_ref, o_ref, cos_ref, sin_ref, start_ref, gains_ref,
        raw_ref, out_ref, wide_ref, total_ref, near_out_ref, far_out_ref,
        query_ref, key_ref, value_ref,
    ) = refs[tokens:]
    full = raw_ref.shape[0]
    count = full // length
    place = place_ref[0]

    for block in range(count):
        target = pl.multiple_of((block ^ place) * length, 8)
        source = slice(block * length, (block + 1) * length)
        raw_ref[source, :] = plain_dot(token_refs[block][...], qkv_ref[...])
        queries, keys, values = load_heads(
            raw_ref, cos_ref, sin_ref, gains_ref, source, target, length, pairs
        )
        for g in range(pairs):
            query_ref[g, pl.ds(target, length), :] = queries[g]
            for h in range(2):
                key_ref[2 * g + h, pl.ds(target, length), :] = keys[g][h]
                value_ref[2 * g + h, pl.ds(target, length), :] = values[g][h]

    half = LANES // 2

    def query_tile(i, _):
        first_query = pl.multiple_of(i * TILE, TILE)

        def key_tile(j, carry):
            first_key = pl.multiple_of(j * TILE, TILE)
            allowed = allowed_tile(start_ref, first_key, first_query)
            sums, outs = carry
            new_sums = []
            new_outs = []
            for g in range(pairs):
                query = query_ref[g, pl.ds(first_query, TILE), :]
                total = outs[g]
                for h in range(2):
                    key = key_ref[2 * g + h, pl.ds(first_key, TILE), :]
                    value = value_ref[2 * g + h, pl.ds(first_key, TILE), :]
                    weight = jnp.where(allowed, jnp.exp(right_dot(key, query)), 0.0)
                    new_sums.append(sums[2 * g + h] + jnp.sum(weight, 0, keepdims=True))
                    total = total + lax.dot_general(
                        value, weight.astype(BF16), (((0,), (0,)), ((), ())),
                        preferred_element_type=F32,
                    )
                new_outs.append(total)
            return (new_sums, new_outs)

        carry = (
            [jnp.zeros((1, TILE), F32) for _ in range(2 * pairs)],
            [jnp.zeros((LANES, TILE), F32) for _ in range(pairs)],
        )
        sums, outs = lax.fori_loop(0, i + 1, key_tile, carry)
        columns = pl.ds(first_query, TILE)
        for g in range(pairs):
            scaled = jnp.concatenate(
                [outs[g][h * half : (h + 1) * half] / sums[2 * g + h] for h in range(2)], 0
            )
            for h in range(2):
                total_ref[2 * g + h : 2 * g + h + 1, columns] = sums[2 * g + h]
            wide_ref[g * LANES : (g + 1) * LANES, columns] = scaled
            query_ref[g, columns, :] = scaled.T.astype(BF16)
        return 0

    lax.fori_loop(0, full // TILE, query_tile, 0)

    for block in range(count):
        side, rows = block_rows(block, count, length)
        source = pl.multiple_of((block ^ place) * length, 8)
        target = slice(block * length, (block + 1) * length)
        for g in range(pairs):
            out_ref[target, g * LANES : (g + 1) * LANES] = query_ref[
                g, pl.ds(source, length), :
            ]
        partial = plain_dot(out_ref[target, :], o_ref[...])
        (near_out_ref, far_out_ref)[side][rows, :] = partial.astype(BF16)


def attention_backward_kernel(place_ref, *refs, length, pairs, tokens):
    token_refs = refs[:tokens]
    (
        qkv_ref, o_ref, cos_ref, sin_ref, start_ref, gains_ref, raw_ref, wide_ref, total_ref,
        out_ref, near_out_ref, far_out_ref, gain_grad_ref,
        query_ref, key_ref, value_ref, hold_ref, dq_ref, dk_ref, dv_ref,
    ) = refs[tokens:]
    full = raw_ref.shape[0]
    count = full // length
    place = place_ref[0]
    half = LANES // 2

    for block in range(count):
        target = pl.multiple_of((block ^ place) * length, 8)
        source = slice(block * length, (block + 1) * length)
        grads = right_dot(token_refs[block][...], o_ref[...]).astype(BF16)
        queries, keys, values = load_heads(
            raw_ref, cos_ref, sin_ref, gains_ref, source, target, length, pairs
        )
        rows = pl.ds(target, length)
        for g in range(pairs):
            query_ref[g, rows, :] = queries[g]
            hold_ref[g, rows, :] = grads[:, g * LANES : (g + 1) * LANES]
            dk_ref[g, rows, :] = jnp.zeros((length, LANES), F32)
            dv_ref[g, rows, :] = jnp.zeros((length, LANES), F32)
            for h in range(2):
                key_ref[2 * g + h, rows, :] = keys[g][h]
                value_ref[2 * g + h, rows, :] = values[g][h]

    lower = half_lanes((TILE, LANES))

    def query_tile(i, _):
        first_query = pl.multiple_of(i * TILE, TILE)
        columns = pl.ds(first_query, TILE)
        inverse = [1.0 / total_ref[n : n + 1, columns] for n in range(2 * pairs)]
        inner = []
        for g in range(pairs):
            grad = hold_ref[g, columns, :].astype(F32).T
            both = grad * wide_ref[g * LANES : (g + 1) * LANES, columns]
            for h in range(2):
                inner.append(jnp.sum(both[h * half : (h + 1) * half], 0, keepdims=True))

        def key_tile(j, outs):
            first_key = pl.multiple_of(j * TILE, TILE)
            rows = pl.ds(first_key, TILE)
            allowed = allowed_tile(start_ref, first_key, first_query)
            new_outs = []
            for g in range(pairs):
                query = query_ref[g, columns, :]
                grad = hold_ref[g, columns, :]
                zero = jnp.zeros_like(query)
                total = outs[g]
                d_key = dk_ref[g, rows, :]
                d_value = dv_ref[g, rows, :]
                for h in range(2):
                    keep = lower if h == 0 else jnp.logical_not(lower)
                    key = key_ref[2 * g + h, rows, :]
                    value = value_ref[2 * g + h, rows, :]
                    weight = jnp.exp(right_dot(key, query)) * inverse[2 * g + h]
                    weight = jnp.where(allowed, weight, 0.0)
                    d_weight = right_dot(value, grad)
                    d_score = (weight * (d_weight - inner[2 * g + h])).astype(BF16)
                    d_value = d_value + plain_dot(
                        weight.astype(BF16), jnp.where(keep, grad, zero)
                    )
                    d_key = d_key + plain_dot(d_score, jnp.where(keep, query, zero))
                    total = total + lax.dot_general(
                        key, d_score, (((0,), (0,)), ((), ())), preferred_element_type=F32
                    )
                dk_ref[g, rows, :] = d_key
                dv_ref[g, rows, :] = d_value
                new_outs.append(total)
            return new_outs

        outs = lax.fori_loop(
            0, i + 1, key_tile, [jnp.zeros((LANES, TILE), F32) for _ in range(pairs)]
        )
        for g in range(pairs):
            dq_ref[g, columns, :] = outs[g].T
        return 0

    lax.fori_loop(0, full // TILE, query_tile, 0)
    scale = half ** (-0.5)

    low = half_lanes((length, LANES))
    query_gain = jnp.zeros((1, LANES), F32)
    key_gain = jnp.zeros((1, LANES), F32)
    for block in range(count):
        side, side_rows = block_rows(block, count, length)
        rows = pl.ds(pl.multiple_of((block ^ place) * length, 8), length)
        target = slice(block * length, (block + 1) * length)
        cosine = cos_ref[rows, :]
        sine = sin_ref[rows, :]

        def back(grad, group, gain):
            grad = grad.astype(BF16).astype(F32)
            unit, inverse = head_unit(raw_ref[target, group * LANES : (group + 1) * LANES])
            d_rot = grad * cosine + swap_quarters(grad * sine)
            weighted = d_rot * gain
            d_raw = inverse * (weighted - unit * head_mean(weighted * unit))
            return (d_raw, d_rot * unit)

        for g in range(pairs):
            d_raw, terms = back(dq_ref[g, rows, :] * scale, g, gains_ref[0:1, :])
            query_gain = query_gain + jnp.sum(terms, 0, keepdims=True)
            out_ref[target, g * LANES : (g + 1) * LANES] = d_raw.astype(BF16)
        groups = {}
        for kind, held in ((0, dk_ref), (1, dv_ref)):
            for g in range(pairs):
                place_of = pairs * LANES + kind * pairs * half + g * half
                group, second = divmod(place_of, LANES)
                value = held[g, rows, :]
                value = value + pltpu.roll(value, half, 1)
                groups.setdefault(group, {})[second // half] = (kind, value)
        for group, parts in groups.items():
            merged = jnp.where(low, parts[0][1], parts[1][1])
            is_key = [parts[n][0] == 0 for n in range(2)]
            result = merged
            if any(is_key):
                d_raw, terms = back(merged, group, gains_ref[1:2, :])
                if not is_key[1]:
                    d_raw = jnp.where(low, d_raw, merged)
                    terms = jnp.where(low, terms, 0.0)
                result = d_raw
                key_gain = key_gain + jnp.sum(terms, 0, keepdims=True)
            out_ref[target, group * LANES : (group + 1) * LANES] = result.astype(BF16)
        partial = right_dot(out_ref[target, :], qkv_ref[...])
        (near_out_ref, far_out_ref)[side][side_rows, :] = partial.astype(BF16)
    gain_grad_ref[0:1, :] = query_gain
    gain_grad_ref[1:2, :] = key_gain


def whole(count):
    return [pl.BlockSpec(memory_space=pltpu.VMEM)] * count


def attention_forward(place, tokens, qkv, o, cosine, sine, start, gains):
    length = tokens[0].shape[0]
    full = len(tokens) * length
    width, columns = qkv.shape
    pairs = columns // (2 * LANES)
    return pl.pallas_call(
        lambda *refs: attention_forward_kernel(
            *refs, length=length, pairs=pairs, tokens=len(tokens)
        ),
        in_specs=[pl.BlockSpec(memory_space=pltpu.SMEM)] + whole(6 + len(tokens)),
        out_specs=tuple(whole(6)),
        out_shape=(
            jax.ShapeDtypeStruct((full, columns), F32),
            jax.ShapeDtypeStruct((full, pairs * LANES), BF16),
            jax.ShapeDtypeStruct((pairs * LANES, full), F32),
            jax.ShapeDtypeStruct((8, full), F32),
            jax.ShapeDtypeStruct((full // 2, width), BF16),
            jax.ShapeDtypeStruct((full // 2, width), BF16),
        ),
        scratch_shapes=[
            pltpu.VMEM((pairs, full, LANES), BF16),
            pltpu.VMEM((2 * pairs, full, LANES), BF16),
            pltpu.VMEM((2 * pairs, full, LANES), BF16),
        ],
        cost_estimate=pl.CostEstimate(
            flops=20_000_000_000, transcendentals=6_000_000, bytes_accessed=20_000_000
        ),
        compiler_params=pltpu.CompilerParams(vmem_limit_bytes=VMEM_LIMIT),
        name="attention_forward",
    )(place, *tokens, qkv, o, cosine, sine, start, gains)


def attention_backward(place, tokens, qkv, o, cosine, sine, start, gains, raw, wide, totals):
    length = tokens[0].shape[0]
    full = len(tokens) * length
    width, columns = qkv.shape
    pairs = columns // (2 * LANES)
    return pl.pallas_call(
        lambda *refs: attention_backward_kernel(
            *refs, length=length, pairs=pairs, tokens=len(tokens)
        ),
        in_specs=[pl.BlockSpec(memory_space=pltpu.SMEM)] + whole(9 + len(tokens)),
        out_specs=tuple(whole(4)),
        out_shape=(
            jax.ShapeDtypeStruct((full, columns), BF16),
            jax.ShapeDtypeStruct((full // 2, width), BF16),
            jax.ShapeDtypeStruct((full // 2, width), BF16),
            jax.ShapeDtypeStruct((2, LANES), F32),
        ),
        scratch_shapes=[
            pltpu.VMEM((pairs, full, LANES), BF16),
            pltpu.VMEM((2 * pairs, full, LANES), BF16),
            pltpu.VMEM((2 * pairs, full, LANES), BF16),
            pltpu.VMEM((pairs, full, LANES), BF16),
            pltpu.VMEM((pairs, full, LANES), F32),
            pltpu.VMEM((pairs, full, LANES), F32),
            pltpu.VMEM((pairs, full, LANES), F32),
        ],
        cost_estimate=pl.CostEstimate(
            flops=20_000_000_000, transcendentals=6_000_000, bytes_accessed=20_000_000
        ),
        compiler_params=pltpu.CompilerParams(vmem_limit_bytes=VMEM_LIMIT),
        name="attention_backward",
    )(place, *tokens, qkv, o, cosine, sine, start, gains, raw, wide, totals)


def column_block(weight, parts):
    size = lax.axis_size("seq")
    place = lax.axis_index("seq")
    rows, columns = weight.shape
    block = columns // parts // size
    split = weight.reshape(rows, parts, size * block)
    return lax.dynamic_slice_in_dim(split, place * block, block, 2).reshape(rows, parts * block)


def deal_pairs():
    size = lax.axis_size("seq")
    count = lax.axis_size("dp")
    pairs = []
    for place in range(size):
        for owner in range(count):
            source = (owner % size) * count + place * (count // size) + owner // size
            pairs.append((source, place * count + owner))
    return pairs


def deal_rows(*weights):
    size = lax.axis_size("seq")
    place = lax.axis_index("seq")
    piece = weights[0].shape[0] // size
    parts = [lax.dynamic_slice_in_dim(w, place * piece, piece, 0) for w in weights]
    dealt = lax.ppermute(jnp.concatenate(parts, 0), ("seq", "dp"), deal_pairs())
    return [dealt[n * piece : (n + 1) * piece] for n in range(len(weights))]


def pack_piece(piece, columns):
    count = piece.shape[1] // columns
    return jnp.concatenate(
        [piece[:, n * columns : (n + 1) * columns] for n in range(count)], 0
    )


def unpack_piece(block, width):
    count = width // block.shape[1]
    rows = block.shape[0] // count
    return jnp.concatenate([block[n * rows : (n + 1) * rows] for n in range(count)], 1)


def pack_rows(rows_block, parts):
    rows, width = rows_block.shape
    piece = rows // parts
    split = rows_block.reshape(parts, piece, width // rows, rows)
    return jnp.swapaxes(split, 1, 2).reshape(width, rows)


def unpack_rows(block, parts):
    width, rows = block.shape
    split = block.reshape(parts, width // rows, rows // parts, rows)
    return jnp.swapaxes(split, 1, 2).reshape(rows, width)


def undeal_rows(part):
    return lax.ppermute(part, ("seq", "dp"), [(b, a) for a, b in deal_pairs()])


def dp_gather(block):
    return lax.all_gather(block, "dp", axis=0, tiled=True)


def dp_scatter(grads):
    return lax.psum_scatter(grads, "dp", scatter_dimension=0, tiled=True)


def swap_dp(array, bit):
    size = lax.axis_size("dp")
    return lax.ppermute(array, "dp", [(i, i ^ bit) for i in range(size)])


def dp_bits():
    return [1, 2, 4] if lax.axis_size("dp") == 8 else []


def dp_gather_small(block, later):
    if not dp_bits():
        return (dp_gather(block), later)
    size = lax.axis_size("dp")
    place = lax.axis_index("dp")
    rows = block.shape[0]
    near, middle, far = dp_bits()
    have = {0: block, far: swap_dp(block, far), middle: swap_dp(block, middle)}
    have[near] = swap_dp(block, near)
    have[far], later = tie(have[far], later)
    have[far | middle] = swap_dp(have[far], middle)
    for turn in (middle, far, far | middle):
        have[turn | near] = swap_dp(have[turn], near)
    result = jnp.zeros((size * rows, block.shape[1]), block.dtype)
    for turn in range(size):
        result = lax.dynamic_update_slice_in_dim(result, have[turn], (place ^ turn) * rows, 0)
    return (result, later)


def dp_scatter_small(grads):
    if not dp_bits():
        return dp_scatter(grads)
    size = lax.axis_size("dp")
    place = lax.axis_index("dp")
    sums = grads.reshape(size, -1, grads.shape[1]).astype(F32)
    for bit in dp_bits():
        split = sums.reshape(-1, 2, *sums.shape[1:])
        side = (place // bit) % 2
        kept = lax.dynamic_index_in_dim(split, side, 1, False)
        sent = lax.dynamic_index_in_dim(split, 1 - side, 1, False).astype(BF16)
        sums = kept + swap_dp(sent, bit).astype(F32)
    return sums[0].astype(BF16)


def dp_scatter_pairs(grads, work, later):
    if not dp_bits():
        grads, later, *work = tie(grads, later, *work)
        return (dp_scatter(grads), work, later)
    size = lax.axis_size("dp")
    side = lax.axis_index("dp") % 2
    columns = grads.shape[1]
    blocks = grads.reshape(size // 2, 2, -1, columns)
    kept = lax.dynamic_index_in_dim(blocks, side, 1, False).reshape(-1, columns)
    sent = lax.dynamic_index_in_dim(blocks, 1 - side, 1, False).reshape(-1, columns)
    got, *work = tie(swap_dp(sent, 1), *work)
    sums = (kept.astype(F32) + got.astype(F32)).astype(BF16)
    sums, later = tie(sums, later)
    groups = [list(range(n, size, 2)) for n in range(2)]
    owned = lax.psum_scatter(
        sums, "dp", scatter_dimension=0, tiled=True, axis_index_groups=groups
    )
    return (owned, work, later)


def share(owned):
    return near_blocks(owned) + near_blocks(far_half(owned))


def assemble_kernel(place_ref, *refs, count, tasks):
    blocks = refs[:count]
    outs = refs[count:]
    place = place_ref[0]
    for turn in range(count):
        for target in range(count):

            @pl.when((place ^ turn) == target)
            def _():
                for (start, columns, split, by_rows), out_ref in zip(tasks, outs):
                    if by_rows:
                        rows = blocks[turn].shape[0] // count
                        for part in range(count):
                            out_ref[
                                target * rows : (target + 1) * rows,
                                part * columns : (part + 1) * columns,
                            ] = blocks[turn][
                                part * rows : (part + 1) * rows, start : start + columns
                            ].astype(F32)
                    else:
                        step = columns // split
                        for part in range(split):
                            first = (part * count + target) * step
                            out_ref[:, first : first + step] = blocks[turn][
                                :, start + part * step : start + (part + 1) * step
                            ].astype(F32)


def assemble(place, blocks, tasks):
    count = len(blocks)
    rows = blocks[0].shape[0]
    if all(columns // split % LANES == 0 for _, columns, split, _ in tasks):
        return pl.pallas_call(
            lambda *refs: assemble_kernel(*refs, count=count, tasks=tasks),
            in_specs=[pl.BlockSpec(memory_space=pltpu.SMEM)] + whole(count),
            out_specs=tuple(whole(len(tasks))),
            out_shape=tuple(
                jax.ShapeDtypeStruct((rows, count * columns), F32) for _, columns, _, _ in tasks
            ),
            compiler_params=pltpu.CompilerParams(vmem_limit_bytes=VMEM_LIMIT),
            name="assemble",
        )(place, *blocks)
    stacked = jnp.stack(blocks, 0)
    ordered = [
        lax.dynamic_index_in_dim(stacked, place[0] ^ i, 0, False) for i in range(count)
    ]
    results = []
    for start, columns, split, by_rows in tasks:
        parts = [block[:, start : start + columns] for block in ordered]
        if by_rows:
            joined = jnp.concatenate([unpack_piece(p, count * columns) for p in parts], 0)
        else:
            step = columns // split
            joined = jnp.concatenate(
                [p[:, n * step : (n + 1) * step] for n in range(split) for p in parts], 1
            )
        results.append(joined.astype(F32))
    return results


def gate_terms(normed, w_gate, w_up):
    gate = plain_dot(normed, w_gate)
    upper = plain_dot(normed, w_up)
    sigma = jax.nn.sigmoid(gate)
    swish = gate * sigma
    return (upper * (sigma + swish * (1.0 - sigma)), swish, swish * upper)


def block_here(refs):
    value = refs[0][...]
    for number, ref in enumerate(refs[1:]):
        value = jnp.where(pl.program_id(0) == number + 1, ref[...], value)
    return value


def ffn_forward_kernel(*refs, count):
    normed_refs = refs[:count]
    gate_ref, up_ref, down_ref = refs[count : count + 3]
    kept_ref, partial_ref = refs[-2:]
    hidden = gate_ref.shape[1]
    slope, swish, act = gate_terms(block_here(normed_refs), gate_ref[...], up_ref[...])
    act = act.astype(BF16)
    kept_ref[:, :hidden] = slope.astype(BF16)
    kept_ref[:, hidden : 2 * hidden] = swish.astype(BF16)
    kept_ref[:, 2 * hidden :] = act
    partial_ref[...] = right_dot(act, down_ref[...]).astype(BF16)


def ffn_turn_kernel(*refs, count):
    normed_refs = refs[:count]
    grad_refs = refs[count : 2 * count]
    gate_ref, up_ref, down_ref = refs[2 * count : 2 * count + 3]
    kept_ref, partial_ref = refs[-2:]
    hidden = gate_ref.shape[1]
    slope, swish, act = gate_terms(block_here(normed_refs), gate_ref[...], up_ref[...])
    d_act = plain_dot(block_here(grad_refs), down_ref[...])
    d_gate = (d_act * slope).astype(BF16)
    d_up = (d_act * swish).astype(BF16)
    kept_ref[:, :hidden] = d_gate
    kept_ref[:, hidden : 2 * hidden] = d_up
    kept_ref[:, 2 * hidden :] = act.astype(BF16)
    partial = right_dot(d_gate, gate_ref[...]) + right_dot(d_up, up_ref[...])
    partial_ref[...] = partial.astype(BF16)


def ffn_backward_kernel(*refs, count):
    grad_refs = refs[:count]
    terms_ref, gate_ref, up_ref, down_ref = refs[count : count + 4]
    kept_ref, partial_ref = refs[-2:]
    hidden = gate_ref.shape[1]
    d_act = plain_dot(block_here(grad_refs), down_ref[...])
    d_gate = (d_act * terms_ref[:, :hidden].astype(F32)).astype(BF16)
    d_up = (d_act * terms_ref[:, hidden:].astype(F32)).astype(BF16)
    kept_ref[:, :hidden] = d_gate
    kept_ref[:, hidden:] = d_up
    partial = right_dot(d_gate, gate_ref[...]) + right_dot(d_up, up_ref[...])
    partial_ref[...] = partial.astype(BF16)


def ffn_call(kernel, name, tokens, terms, weights, hidden, first, full, kept_width, kept):
    width = weights.shape[0]
    count = len(tokens[0])
    length = tokens[0][0].shape[0]
    operands = [block for blocks in tokens for block in blocks]
    in_specs = [
        pl.BlockSpec((length, width), lambda i: (0, 0), pipeline_mode=pl.Buffered(1))
        for _ in operands
    ]
    if terms is not None:
        in_specs.append(pl.BlockSpec((length, 2 * hidden), lambda i: (i + first, 0)))
        operands.append(terms)
    for place in range(3):
        in_specs.append(
            pl.BlockSpec(
                (width, hidden), lambda i, place=place: (0, place), pipeline_mode=pl.Buffered(1)
            )
        )
        operands.append(weights)
    aliases = {}
    if kept is not None:
        aliases = {len(operands): 0}
        in_specs.append(pl.BlockSpec(memory_space=pl.ANY))
        operands.append(kept)
    return pl.pallas_call(
        lambda *refs: kernel(*refs, count=count),
        grid=(count,),
        in_specs=in_specs,
        out_specs=(
            pl.BlockSpec((length, kept_width), lambda i: (i + first, 0)),
            pl.BlockSpec((length, width), lambda i: (i, 0)),
        ),
        out_shape=(
            jax.ShapeDtypeStruct((full, kept_width), BF16),
            jax.ShapeDtypeStruct((count * length, width), BF16),
        ),
        input_output_aliases=aliases,
        cost_estimate=pl.CostEstimate(
            flops=6_000_000_000, transcendentals=1_000_000, bytes_accessed=20_000_000
        ),
        compiler_params=pltpu.CompilerParams(vmem_limit_bytes=VMEM_LIMIT),
        name=name,
    )(*operands)


def split_weights(weights, hidden):
    return [weights[:, n * hidden : (n + 1) * hidden] for n in range(3)]


def halves_of(array):
    half = array.shape[0] // 2
    return (array[:half], array[half:])


def place_rows(kept, part, number):
    if kept is None:
        kept = jnp.zeros((2 * part.shape[0], part.shape[1]), part.dtype)
    return lax.dynamic_update_slice_in_dim(kept, part, number * part.shape[0], 0)


def ffn_forward(normed, weights, hidden):
    if hidden % LANES:
        w_gate, w_up, w_down = split_weights(weights, hidden)
        terms = gate_terms(jnp.concatenate(normed, 0), w_gate, w_up)
        terms = jnp.concatenate(terms, 1).astype(BF16)
        return (terms, right_dot(terms[:, 2 * hidden :], w_down).astype(BF16))
    return ffn_call(
        ffn_forward_kernel, "ffn_forward", [normed], None, weights, hidden,
        0, len(normed) * normed[0].shape[0], 3 * hidden, None,
    )


def ffn_turn(normed, grads, weights, hidden, number, kept):
    if hidden % LANES:
        w_gate, w_up, w_down = split_weights(weights, hidden)
        slope, swish, act = gate_terms(jnp.concatenate(normed, 0), w_gate, w_up)
        d_act = plain_dot(jnp.concatenate(grads, 0), w_down)
        part = jnp.concatenate([d_act * slope, d_act * swish, act], 1).astype(BF16)
        partial = right_dot(part[:, : 2 * hidden], weights[:, : 2 * hidden]).astype(BF16)
        return (place_rows(kept, part, number), partial)
    count = len(normed)
    return ffn_call(
        ffn_turn_kernel, "ffn_turn", [normed, grads], None, weights, hidden,
        number * count, 2 * count * normed[0].shape[0], 3 * hidden, kept,
    )


def ffn_backward(grads, terms, weights, hidden, number, kept):
    count = len(grads)
    length = grads[0].shape[0]
    if hidden % LANES:
        w_gate, w_up, w_down = split_weights(weights, hidden)
        rows = slice(number * count * length, (number + 1) * count * length)
        d_act = plain_dot(jnp.concatenate(grads, 0), w_down)
        slope = terms[rows, :hidden].astype(F32)
        swish = terms[rows, hidden : 2 * hidden].astype(F32)
        part = jnp.concatenate([d_act * slope, d_act * swish], 1).astype(BF16)
        partial = right_dot(part, weights[:, : 2 * hidden]).astype(BF16)
        return (place_rows(kept, part, number), partial)
    return ffn_call(
        ffn_backward_kernel, "ffn_backward", [grads], terms, weights, hidden,
        number * count, 2 * count * length, 2 * hidden, kept,
    )


def row_starts(bounds_ref, token):
    start = jnp.zeros(token.shape, jnp.int32)
    for number in range(1, bounds_ref.shape[0]):
        bound = bounds_ref[number]
        start = jnp.where(bound <= token, jnp.maximum(start, bound), start)
    return start


def conv_backward_kernel(*refs, length, tokens, taps):
    place_ref, bounds_ref = refs[:2]
    grad_refs = refs[2 : 2 + tokens]
    (
        projected_ref, in_ref, out_w_ref, tap_ref,
        d_projected_ref, near_out_ref, far_out_ref, tap_grad_ref,
        product_ref, d_gated_ref, d_conv_ref,
    ) = refs[2 + tokens :]
    place = place_ref[0]
    channels = out_w_ref.shape[0]
    full = tokens * length
    product_ref[0:8, :] = jnp.zeros((8, channels), F32)
    d_conv_ref[full : full + 8, :] = jnp.zeros((8, channels), F32)
    for block in range(tokens):
        rows = slice(block * length, (block + 1) * length)
        first = pl.multiple_of((block ^ place) * length, 8)
        d_gated_ref[rows, :] = right_dot(grad_refs[block][...], out_w_ref[...])
        product = projected_ref[rows, :channels] * projected_ref[rows, 2 * channels :]
        product_ref[pl.ds(pl.multiple_of(8 + first, 8), length), :] = product.astype(BF16).astype(F32)
    tap_grads = [jnp.zeros((1, channels), F32) for _ in range(taps)]
    for block in range(tokens):
        rows = slice(block * length, (block + 1) * length)
        first = pl.multiple_of((block ^ place) * length, 8)
        window = product_ref[pl.ds(first, length + 8), :]
        token = first + lax.broadcasted_iota(jnp.int32, (length, channels), 0)
        start = row_starts(bounds_ref, token)
        d_gated = d_gated_ref[rows, :]
        d_conv = d_gated * projected_ref[rows, channels : 2 * channels]
        conv = jnp.zeros((length, channels), F32)
        for tap in range(taps):
            moved = window[8 - tap : 8 - tap + length, :]
            moved = jnp.where(token - tap >= start, moved, 0.0)
            conv = conv + tap_ref[tap : tap + 1, :] * moved
            tap_grads[tap] = tap_grads[tap] + jnp.sum(d_conv * moved, 0, keepdims=True)
        d_projected_ref[rows, channels : 2 * channels] = (d_gated * conv).astype(BF16)
        d_conv_ref[pl.ds(first, length), :] = d_conv
    for tap in range(taps):
        tap_grad_ref[tap : tap + 1, :] = tap_grads[tap]
    for block in range(tokens):
        side, side_rows = block_rows(block, tokens, length)
        rows = slice(block * length, (block + 1) * length)
        first = pl.multiple_of((block ^ place) * length, 8)
        window = d_conv_ref[pl.ds(first, length + 8), :]
        token = first + lax.broadcasted_iota(jnp.int32, (length, channels), 0)
        total = tap_ref[0:1, :] * window[:length, :]
        for tap in range(1, taps):
            same = token >= row_starts(bounds_ref, token + tap)
            total = total + tap_ref[tap : tap + 1, :] * jnp.where(
                same, window[tap : tap + length, :], 0.0
            )
        d_product = total.astype(BF16).astype(F32)
        d_projected_ref[rows, :channels] = (
            d_product * projected_ref[rows, 2 * channels :]
        ).astype(BF16)
        d_projected_ref[rows, 2 * channels :] = (
            d_product * projected_ref[rows, :channels]
        ).astype(BF16)
        partial = right_dot(d_projected_ref[rows, :], in_ref[:, : 3 * channels])
        (near_out_ref, far_out_ref)[side][side_rows, :] = partial.astype(BF16)


def conv_backward(place, bounds, grads, projected, in_weights, out_weights, kernel):
    length, width = grads[0].shape
    full = len(grads) * length
    channels = out_weights.shape[0]
    taps = kernel.shape[0]
    scalar = pl.BlockSpec(memory_space=pltpu.SMEM)
    return pl.pallas_call(
        lambda *refs: conv_backward_kernel(*refs, length=length, tokens=len(grads), taps=taps),
        in_specs=[scalar, scalar] + whole(len(grads) + 4),
        out_specs=tuple(whole(4)),
        out_shape=(
            jax.ShapeDtypeStruct((full, 3 * channels), BF16),
            jax.ShapeDtypeStruct((full // 2, width), BF16),
            jax.ShapeDtypeStruct((full // 2, width), BF16),
            jax.ShapeDtypeStruct((taps, channels), F32),
        ),
        scratch_shapes=[
            pltpu.VMEM((full + 8, channels), F32),
            pltpu.VMEM((full, channels), F32),
            pltpu.VMEM((full + 8, channels), F32),
        ],
        cost_estimate=pl.CostEstimate(flops=0, transcendentals=0, bytes_accessed=100_000),
        compiler_params=pltpu.CompilerParams(vmem_limit_bytes=VMEM_LIMIT),
        name="conv_backward",
    )(place, bounds, *grads, projected, in_weights, out_weights, kernel)


def conv_forward_kernel(*refs, length, tokens, taps):
    place_ref, bounds_ref = refs[:2]
    token_refs = refs[2 : 2 + tokens]
    (
        in_ref, out_w_ref, tap_ref, gain_ref,
        normed_ref, projected_ref, gated_ref, near_out_ref, far_out_ref, product_ref,
    ) = refs[2 + tokens :]
    place = place_ref[0]
    channels = gated_ref.shape[1]
    product_ref[0:8, :] = jnp.zeros((8, channels), F32)
    for block in range(tokens):
        rows = slice(block * length, (block + 1) * length)
        value = token_refs[block][...].astype(F32)
        scale = lax.rsqrt(jnp.mean(value * value, -1, keepdims=True) + EPS)
        normed = (value * scale * gain_ref[...]).astype(BF16)
        normed_ref[rows, :] = normed
        projected = plain_dot(normed, in_ref[:, : 3 * channels])
        projected_ref[rows, :] = projected
        product = (projected[:, :channels] * projected[:, 2 * channels :]).astype(BF16)
        target = pl.multiple_of(8 + (block ^ place) * length, 8)
        product_ref[pl.ds(target, length), :] = product.astype(F32)
    for block in range(tokens):
        side, side_rows = block_rows(block, tokens, length)
        rows = slice(block * length, (block + 1) * length)
        first = pl.multiple_of((block ^ place) * length, 8)
        window = product_ref[pl.ds(first, length + 8), :]
        token = first + lax.broadcasted_iota(jnp.int32, (length, channels), 0)
        start = row_starts(bounds_ref, token)
        conv = tap_ref[0:1, :] * window[8:, :]
        for tap in range(1, taps):
            moved = window[8 - tap : 8 - tap + length, :]
            moved = jnp.where(token - tap >= start, moved, 0.0)
            conv = conv + tap_ref[tap : tap + 1, :] * moved
        gated = (projected_ref[rows, channels : 2 * channels] * conv).astype(BF16)
        gated_ref[rows, :] = gated
        partial = plain_dot(gated, out_w_ref[...]).astype(BF16)
        (near_out_ref, far_out_ref)[side][side_rows, :] = partial


def conv_forward(place, bounds, tokens, in_weights, out_weights, kernel, gain):
    length, width = tokens[0].shape
    full = len(tokens) * length
    channels = out_weights.shape[0]
    taps = kernel.shape[0]
    scalar = pl.BlockSpec(memory_space=pltpu.SMEM)
    return pl.pallas_call(
        lambda *refs: conv_forward_kernel(*refs, length=length, tokens=len(tokens), taps=taps),
        in_specs=[scalar, scalar] + whole(len(tokens) + 4),
        out_specs=tuple(whole(5)),
        out_shape=(
            jax.ShapeDtypeStruct((full, width), BF16),
            jax.ShapeDtypeStruct((full, 3 * channels), F32),
            jax.ShapeDtypeStruct((full, channels), BF16),
            jax.ShapeDtypeStruct((full // 2, width), BF16),
            jax.ShapeDtypeStruct((full // 2, width), BF16),
        ),
        scratch_shapes=[pltpu.VMEM((full + 8, channels), F32)],
        cost_estimate=pl.CostEstimate(
            flops=4_000_000_000, transcendentals=2_000, bytes_accessed=20_000_000
        ),
        compiler_params=pltpu.CompilerParams(vmem_limit_bytes=VMEM_LIMIT),
        name="conv_forward",
    )(place, bounds, *tokens, in_weights, out_weights, kernel, gain)


def local(
    x_in,
    cu_seqlens,
    positions,
    cotangent,
    w_in,
    conv_w,
    w_out,
    w_gate1,
    w_up1,
    w_down1,
    g_mix1,
    g_ffn1,
    w_q,
    key_projection_weight,
    value_projection_weight,
    w_o,
    g_q,
    g_k,
    w_gate2,
    w_up2,
    w_down2,
    g_attn2,
    g_ffn2,
):
    rows, length, width = x_in.shape
    assert rows == 1
    seq_count = lax.axis_size("seq")
    dp_count = lax.axis_size("dp")
    seq_place = lax.axis_index("seq")
    full = length * seq_count
    channels = width // seq_count
    slots = width // dp_count
    head = g_q.shape[0] * dp_count
    taps = conv_w.shape[0]

    dealt_out, dealt_o = deal_rows(w_out, w_o)
    x_low, dealt_out, dealt_o = tie(x_in.reshape(length, width), dealt_out, dealt_o)
    x_far = far_half(x_low)
    cotangent_low, x_far = tie(cotangent.reshape(length, width), x_far)
    x_blocks = near_blocks(x_low) + near_blocks(x_far)
    cotangent_blocks = near_blocks(cotangent_low) + near_blocks(far_half(cotangent_low))
    head_gains = jnp.pad(jnp.stack([g_q, g_k], 1), ((0, slots - head // dp_count), (0, 0)))
    small = jnp.concatenate(
        [conv_w.T, jnp.stack([g_mix1, g_ffn1, g_attn2, g_ffn2], 1), head_gains], 1
    )
    small = jnp.pad(small, ((0, 0), (0, 128 - small.shape[1])))
    out_piece = pack_piece(dealt_out, channels)
    o_piece = pack_piece(dealt_o, channels)
    mix_block = jnp.concatenate([column_block(w_in, 3), small, out_piece], 1)
    mix_block, w_gate1, w_up1, w_down1, w_q, key_projection_weight, value_projection_weight = tie(
        mix_block, w_gate1, w_up1, w_down1, w_q, key_projection_weight, value_projection_weight
    )
    hidden = w_gate1.shape[1] // seq_count
    ffn_one = jnp.concatenate(
        [
            column_block(w, 1)
            for w in (
                w_gate1, w_up1, w_down1, w_q, key_projection_weight, value_projection_weight
            )
        ]
        + [o_piece],
        1,
    )
    mix_all, ffn_one = dp_gather_small(mix_block, ffn_one)
    ffn_one = dp_gather(ffn_one)
    attn_all = ffn_one[:, 3 * hidden :]
    ffn_two = dp_gather(
        jnp.concatenate([column_block(w, 1) for w in (w_gate2, w_up2, w_down2)], 1)
    )
    qkv_width = attn_all.shape[1] - channels
    qkv_block = attn_all[:, :qkv_width]
    o_block = unpack_rows(attn_all[:, qkv_width:], dp_count)
    bounds = cu_seqlens[0]
    place = seq_place.reshape(1).astype(jnp.int32)
    out_block = unpack_rows(mix_all[:, 3 * channels + 128 :], dp_count)
    small_all = mix_all[:, 3 * channels : 3 * channels + 128].astype(F32).T
    kernel = lax.dynamic_slice_in_dim(small_all[:taps], seq_place * channels, channels, 1)
    gain_mix, gain_ffn_one, gain_attn, gain_ffn_two = (small_all[taps + i] for i in range(4))
    head_gains = small_all[taps + 4 : taps + 6].reshape(2, dp_count, slots)
    head_gains = jnp.tile(head_gains[:, :, : head // dp_count].reshape(2, head), (1, 2))

    x_flat = x_in.reshape(length, width).astype(F32)
    normed_one, projected, gated, near_out, far_out = conv_forward(
        place, bounds, x_blocks, mix_all, out_block, kernel, gain_mix[None, :]
    )
    near_out, late_bounds, *cotangent_blocks = tie(near_out, bounds, *cotangent_blocks)
    order = jnp.arange(full, dtype=jnp.int32)
    starts = doc_starts(late_bounds, order)
    cosine, sine = rope_tables(order - starts, head)
    mixed, cosine, sine = seq_scatter(near_out, far_out, cosine, sine)
    hidden_one = x_flat + mixed
    starts = starts[None, :]

    unit_two, scale_two = unit_scale(hidden_one)
    near_two = (unit_two * gain_ffn_one).astype(BF16)
    far_two = far_half(near_two)
    blocks_two = near_blocks(near_two) + near_blocks(far_two)
    terms_one, partial_one = ffn_forward(blocks_two, ffn_one, hidden)
    mixed, qkv_block, o_block = seq_scatter(*halves_of(partial_one), qkv_block, o_block)
    hidden_two = hidden_one + mixed

    unit_three, scale_three = unit_scale(hidden_two)
    near_three = (unit_three * gain_attn).astype(BF16)
    blocks_three = near_blocks(near_three) + near_blocks(far_half(near_three))
    kv_width = (qkv_width - channels) // 2
    raw, attended_low, wide, totals, near_out, far_out = attention_forward(
        place, blocks_three, qkv_block, o_block, cosine, sine, starts, head_gains
    )
    hidden_three = hidden_two + seq_scatter(near_out, far_out)

    unit_four, scale_four = unit_scale(hidden_three)
    near_four = (unit_four * gain_ffn_two).astype(BF16)
    far_four = far_half(near_four)
    near_four = near_blocks(near_four)
    half = len(near_four)
    kept_two, near_out = ffn_turn(
        near_four, cotangent_blocks[:half], ffn_two, hidden, 0, None
    )
    far_four, near_out = tie(far_four, near_out)
    far_four = near_blocks(far_four)
    kept_two, far_out = ffn_turn(
        far_four, cotangent_blocks[half:], ffn_two, hidden, 1, kept_two
    )

    grad_four = cotangent.reshape(length, width).astype(F32)
    kept_two, far_out = tie(kept_two, far_out)
    normed_four = jnp.concatenate(near_four + far_four, 0)
    d_gate_up = left_dot(normed_four, kept_two[:, : 2 * hidden]).astype(BF16)
    d_ffn_in, d_gate_up = seq_scatter(near_out, far_out, d_gate_up)
    d_hidden, d_gain_ffn_two = norm_back(d_ffn_in, gain_ffn_two, unit_four, scale_four)
    grad_three = grad_four + d_hidden

    grad_attn = grad_three.astype(BF16)
    far_attn = far_half(grad_attn)
    d_down = left_dot(jnp.concatenate(cotangent_blocks, 0), kept_two[:, 2 * hidden :])
    grads_two = jnp.concatenate([d_gate_up, d_down.astype(BF16)], 1)
    far_attn, grads_two = tie(far_attn, grads_two)
    owned_two = dp_scatter(grads_two)
    grad_blocks = near_blocks(grad_attn) + near_blocks(far_attn)
    d_raw, near_out, far_out, d_head_gains = attention_backward(
        place, grad_blocks, qkv_block, o_block, cosine, sine, starts, head_gains,
        raw, wide, totals,
    )
    d_head_gains = d_head_gains[:, :head] + d_head_gains[:, head:]
    d_qkv = left_dot(jnp.concatenate(blocks_three, 0), d_raw)
    d_w_o = left_dot(attended_low, jnp.concatenate(grad_blocks, 0))
    d_w_o = pack_rows(d_w_o.astype(BF16), dp_count)
    d_attn_in, *grads_attn = seq_scatter(near_out, far_out, d_qkv.astype(BF16), d_w_o)
    d_attn_h, d_gain_attn = norm_back(d_attn_in, gain_attn, unit_three, scale_three)
    grad_two = grad_three + d_attn_h

    near_grad = grad_two.astype(BF16)
    far_grad = far_half(near_grad)
    near_grad = near_blocks(near_grad)
    kept_one, near_out = ffn_backward(near_grad, terms_one, ffn_one, hidden, 0, None)
    far_grad, near_out = tie(far_grad, near_out)
    far_grad = near_blocks(far_grad)
    kept_one, far_out = ffn_backward(far_grad, terms_one, ffn_one, hidden, 1, kept_one)
    kept_one, far_out = tie(kept_one, far_out)
    d_gate_up = left_dot(jnp.concatenate(blocks_two, 0), kept_one).astype(BF16)
    d_ffn_in_one, d_gate_up = seq_scatter(near_out, far_out, d_gate_up)
    owned_one = dp_scatter(jnp.concatenate([d_gate_up, *grads_attn], 1))
    d_hidden_one, d_gain_ffn_one = norm_back(d_ffn_in_one, gain_ffn_one, unit_two, scale_two)
    grad_one = grad_two + d_hidden_one

    grad_mix = grad_one.astype(BF16)
    far_mix = far_half(grad_mix)
    d_down = left_dot(
        jnp.concatenate(near_grad + far_grad, 0), terms_one[:, 2 * hidden :]
    ).astype(BF16)
    far_mix, d_down = tie(far_mix, d_down)
    mix_blocks = near_blocks(grad_mix) + near_blocks(far_mix)
    mix_blocks[-1], owned_two = tie(mix_blocks[-1], owned_two)
    d_projected, near_out, far_out, kernel_grads = conv_backward(
        place, bounds, mix_blocks, projected, mix_all, out_block, kernel
    )
    d_w_in = left_dot(normed_one, d_projected)
    d_w_out = left_dot(gated, jnp.concatenate(mix_blocks, 0))
    grads_mix = jnp.concatenate(
        [d_down, d_w_in.astype(BF16), pack_rows(d_w_out.astype(BF16), dp_count)], 1
    )
    grads_mix, kept_two = tie(grads_mix, kept_two)
    d_normed = seq_scatter(near_out, far_out)
    unit_one, scale_one = unit_scale(x_flat)
    d_x_part, d_gain_mix = norm_back(d_normed, gain_mix, unit_one, scale_one)
    d_x = (grad_one + d_x_part).reshape(rows, length, width)

    kernel_wide = lax.dynamic_update_slice_in_dim(
        jnp.zeros((taps, width), F32), kernel_grads, seq_place * channels, 1
    )
    head_wide = jnp.pad(
        d_head_gains.reshape(2, dp_count, -1),
        ((0, 0), (0, 0), (0, slots - head // dp_count)),
    ).reshape(2, width)
    vectors = jnp.concatenate(
        [
            jnp.stack([d_gain_mix, d_gain_ffn_one, d_gain_attn, d_gain_ffn_two]),
            kernel_wide,
            head_wide,
        ],
        0,
    )
    vector_columns = jnp.pad(vectors.T, ((0, 0), (0, 128 - vectors.shape[0])))
    owned_vectors = dp_scatter_small(vector_columns.astype(BF16))

    def redeal(block):
        return pack_piece(undeal_rows(unpack_piece(block, width)), channels)

    ffn_out = right_dot(kept_two[:, 2 * hidden :], ffn_two[:, 2 * hidden :])
    hidden_four = hidden_three + seq_scatter(*halves_of(ffn_out))
    out = hidden_four.astype(BF16).reshape(rows, length, width)
    d_wgate_two, d_wup_two, d_down_two = assemble(
        place, share(owned_two), [(n * hidden, hidden, 1, False) for n in range(3)]
    )
    owned_mix, (out, d_x, d_wgate_two, d_wup_two, d_down_two), owned_one = dp_scatter_pairs(
        grads_mix, (out, d_x, d_wgate_two, d_wup_two, d_down_two), owned_one
    )
    tasks = [(n * hidden, hidden, 1, False) for n in range(2)]
    for columns in (channels, kv_width, kv_width):
        tasks.append((tasks[-1][0] + tasks[-1][1], columns, 1, False))
    d_wgate_one, d_wup_one, d_w_q, d_w_k, d_w_v = assemble(
        place, share(owned_one[:, :-channels]), tasks
    )
    (d_w_o_full,) = assemble(
        place, share(redeal(owned_one[:, -channels:])), [(0, channels, 1, True)]
    )
    shared_vectors = share(owned_vectors)
    owned_mix, d_wgate_one, d_w_o_full, *shared_vectors = tie(
        owned_mix, d_wgate_one, d_w_o_full, *shared_vectors
    )
    shared_mix = share(owned_mix[:, :-channels])
    shared_out = share(redeal(owned_mix[:, -channels:]))
    d_down_one, d_w_in_full = assemble(
        place, shared_mix, [(0, hidden, 1, False), (hidden, 3 * channels, 3, False)]
    )
    (d_w_out_full,) = assemble(place, shared_out, [(0, channels, 1, True)])
    sums = sum(block.astype(F32) for block in shared_vectors).T
    small_head = head // dp_count
    return (
        out,
        d_x,
        d_w_in_full,
        sums[4 : 4 + taps],
        d_w_out_full,
        d_wgate_one,
        d_wup_one,
        d_down_one,
        sums[0],
        sums[1],
        d_w_q,
        d_w_k,
        d_w_v,
        d_w_o_full,
        sums[4 + taps, :small_head],
        sums[5 + taps, :small_head],
        d_wgate_two,
        d_wup_two,
        d_down_two,
        sums[2],
        sums[3],
    )


def solution(mesh):
    matrix = P("dp", None)
    vector = P("dp")
    tokens = P("dp", "seq", None)
    kernel = P(None, "dp")
    in_specs = (
        (tokens, matrix, P("dp", "seq"), tokens, matrix, kernel)
        + (matrix,) * 4
        + (vector,) * 2
        + (matrix,) * 4
        + (vector,) * 2
        + (matrix,) * 3
        + (vector,) * 2
    )
    out_specs = (
        (tokens, tokens, matrix, kernel)
        + (matrix,) * 4
        + (vector,) * 2
        + (matrix,) * 4
        + (vector,) * 2
        + (matrix,) * 3
        + (vector,) * 2
    )
    return jax.shard_map(local, mesh=mesh, in_specs=in_specs, out_specs=out_specs, check_vma=False)
```

```python
import jax
import jax.numpy as jnp
from jax import lax
from jax.experimental import pallas as pl
from jax.experimental.pallas import tpu as pltpu
from jax.sharding import PartitionSpec as P

EPS = 1e-05
THETA = 1000000.0
NEG = -1e30
F32 = jnp.float32
BF16 = jnp.bfloat16
TILE = 256
LANES = 128
VMEM_LIMIT = 48 << 20


def left_dot(left, right):
    return lax.dot_general(left, right, (((0,), (0,)), ((), ())), preferred_element_type=F32)


def right_dot(left, right):
    return lax.dot_general(left, right, (((1,), (1,)), ((), ())), preferred_element_type=F32)


def plain_dot(left, right):
    return jnp.dot(left, right, preferred_element_type=F32)


def unit_scale(value):
    scale = lax.rsqrt(jnp.mean(value * value, -1, keepdims=True) + EPS)
    return (value * scale, scale)


def norm_back(grad_out, gain, unit, scale):
    weighted = grad_out * gain
    grad_in = scale * (weighted - unit * jnp.mean(weighted * unit, -1, keepdims=True))
    gain_grad = jnp.sum((grad_out * unit).reshape(-1, unit.shape[-1]), 0)
    return (grad_in, gain_grad)


def doc_starts(bounds, places):
    return jnp.max(jnp.where(bounds <= places[..., None], bounds, 0), -1)


def rope_tables(places, head):
    half = head // 2
    freqs = THETA ** (-(2.0 * jnp.arange(half, dtype=F32)) / head)
    angles = places.astype(F32)[:, None] * freqs
    cosine = jnp.cos(angles)
    sine = jnp.sin(angles)
    return (
        jnp.concatenate([cosine] * 4, 1),
        jnp.concatenate([-sine, sine, -sine, sine], 1),
    )


def seq_bits():
    size = lax.axis_size("seq")
    bits = []
    bit = 1
    while bit < size:
        bits.append(bit)
        bit = bit * 2
    return bits


def swap_seq(array, bit):
    size = lax.axis_size("seq")
    return lax.ppermute(array, "seq", [(i, i ^ bit) for i in range(size)])


def tie(*values):
    return lax.optimization_barrier(values)


def near_blocks(block):
    have = {0: block}
    for bit in reversed(seq_bits()[:-1]):
        for place in sorted(have):
            have[place | bit] = swap_seq(have[place], bit)
    return [have[place] for place in sorted(have)]


def far_half(block):
    return swap_seq(block, seq_bits()[-1])


def near_sum(half):
    size = lax.axis_size("seq") // 2
    length = half.shape[0] // size
    have = {place: half[place * length : (place + 1) * length] for place in range(size)}
    for bit in seq_bits()[:-1]:
        for place in sorted(have, reverse=True):
            if place & bit:
                got = swap_seq(have.pop(place).astype(BF16), bit).astype(F32)
                have[place ^ bit] = have[place ^ bit].astype(F32) + got
    return have[0].astype(F32)


def seq_scatter(near, far, *work):
    sent = far_half(near_sum(far).astype(BF16))
    kept = near_sum(near)
    sent, kept, *work = tie(sent, kept, *work)
    total = kept + sent.astype(F32)
    return (total, *work) if work else total


def half_lanes(shape):
    return lax.broadcasted_iota(jnp.int32, shape, 1) < LANES // 2


def head_mean(value):
    row = lax.broadcasted_iota(jnp.int32, (LANES, LANES), 0) < LANES // 2
    column = half_lanes((LANES, LANES))
    ones = jnp.where(row == column, 2.0 / LANES, 0.0).astype(BF16)
    high = value.astype(BF16)
    low = (value - high.astype(F32)).astype(BF16)
    return plain_dot(high, ones) + plain_dot(low, ones)


def swap_quarters(value):
    quarter = LANES // 4
    lane = lax.broadcasted_iota(jnp.int32, value.shape, 1)
    first = (lane // quarter) % 2 == 0
    return jnp.where(
        first, pltpu.roll(value, LANES - quarter, 1), pltpu.roll(value, quarter, 1)
    )


def head_unit(value):
    scale = lax.rsqrt(head_mean(value * value) + EPS)
    return (value * scale, scale)


def pad_pair(value, second):
    lower = half_lanes(value.shape)
    if second:
        high = jnp.where(lower, 0.0, value)
        return (pltpu.roll(high, LANES // 2, 1), high)
    low = jnp.where(lower, value, 0.0)
    return (low, pltpu.roll(low, LANES // 2, 1))


def load_heads(raw_ref, cos_ref, sin_ref, gains_ref, rows, target, length, pairs):
    cosine = cos_ref[pl.ds(target, length), :]
    sine = sin_ref[pl.ds(target, length), :]
    groups = raw_ref.shape[1] // LANES

    def turned(group, gain):
        value = head_unit(raw_ref[rows, group * LANES : (group + 1) * LANES])[0] * gain
        return value * cosine + swap_quarters(value) * sine

    scale = (LANES // 2) ** (-0.5)
    queries = [(turned(g, gains_ref[0:1, :]) * scale).astype(BF16) for g in range(pairs)]
    keys = []
    values = []
    cached = {}
    for g in range(pairs):
        place = pairs * LANES + g * (LANES // 2)
        group, second = divmod(place, LANES)
        if group not in cached:
            cached[group] = turned(group, gains_ref[1:2, :]).astype(BF16).astype(F32)
        keys.append([k.astype(BF16) for k in pad_pair(cached[group], second > 0)])
        place = place + pairs * (LANES // 2)
        group, second = divmod(place, LANES)
        value = raw_ref[rows, group * LANES : (group + 1) * LANES]
        values.append([v.astype(BF16) for v in pad_pair(value, second > 0)])
    return (queries, keys, values)


def allowed_tile(start_ref, first_key, first_query):
    query = first_query + lax.broadcasted_iota(jnp.int32, (1, TILE), 1)
    start = start_ref[0:1, pl.ds(first_query, TILE)]
    key = first_key + lax.broadcasted_iota(jnp.int32, (TILE, TILE), 0)
    return (key >= start) & (key <= query)


def block_rows(block, count, length):
    half, offset = divmod(block, count // 2)
    return (half, slice(offset * length, (offset + 1) * length))


def attention_forward_kernel(place_ref, *refs, length, pairs, tokens):
    token_refs = refs[:tokens]
    (
        qkv_ref, o_ref, cos_ref, sin_ref, start_ref, gains_ref,
        raw_ref, out_ref, wide_ref, total_ref, near_out_ref, far_out_ref,
        query_ref, key_ref, value_ref,
    ) = refs[tokens:]
    full = raw_ref.shape[0]
    count = full // length
    place = place_ref[0]

    for block in range(count):
        target = pl.multiple_of((block ^ place) * length, 8)
        source = slice(block * length, (block + 1) * length)
        raw_ref[source, :] = plain_dot(token_refs[block][...], qkv_ref[...])
        queries, keys, values = load_heads(
            raw_ref, cos_ref, sin_ref, gains_ref, source, target, length, pairs
        )
        for g in range(pairs):
            query_ref[g, pl.ds(target, length), :] = queries[g]
            for h in range(2):
                key_ref[2 * g + h, pl.ds(target, length), :] = keys[g][h]
                value_ref[2 * g + h, pl.ds(target, length), :] = values[g][h]

    half = LANES // 2

    def query_tile(i, _):
        first_query = pl.multiple_of(i * TILE, TILE)

        def key_tile(j, carry):
            first_key = pl.multiple_of(j * TILE, TILE)
            allowed = allowed_tile(start_ref, first_key, first_query)
            sums, outs = carry
            new_sums = []
            new_outs = []
            for g in range(pairs):
                query = query_ref[g, pl.ds(first_query, TILE), :]
                total = outs[g]
                for h in range(2):
                    key = key_ref[2 * g + h, pl.ds(first_key, TILE), :]
                    value = value_ref[2 * g + h, pl.ds(first_key, TILE), :]
                    weight = jnp.where(allowed, jnp.exp(right_dot(key, query)), 0.0)
                    new_sums.append(sums[2 * g + h] + jnp.sum(weight, 0, keepdims=True))
                    total = total + lax.dot_general(
                        value, weight.astype(BF16), (((0,), (0,)), ((), ())),
                        preferred_element_type=F32,
                    )
                new_outs.append(total)
            return (new_sums, new_outs)

        carry = (
            [jnp.zeros((1, TILE), F32) for _ in range(2 * pairs)],
            [jnp.zeros((LANES, TILE), F32) for _ in range(pairs)],
        )
        sums, outs = lax.fori_loop(0, i + 1, key_tile, carry)
        columns = pl.ds(first_query, TILE)
        for g in range(pairs):
            scaled = jnp.concatenate(
                [outs[g][h * half : (h + 1) * half] / sums[2 * g + h] for h in range(2)], 0
            )
            for h in range(2):
                total_ref[2 * g + h : 2 * g + h + 1, columns] = sums[2 * g + h]
            wide_ref[g * LANES : (g + 1) * LANES, columns] = scaled
            query_ref[g, columns, :] = scaled.T.astype(BF16)
        return 0

    lax.fori_loop(0, full // TILE, query_tile, 0)

    for block in range(count):
        side, rows = block_rows(block, count, length)
        source = pl.multiple_of((block ^ place) * length, 8)
        target = slice(block * length, (block + 1) * length)
        for g in range(pairs):
            out_ref[target, g * LANES : (g + 1) * LANES] = query_ref[
                g, pl.ds(source, length), :
            ]
        partial = plain_dot(out_ref[target, :], o_ref[...])
        (near_out_ref, far_out_ref)[side][rows, :] = partial.astype(BF16)


def attention_backward_kernel(place_ref, *refs, length, pairs, tokens):
    token_refs = refs[:tokens]
    (
        qkv_ref, o_ref, cos_ref, sin_ref, start_ref, gains_ref, raw_ref, wide_ref, total_ref,
        out_ref, near_out_ref, far_out_ref, gain_grad_ref,
        query_ref, key_ref, value_ref, hold_ref, dq_ref, dk_ref, dv_ref,
    ) = refs[tokens:]
    full = raw_ref.shape[0]
    count = full // length
    place = place_ref[0]
    half = LANES // 2

    for block in range(count):
        target = pl.multiple_of((block ^ place) * length, 8)
        source = slice(block * length, (block + 1) * length)
        grads = right_dot(token_refs[block][...], o_ref[...]).astype(BF16)
        queries, keys, values = load_heads(
            raw_ref, cos_ref, sin_ref, gains_ref, source, target, length, pairs
        )
        rows = pl.ds(target, length)
        for g in range(pairs):
            query_ref[g, rows, :] = queries[g]
            hold_ref[g, rows, :] = grads[:, g * LANES : (g + 1) * LANES]
            dk_ref[g, rows, :] = jnp.zeros((length, LANES), F32)
            dv_ref[g, rows, :] = jnp.zeros((length, LANES), F32)
            for h in range(2):
                key_ref[2 * g + h, rows, :] = keys[g][h]
                value_ref[2 * g + h, rows, :] = values[g][h]

    lower = half_lanes((TILE, LANES))

    def query_tile(i, _):
        first_query = pl.multiple_of(i * TILE, TILE)
        columns = pl.ds(first_query, TILE)
        inverse = [1.0 / total_ref[n : n + 1, columns] for n in range(2 * pairs)]
        inner = []
        for g in range(pairs):
            grad = hold_ref[g, columns, :].astype(F32).T
            both = grad * wide_ref[g * LANES : (g + 1) * LANES, columns]
            for h in range(2):
                inner.append(jnp.sum(both[h * half : (h + 1) * half], 0, keepdims=True))

        def key_tile(j, outs):
            first_key = pl.multiple_of(j * TILE, TILE)
            rows = pl.ds(first_key, TILE)
            allowed = allowed_tile(start_ref, first_key, first_query)
            new_outs = []
            for g in range(pairs):
                query = query_ref[g, columns, :]
                grad = hold_ref[g, columns, :]
                zero = jnp.zeros_like(query)
                total = outs[g]
                d_key = dk_ref[g, rows, :]
                d_value = dv_ref[g, rows, :]
                for h in range(2):
                    keep = lower if h == 0 else jnp.logical_not(lower)
                    key = key_ref[2 * g + h, rows, :]
                    value = value_ref[2 * g + h, rows, :]
                    weight = jnp.exp(right_dot(key, query)) * inverse[2 * g + h]
                    weight = jnp.where(allowed, weight, 0.0)
                    d_weight = right_dot(value, grad)
                    d_score = (weight * (d_weight - inner[2 * g + h])).astype(BF16)
                    d_value = d_value + plain_dot(
                        weight.astype(BF16), jnp.where(keep, grad, zero)
                    )
                    d_key = d_key + plain_dot(d_score, jnp.where(keep, query, zero))
                    total = total + lax.dot_general(
                        key, d_score, (((0,), (0,)), ((), ())), preferred_element_type=F32
                    )
                dk_ref[g, rows, :] = d_key
                dv_ref[g, rows, :] = d_value
                new_outs.append(total)
            return new_outs

        outs = lax.fori_loop(
            0, i + 1, key_tile, [jnp.zeros((LANES, TILE), F32) for _ in range(pairs)]
        )
        for g in range(pairs):
            dq_ref[g, columns, :] = outs[g].T
        return 0

    lax.fori_loop(0, full // TILE, query_tile, 0)
    scale = half ** (-0.5)

    low = half_lanes((length, LANES))
    query_gain = jnp.zeros((1, LANES), F32)
    key_gain = jnp.zeros((1, LANES), F32)
    for block in range(count):
        side, side_rows = block_rows(block, count, length)
        rows = pl.ds(pl.multiple_of((block ^ place) * length, 8), length)
        target = slice(block * length, (block + 1) * length)
        cosine = cos_ref[rows, :]
        sine = sin_ref[rows, :]

        def back(grad, group, gain):
            grad = grad.astype(BF16).astype(F32)
            unit, inverse = head_unit(raw_ref[target, group * LANES : (group + 1) * LANES])
            d_rot = grad * cosine + swap_quarters(grad * sine)
            weighted = d_rot * gain
            d_raw = inverse * (weighted - unit * head_mean(weighted * unit))
            return (d_raw, d_rot * unit)

        for g in range(pairs):
            d_raw, terms = back(dq_ref[g, rows, :] * scale, g, gains_ref[0:1, :])
            query_gain = query_gain + jnp.sum(terms, 0, keepdims=True)
            out_ref[target, g * LANES : (g + 1) * LANES] = d_raw.astype(BF16)
        groups = {}
        for kind, held in ((0, dk_ref), (1, dv_ref)):
            for g in range(pairs):
                place_of = pairs * LANES + kind * pairs * half + g * half
                group, second = divmod(place_of, LANES)
                value = held[g, rows, :]
                value = value + pltpu.roll(value, half, 1)
                groups.setdefault(group, {})[second // half] = (kind, value)
        for group, parts in groups.items():
            merged = jnp.where(low, parts[0][1], parts[1][1])
            is_key = [parts[n][0] == 0 for n in range(2)]
            result = merged
            if any(is_key):
                d_raw, terms = back(merged, group, gains_ref[1:2, :])
                if not is_key[1]:
                    d_raw = jnp.where(low, d_raw, merged)
                    terms = jnp.where(low, terms, 0.0)
                result = d_raw
                key_gain = key_gain + jnp.sum(terms, 0, keepdims=True)
            out_ref[target, group * LANES : (group + 1) * LANES] = result.astype(BF16)
        partial = right_dot(out_ref[target, :], qkv_ref[...])
        (near_out_ref, far_out_ref)[side][side_rows, :] = partial.astype(BF16)
    gain_grad_ref[0:1, :] = query_gain
    gain_grad_ref[1:2, :] = key_gain


def whole(count):
    return [pl.BlockSpec(memory_space=pltpu.VMEM)] * count


def attention_forward(place, tokens, qkv, o, cosine, sine, start, gains):
    length = tokens[0].shape[0]
    full = len(tokens) * length
    width, columns = qkv.shape
    pairs = columns // (2 * LANES)
    return pl.pallas_call(
        lambda *refs: attention_forward_kernel(
            *refs, length=length, pairs=pairs, tokens=len(tokens)
        ),
        in_specs=[pl.BlockSpec(memory_space=pltpu.SMEM)] + whole(6 + len(tokens)),
        out_specs=tuple(whole(6)),
        out_shape=(
            jax.ShapeDtypeStruct((full, columns), F32),
            jax.ShapeDtypeStruct((full, pairs * LANES), BF16),
            jax.ShapeDtypeStruct((pairs * LANES, full), F32),
            jax.ShapeDtypeStruct((8, full), F32),
            jax.ShapeDtypeStruct((full // 2, width), BF16),
            jax.ShapeDtypeStruct((full // 2, width), BF16),
        ),
        scratch_shapes=[
            pltpu.VMEM((pairs, full, LANES), BF16),
            pltpu.VMEM((2 * pairs, full, LANES), BF16),
            pltpu.VMEM((2 * pairs, full, LANES), BF16),
        ],
        cost_estimate=pl.CostEstimate(
            flops=20_000_000_000, transcendentals=6_000_000, bytes_accessed=20_000_000
        ),
        compiler_params=pltpu.CompilerParams(vmem_limit_bytes=VMEM_LIMIT),
        name="attention_forward",
    )(place, *tokens, qkv, o, cosine, sine, start, gains)


def attention_backward(place, tokens, qkv, o, cosine, sine, start, gains, raw, wide, totals):
    length = tokens[0].shape[0]
    full = len(tokens) * length
    width, columns = qkv.shape
    pairs = columns // (2 * LANES)
    return pl.pallas_call(
        lambda *refs: attention_backward_kernel(
            *refs, length=length, pairs=pairs, tokens=len(tokens)
        ),
        in_specs=[pl.BlockSpec(memory_space=pltpu.SMEM)] + whole(9 + len(tokens)),
        out_specs=tuple(whole(4)),
        out_shape=(
            jax.ShapeDtypeStruct((full, columns), BF16),
            jax.ShapeDtypeStruct((full // 2, width), BF16),
            jax.ShapeDtypeStruct((full // 2, width), BF16),
            jax.ShapeDtypeStruct((2, LANES), F32),
        ),
        scratch_shapes=[
            pltpu.VMEM((pairs, full, LANES), BF16),
            pltpu.VMEM((2 * pairs, full, LANES), BF16),
            pltpu.VMEM((2 * pairs, full, LANES), BF16),
            pltpu.VMEM((pairs, full, LANES), BF16),
            pltpu.VMEM((pairs, full, LANES), F32),
            pltpu.VMEM((pairs, full, LANES), F32),
            pltpu.VMEM((pairs, full, LANES), F32),
        ],
        cost_estimate=pl.CostEstimate(
            flops=20_000_000_000, transcendentals=6_000_000, bytes_accessed=20_000_000
        ),
        compiler_params=pltpu.CompilerParams(vmem_limit_bytes=VMEM_LIMIT),
        name="attention_backward",
    )(place, *tokens, qkv, o, cosine, sine, start, gains, raw, wide, totals)


def column_block(weight, parts):
    size = lax.axis_size("seq")
    place = lax.axis_index("seq")
    rows, columns = weight.shape
    block = columns // parts // size
    split = weight.reshape(rows, parts, size * block)
    return lax.dynamic_slice_in_dim(split, place * block, block, 2).reshape(rows, parts * block)


def deal_pairs():
    size = lax.axis_size("seq")
    count = lax.axis_size("dp")
    pairs = []
    for place in range(size):
        for owner in range(count):
            source = (owner % size) * count + place * (count // size) + owner // size
            pairs.append((source, place * count + owner))
    return pairs


def deal_rows(*weights):
    size = lax.axis_size("seq")
    place = lax.axis_index("seq")
    piece = weights[0].shape[0] // size
    parts = [lax.dynamic_slice_in_dim(w, place * piece, piece, 0) for w in weights]
    dealt = lax.ppermute(jnp.concatenate(parts, 0), ("seq", "dp"), deal_pairs())
    return [dealt[n * piece : (n + 1) * piece] for n in range(len(weights))]


def pack_piece(piece, columns):
    count = piece.shape[1] // columns
    return jnp.concatenate(
        [piece[:, n * columns : (n + 1) * columns] for n in range(count)], 0
    )


def unpack_piece(block, width):
    count = width // block.shape[1]
    rows = block.shape[0] // count
    return jnp.concatenate([block[n * rows : (n + 1) * rows] for n in range(count)], 1)


def pack_rows(rows_block, parts):
    rows, width = rows_block.shape
    piece = rows // parts
    split = rows_block.reshape(parts, piece, width // rows, rows)
    return jnp.swapaxes(split, 1, 2).reshape(width, rows)


def unpack_rows(block, parts):
    width, rows = block.shape
    split = block.reshape(parts, width // rows, rows // parts, rows)
    return jnp.swapaxes(split, 1, 2).reshape(rows, width)


def undeal_rows(part):
    return lax.ppermute(part, ("seq", "dp"), [(b, a) for a, b in deal_pairs()])


def dp_gather(block):
    return lax.all_gather(block, "dp", axis=0, tiled=True)


def dp_scatter(grads):
    return lax.psum_scatter(grads, "dp", scatter_dimension=0, tiled=True)


def swap_dp(array, bit):
    size = lax.axis_size("dp")
    return lax.ppermute(array, "dp", [(i, i ^ bit) for i in range(size)])


def dp_bits():
    return [1, 2, 4] if lax.axis_size("dp") == 8 else []


def dp_gather_small(block, later):
    if not dp_bits():
        return (dp_gather(block), later)
    size = lax.axis_size("dp")
    place = lax.axis_index("dp")
    rows = block.shape[0]
    near, middle, far = dp_bits()
    have = {0: block, far: swap_dp(block, far), middle: swap_dp(block, middle)}
    have[near] = swap_dp(block, near)
    have[far], later = tie(have[far], later)
    have[far | middle] = swap_dp(have[far], middle)
    for turn in (middle, far, far | middle):
        have[turn | near] = swap_dp(have[turn], near)
    result = jnp.zeros((size * rows, block.shape[1]), block.dtype)
    for turn in range(size):
        result = lax.dynamic_update_slice_in_dim(result, have[turn], (place ^ turn) * rows, 0)
    return (result, later)


def dp_scatter_small(grads):
    if not dp_bits():
        return dp_scatter(grads)
    size = lax.axis_size("dp")
    place = lax.axis_index("dp")
    sums = grads.reshape(size, -1, grads.shape[1]).astype(F32)
    for bit in dp_bits():
        split = sums.reshape(-1, 2, *sums.shape[1:])
        side = (place // bit) % 2
        kept = lax.dynamic_index_in_dim(split, side, 1, False)
        sent = lax.dynamic_index_in_dim(split, 1 - side, 1, False).astype(BF16)
        sums = kept + swap_dp(sent, bit).astype(F32)
    return sums[0].astype(BF16)


def dp_pair_parts(grads):
    if not dp_bits():
        return (grads, grads[:8])
    size = lax.axis_size("dp")
    side = lax.axis_index("dp") % 2
    columns = grads.shape[1]
    blocks = grads.reshape(size // 2, 2, -1, columns)
    kept = lax.dynamic_index_in_dim(blocks, side, 1, False).reshape(-1, columns)
    sent = lax.dynamic_index_in_dim(blocks, 1 - side, 1, False).reshape(-1, columns)
    return (kept, sent)


def dp_scatter_pairs(kept, sent, work, later):
    if not dp_bits():
        kept, later, *work = tie(kept, later, *work)
        return (dp_scatter(kept), work, later)
    size = lax.axis_size("dp")
    got, *work = tie(swap_dp(sent, 1), *work)
    sums = (kept.astype(F32) + got.astype(F32)).astype(BF16)
    sums, later = tie(sums, later)
    groups = [list(range(n, size, 2)) for n in range(2)]
    owned = lax.psum_scatter(
        sums, "dp", scatter_dimension=0, tiled=True, axis_index_groups=groups
    )
    return (owned, work, later)


def share(owned):
    return near_blocks(owned) + near_blocks(far_half(owned))


def assemble_kernel(place_ref, *refs, count, tasks):
    blocks = refs[:count]
    outs = refs[count:]
    place = place_ref[0]
    for turn in range(count):
        for target in range(count):

            @pl.when((place ^ turn) == target)
            def _():
                for (start, columns, split, by_rows), out_ref in zip(tasks, outs):
                    if by_rows:
                        rows = blocks[turn].shape[0] // count
                        for part in range(count):
                            out_ref[
                                target * rows : (target + 1) * rows,
                                part * columns : (part + 1) * columns,
                            ] = blocks[turn][
                                part * rows : (part + 1) * rows, start : start + columns
                            ].astype(F32)
                    else:
                        step = columns // split
                        for part in range(split):
                            first = (part * count + target) * step
                            out_ref[:, first : first + step] = blocks[turn][
                                :, start + part * step : start + (part + 1) * step
                            ].astype(F32)


def assemble(place, blocks, tasks):
    count = len(blocks)
    rows = blocks[0].shape[0]
    if all(columns // split % LANES == 0 for _, columns, split, _ in tasks):
        return pl.pallas_call(
            lambda *refs: assemble_kernel(*refs, count=count, tasks=tasks),
            in_specs=[pl.BlockSpec(memory_space=pltpu.SMEM)] + whole(count),
            out_specs=tuple(whole(len(tasks))),
            out_shape=tuple(
                jax.ShapeDtypeStruct((rows, count * columns), F32) for _, columns, _, _ in tasks
            ),
            compiler_params=pltpu.CompilerParams(vmem_limit_bytes=VMEM_LIMIT),
            name="assemble",
        )(place, *blocks)
    stacked = jnp.stack(blocks, 0)
    ordered = [
        lax.dynamic_index_in_dim(stacked, place[0] ^ i, 0, False) for i in range(count)
    ]
    results = []
    for start, columns, split, by_rows in tasks:
        parts = [block[:, start : start + columns] for block in ordered]
        if by_rows:
            joined = jnp.concatenate([unpack_piece(p, count * columns) for p in parts], 0)
        else:
            step = columns // split
            joined = jnp.concatenate(
                [p[:, n * step : (n + 1) * step] for n in range(split) for p in parts], 1
            )
        results.append(joined.astype(F32))
    return results


def gate_terms(normed, w_gate, w_up):
    gate = plain_dot(normed, w_gate)
    upper = plain_dot(normed, w_up)
    sigma = jax.nn.sigmoid(gate)
    swish = gate * sigma
    return (upper * (sigma + swish * (1.0 - sigma)), swish, swish * upper)


def block_here(refs):
    value = refs[0][...]
    for number, ref in enumerate(refs[1:]):
        value = jnp.where(pl.program_id(0) == number + 1, ref[...], value)
    return value


def ffn_forward_kernel(*refs, count):
    normed_refs = refs[:count]
    gate_ref, up_ref, down_ref = refs[count : count + 3]
    kept_ref, partial_ref = refs[-2:]
    hidden = gate_ref.shape[1]
    slope, swish, act = gate_terms(block_here(normed_refs), gate_ref[...], up_ref[...])
    act = act.astype(BF16)
    kept_ref[:, :hidden] = slope.astype(BF16)
    kept_ref[:, hidden : 2 * hidden] = swish.astype(BF16)
    kept_ref[:, 2 * hidden :] = act
    partial_ref[...] = right_dot(act, down_ref[...]).astype(BF16)


def ffn_turn_kernel(*refs, count):
    normed_refs = refs[:count]
    grad_refs = refs[count : 2 * count]
    gate_ref, up_ref, down_ref = refs[2 * count : 2 * count + 3]
    kept_ref, partial_ref = refs[-2:]
    hidden = gate_ref.shape[1]
    slope, swish, act = gate_terms(block_here(normed_refs), gate_ref[...], up_ref[...])
    d_act = plain_dot(block_here(grad_refs), down_ref[...])
    d_gate = (d_act * slope).astype(BF16)
    d_up = (d_act * swish).astype(BF16)
    kept_ref[:, :hidden] = d_gate
    kept_ref[:, hidden : 2 * hidden] = d_up
    kept_ref[:, 2 * hidden :] = act.astype(BF16)
    partial = right_dot(d_gate, gate_ref[...]) + right_dot(d_up, up_ref[...])
    partial_ref[...] = partial.astype(BF16)


def ffn_backward_kernel(*refs, count):
    grad_refs = refs[:count]
    terms_ref, gate_ref, up_ref, down_ref = refs[count : count + 4]
    kept_ref, partial_ref = refs[-2:]
    hidden = gate_ref.shape[1]
    d_act = plain_dot(block_here(grad_refs), down_ref[...])
    d_gate = (d_act * terms_ref[:, :hidden].astype(F32)).astype(BF16)
    d_up = (d_act * terms_ref[:, hidden:].astype(F32)).astype(BF16)
    kept_ref[:, :hidden] = d_gate
    kept_ref[:, hidden:] = d_up
    partial = right_dot(d_gate, gate_ref[...]) + right_dot(d_up, up_ref[...])
    partial_ref[...] = partial.astype(BF16)


def ffn_call(kernel, name, tokens, terms, weights, hidden, first, full, kept_width, kept):
    width = weights.shape[0]
    count = len(tokens[0])
    length = tokens[0][0].shape[0]
    operands = [block for blocks in tokens for block in blocks]
    in_specs = [
        pl.BlockSpec((length, width), lambda i: (0, 0), pipeline_mode=pl.Buffered(1))
        for _ in operands
    ]
    if terms is not None:
        in_specs.append(pl.BlockSpec((length, 2 * hidden), lambda i: (i + first, 0)))
        operands.append(terms)
    for place in range(3):
        in_specs.append(
            pl.BlockSpec(
                (width, hidden), lambda i, place=place: (0, place), pipeline_mode=pl.Buffered(1)
            )
        )
        operands.append(weights)
    aliases = {}
    if kept is not None:
        aliases = {len(operands): 0}
        in_specs.append(pl.BlockSpec(memory_space=pl.ANY))
        operands.append(kept)
    return pl.pallas_call(
        lambda *refs: kernel(*refs, count=count),
        grid=(count,),
        in_specs=in_specs,
        out_specs=(
            pl.BlockSpec((length, kept_width), lambda i: (i + first, 0)),
            pl.BlockSpec((length, width), lambda i: (i, 0)),
        ),
        out_shape=(
            jax.ShapeDtypeStruct((full, kept_width), BF16),
            jax.ShapeDtypeStruct((count * length, width), BF16),
        ),
        input_output_aliases=aliases,
        cost_estimate=pl.CostEstimate(
            flops=6_000_000_000, transcendentals=1_000_000, bytes_accessed=20_000_000
        ),
        compiler_params=pltpu.CompilerParams(vmem_limit_bytes=VMEM_LIMIT),
        name=name,
    )(*operands)


def split_weights(weights, hidden):
    return [weights[:, n * hidden : (n + 1) * hidden] for n in range(3)]


def halves_of(array):
    half = array.shape[0] // 2
    return (array[:half], array[half:])


def place_rows(kept, part, number):
    if kept is None:
        kept = jnp.zeros((2 * part.shape[0], part.shape[1]), part.dtype)
    return lax.dynamic_update_slice_in_dim(kept, part, number * part.shape[0], 0)


def ffn_forward(normed, weights, hidden):
    if hidden % LANES:
        w_gate, w_up, w_down = split_weights(weights, hidden)
        terms = gate_terms(jnp.concatenate(normed, 0), w_gate, w_up)
        terms = jnp.concatenate(terms, 1).astype(BF16)
        return (terms, right_dot(terms[:, 2 * hidden :], w_down).astype(BF16))
    return ffn_call(
        ffn_forward_kernel, "ffn_forward", [normed], None, weights, hidden,
        0, len(normed) * normed[0].shape[0], 3 * hidden, None,
    )


def ffn_turn(normed, grads, weights, hidden, number, kept):
    if hidden % LANES:
        w_gate, w_up, w_down = split_weights(weights, hidden)
        slope, swish, act = gate_terms(jnp.concatenate(normed, 0), w_gate, w_up)
        d_act = plain_dot(jnp.concatenate(grads, 0), w_down)
        part = jnp.concatenate([d_act * slope, d_act * swish, act], 1).astype(BF16)
        partial = right_dot(part[:, : 2 * hidden], weights[:, : 2 * hidden]).astype(BF16)
        return (place_rows(kept, part, number), partial)
    count = len(normed)
    return ffn_call(
        ffn_turn_kernel, "ffn_turn", [normed, grads], None, weights, hidden,
        number * count, 2 * count * normed[0].shape[0], 3 * hidden, kept,
    )


def ffn_backward(grads, terms, weights, hidden, number, kept):
    count = len(grads)
    length = grads[0].shape[0]
    if hidden % LANES:
        w_gate, w_up, w_down = split_weights(weights, hidden)
        rows = slice(number * count * length, (number + 1) * count * length)
        d_act = plain_dot(jnp.concatenate(grads, 0), w_down)
        slope = terms[rows, :hidden].astype(F32)
        swish = terms[rows, hidden : 2 * hidden].astype(F32)
        part = jnp.concatenate([d_act * slope, d_act * swish], 1).astype(BF16)
        partial = right_dot(part, weights[:, : 2 * hidden]).astype(BF16)
        return (place_rows(kept, part, number), partial)
    return ffn_call(
        ffn_backward_kernel, "ffn_backward", [grads], terms, weights, hidden,
        number * count, 2 * count * length, 2 * hidden, kept,
    )


def row_starts(bounds_ref, token):
    start = jnp.zeros(token.shape, jnp.int32)
    for number in range(1, bounds_ref.shape[0]):
        bound = bounds_ref[number]
        start = jnp.where(bound <= token, jnp.maximum(start, bound), start)
    return start


def conv_backward_kernel(*refs, length, tokens, taps):
    place_ref, bounds_ref = refs[:2]
    grad_refs = refs[2 : 2 + tokens]
    (
        projected_ref, in_ref, out_w_ref, tap_ref,
        d_projected_ref, near_out_ref, far_out_ref, tap_grad_ref,
        product_ref, d_gated_ref, d_conv_ref,
    ) = refs[2 + tokens :]
    place = place_ref[0]
    channels = out_w_ref.shape[0]
    full = tokens * length
    product_ref[0:8, :] = jnp.zeros((8, channels), F32)
    d_conv_ref[full : full + 8, :] = jnp.zeros((8, channels), F32)
    for block in range(tokens):
        rows = slice(block * length, (block + 1) * length)
        first = pl.multiple_of((block ^ place) * length, 8)
        d_gated_ref[rows, :] = right_dot(grad_refs[block][...], out_w_ref[...])
        product = projected_ref[rows, :channels] * projected_ref[rows, 2 * channels :]
        product_ref[pl.ds(pl.multiple_of(8 + first, 8), length), :] = product.astype(BF16).astype(F32)
    tap_grads = [jnp.zeros((1, channels), F32) for _ in range(taps)]
    for block in range(tokens):
        rows = slice(block * length, (block + 1) * length)
        first = pl.multiple_of((block ^ place) * length, 8)
        window = product_ref[pl.ds(first, length + 8), :]
        token = first + lax.broadcasted_iota(jnp.int32, (length, channels), 0)
        start = row_starts(bounds_ref, token)
        d_gated = d_gated_ref[rows, :]
        d_conv = d_gated * projected_ref[rows, channels : 2 * channels]
        conv = jnp.zeros((length, channels), F32)
        for tap in range(taps):
            moved = window[8 - tap : 8 - tap + length, :]
            moved = jnp.where(token - tap >= start, moved, 0.0)
            conv = conv + tap_ref[tap : tap + 1, :] * moved
            tap_grads[tap] = tap_grads[tap] + jnp.sum(d_conv * moved, 0, keepdims=True)
        d_projected_ref[rows, channels : 2 * channels] = (d_gated * conv).astype(BF16)
        d_conv_ref[pl.ds(first, length), :] = d_conv
    for tap in range(taps):
        tap_grad_ref[tap : tap + 1, :] = tap_grads[tap]
    for block in range(tokens):
        side, side_rows = block_rows(block, tokens, length)
        rows = slice(block * length, (block + 1) * length)
        first = pl.multiple_of((block ^ place) * length, 8)
        window = d_conv_ref[pl.ds(first, length + 8), :]
        token = first + lax.broadcasted_iota(jnp.int32, (length, channels), 0)
        total = tap_ref[0:1, :] * window[:length, :]
        for tap in range(1, taps):
            same = token >= row_starts(bounds_ref, token + tap)
            total = total + tap_ref[tap : tap + 1, :] * jnp.where(
                same, window[tap : tap + length, :], 0.0
            )
        d_product = total.astype(BF16).astype(F32)
        d_projected_ref[rows, :channels] = (
            d_product * projected_ref[rows, 2 * channels :]
        ).astype(BF16)
        d_projected_ref[rows, 2 * channels :] = (
            d_product * projected_ref[rows, :channels]
        ).astype(BF16)
        partial = right_dot(d_projected_ref[rows, :], in_ref[:, : 3 * channels])
        (near_out_ref, far_out_ref)[side][side_rows, :] = partial.astype(BF16)


def conv_backward(place, bounds, grads, projected, in_weights, out_weights, kernel):
    length, width = grads[0].shape
    full = len(grads) * length
    channels = out_weights.shape[0]
    taps = kernel.shape[0]
    scalar = pl.BlockSpec(memory_space=pltpu.SMEM)
    return pl.pallas_call(
        lambda *refs: conv_backward_kernel(*refs, length=length, tokens=len(grads), taps=taps),
        in_specs=[scalar, scalar] + whole(len(grads) + 4),
        out_specs=tuple(whole(4)),
        out_shape=(
            jax.ShapeDtypeStruct((full, 3 * channels), BF16),
            jax.ShapeDtypeStruct((full // 2, width), BF16),
            jax.ShapeDtypeStruct((full // 2, width), BF16),
            jax.ShapeDtypeStruct((taps, channels), F32),
        ),
        scratch_shapes=[
            pltpu.VMEM((full + 8, channels), F32),
            pltpu.VMEM((full, channels), F32),
            pltpu.VMEM((full + 8, channels), F32),
        ],
        cost_estimate=pl.CostEstimate(flops=0, transcendentals=0, bytes_accessed=100_000),
        compiler_params=pltpu.CompilerParams(vmem_limit_bytes=VMEM_LIMIT),
        name="conv_backward",
    )(place, bounds, *grads, projected, in_weights, out_weights, kernel)


def conv_forward_kernel(*refs, length, tokens, taps):
    place_ref, bounds_ref = refs[:2]
    token_refs = refs[2 : 2 + tokens]
    (
        in_ref, out_w_ref, tap_ref, gain_ref,
        normed_ref, projected_ref, gated_ref, near_out_ref, far_out_ref, product_ref,
    ) = refs[2 + tokens :]
    place = place_ref[0]
    channels = gated_ref.shape[1]
    product_ref[0:8, :] = jnp.zeros((8, channels), F32)
    for block in range(tokens):
        rows = slice(block * length, (block + 1) * length)
        value = token_refs[block][...].astype(F32)
        scale = lax.rsqrt(jnp.mean(value * value, -1, keepdims=True) + EPS)
        normed = (value * scale * gain_ref[...]).astype(BF16)
        normed_ref[rows, :] = normed
        projected = plain_dot(normed, in_ref[:, : 3 * channels])
        projected_ref[rows, :] = projected
        product = (projected[:, :channels] * projected[:, 2 * channels :]).astype(BF16)
        target = pl.multiple_of(8 + (block ^ place) * length, 8)
        product_ref[pl.ds(target, length), :] = product.astype(F32)
    for block in range(tokens):
        side, side_rows = block_rows(block, tokens, length)
        rows = slice(block * length, (block + 1) * length)
        first = pl.multiple_of((block ^ place) * length, 8)
        window = product_ref[pl.ds(first, length + 8), :]
        token = first + lax.broadcasted_iota(jnp.int32, (length, channels), 0)
        start = row_starts(bounds_ref, token)
        conv = tap_ref[0:1, :] * window[8:, :]
        for tap in range(1, taps):
            moved = window[8 - tap : 8 - tap + length, :]
            moved = jnp.where(token - tap >= start, moved, 0.0)
            conv = conv + tap_ref[tap : tap + 1, :] * moved
        gated = (projected_ref[rows, channels : 2 * channels] * conv).astype(BF16)
        gated_ref[rows, :] = gated
        partial = plain_dot(gated, out_w_ref[...]).astype(BF16)
        (near_out_ref, far_out_ref)[side][side_rows, :] = partial


def conv_forward(place, bounds, tokens, in_weights, out_weights, kernel, gain):
    length, width = tokens[0].shape
    full = len(tokens) * length
    channels = out_weights.shape[0]
    taps = kernel.shape[0]
    scalar = pl.BlockSpec(memory_space=pltpu.SMEM)
    return pl.pallas_call(
        lambda *refs: conv_forward_kernel(*refs, length=length, tokens=len(tokens), taps=taps),
        in_specs=[scalar, scalar] + whole(len(tokens) + 4),
        out_specs=tuple(whole(5)),
        out_shape=(
            jax.ShapeDtypeStruct((full, width), BF16),
            jax.ShapeDtypeStruct((full, 3 * channels), F32),
            jax.ShapeDtypeStruct((full, channels), BF16),
            jax.ShapeDtypeStruct((full // 2, width), BF16),
            jax.ShapeDtypeStruct((full // 2, width), BF16),
        ),
        scratch_shapes=[pltpu.VMEM((full + 8, channels), F32)],
        cost_estimate=pl.CostEstimate(
            flops=4_000_000_000, transcendentals=2_000, bytes_accessed=20_000_000
        ),
        compiler_params=pltpu.CompilerParams(vmem_limit_bytes=VMEM_LIMIT),
        name="conv_forward",
    )(place, bounds, *tokens, in_weights, out_weights, kernel, gain)


def local(
    x_in,
    cu_seqlens,
    positions,
    cotangent,
    w_in,
    conv_w,
    w_out,
    w_gate1,
    w_up1,
    w_down1,
    g_mix1,
    g_ffn1,
    w_q,
    key_projection_weight,
    value_projection_weight,
    w_o,
    g_q,
    g_k,
    w_gate2,
    w_up2,
    w_down2,
    g_attn2,
    g_ffn2,
):
    rows, length, width = x_in.shape
    assert rows == 1
    seq_count = lax.axis_size("seq")
    dp_count = lax.axis_size("dp")
    seq_place = lax.axis_index("seq")
    full = length * seq_count
    channels = width // seq_count
    slots = width // dp_count
    head = g_q.shape[0] * dp_count
    taps = conv_w.shape[0]

    dealt_out, dealt_o = deal_rows(w_out, w_o)
    x_low, dealt_out, dealt_o = tie(x_in.reshape(length, width), dealt_out, dealt_o)
    x_far = far_half(x_low)
    cotangent_low, x_far = tie(cotangent.reshape(length, width), x_far)
    x_blocks = near_blocks(x_low) + near_blocks(x_far)
    cotangent_blocks = near_blocks(cotangent_low) + near_blocks(far_half(cotangent_low))
    head_gains = jnp.pad(jnp.stack([g_q, g_k], 1), ((0, slots - head // dp_count), (0, 0)))
    small = jnp.concatenate(
        [conv_w.T, jnp.stack([g_mix1, g_ffn1, g_attn2, g_ffn2], 1), head_gains], 1
    )
    small = jnp.pad(small, ((0, 0), (0, 128 - small.shape[1])))
    out_piece = pack_piece(dealt_out, channels)
    o_piece = pack_piece(dealt_o, channels)
    mix_block = jnp.concatenate([column_block(w_in, 3), small, out_piece], 1)
    mix_block, w_gate1, w_up1, w_down1, w_q, key_projection_weight, value_projection_weight = tie(
        mix_block, w_gate1, w_up1, w_down1, w_q, key_projection_weight, value_projection_weight
    )
    hidden = w_gate1.shape[1] // seq_count
    ffn_one = jnp.concatenate(
        [
            column_block(w, 1)
            for w in (
                w_gate1, w_up1, w_down1, w_q, key_projection_weight, value_projection_weight
            )
        ]
        + [o_piece],
        1,
    )
    mix_all, ffn_one = dp_gather_small(mix_block, ffn_one)
    ffn_one = dp_gather(ffn_one)
    attn_all = ffn_one[:, 3 * hidden :]
    ffn_two = dp_gather(
        jnp.concatenate([column_block(w, 1) for w in (w_gate2, w_up2, w_down2)], 1)
    )
    qkv_width = attn_all.shape[1] - channels
    qkv_block = attn_all[:, :qkv_width]
    o_block = unpack_rows(attn_all[:, qkv_width:], dp_count)
    bounds = cu_seqlens[0]
    place = seq_place.reshape(1).astype(jnp.int32)
    out_block = unpack_rows(mix_all[:, 3 * channels + 128 :], dp_count)
    small_all = mix_all[:, 3 * channels : 3 * channels + 128].astype(F32).T
    kernel = lax.dynamic_slice_in_dim(small_all[:taps], seq_place * channels, channels, 1)
    gain_mix, gain_ffn_one, gain_attn, gain_ffn_two = (small_all[taps + i] for i in range(4))
    head_gains = small_all[taps + 4 : taps + 6].reshape(2, dp_count, slots)
    head_gains = jnp.tile(head_gains[:, :, : head // dp_count].reshape(2, head), (1, 2))

    x_flat = x_in.reshape(length, width).astype(F32)
    normed_one, projected, gated, near_out, far_out = conv_forward(
        place, bounds, x_blocks, mix_all, out_block, kernel, gain_mix[None, :]
    )
    near_out, late_bounds, *cotangent_blocks = tie(near_out, bounds, *cotangent_blocks)
    order = jnp.arange(full, dtype=jnp.int32)
    starts = doc_starts(late_bounds, order)
    cosine, sine = rope_tables(order - starts, head)
    mixed, cosine, sine = seq_scatter(near_out, far_out, cosine, sine)
    hidden_one = x_flat + mixed
    starts = starts[None, :]

    unit_two, scale_two = unit_scale(hidden_one)
    near_two = (unit_two * gain_ffn_one).astype(BF16)
    far_two = far_half(near_two)
    blocks_two = near_blocks(near_two) + near_blocks(far_two)
    terms_one, partial_one = ffn_forward(blocks_two, ffn_one, hidden)
    mixed, qkv_block, o_block = seq_scatter(*halves_of(partial_one), qkv_block, o_block)
    hidden_two = hidden_one + mixed

    unit_three, scale_three = unit_scale(hidden_two)
    near_three = (unit_three * gain_attn).astype(BF16)
    blocks_three = near_blocks(near_three) + near_blocks(far_half(near_three))
    kv_width = (qkv_width - channels) // 2
    raw, attended_low, wide, totals, near_out, far_out = attention_forward(
        place, blocks_three, qkv_block, o_block, cosine, sine, starts, head_gains
    )
    hidden_three = hidden_two + seq_scatter(near_out, far_out)

    unit_four, scale_four = unit_scale(hidden_three)
    near_four = (unit_four * gain_ffn_two).astype(BF16)
    far_four = far_half(near_four)
    near_four = near_blocks(near_four)
    half = len(near_four)
    kept_two, near_out = ffn_turn(
        near_four, cotangent_blocks[:half], ffn_two, hidden, 0, None
    )
    far_four, near_out = tie(far_four, near_out)
    far_four = near_blocks(far_four)
    kept_two, far_out = ffn_turn(
        far_four, cotangent_blocks[half:], ffn_two, hidden, 1, kept_two
    )

    grad_four = cotangent.reshape(length, width).astype(F32)
    kept_two, far_out = tie(kept_two, far_out)
    normed_four = jnp.concatenate(near_four + far_four, 0)
    d_gate_up = left_dot(normed_four, kept_two[:, : 2 * hidden]).astype(BF16)
    d_ffn_in, d_gate_up = seq_scatter(near_out, far_out, d_gate_up)
    d_hidden, d_gain_ffn_two = norm_back(d_ffn_in, gain_ffn_two, unit_four, scale_four)
    grad_three = grad_four + d_hidden

    grad_attn = grad_three.astype(BF16)
    far_attn = far_half(grad_attn)
    d_down = left_dot(jnp.concatenate(cotangent_blocks, 0), kept_two[:, 2 * hidden :])
    grads_two = jnp.concatenate([d_gate_up, d_down.astype(BF16)], 1)
    far_attn, grads_two = tie(far_attn, grads_two)
    owned_two = dp_scatter(grads_two)
    grad_blocks = near_blocks(grad_attn) + near_blocks(far_attn)
    d_raw, near_out, far_out, d_head_gains = attention_backward(
        place, grad_blocks, qkv_block, o_block, cosine, sine, starts, head_gains,
        raw, wide, totals,
    )
    d_head_gains = d_head_gains[:, :head] + d_head_gains[:, head:]
    d_qkv = left_dot(jnp.concatenate(blocks_three, 0), d_raw)
    d_w_o = left_dot(attended_low, jnp.concatenate(grad_blocks, 0))
    d_w_o = pack_rows(d_w_o.astype(BF16), dp_count)
    d_attn_in, *grads_attn = seq_scatter(near_out, far_out, d_qkv.astype(BF16), d_w_o)
    d_attn_h, d_gain_attn = norm_back(d_attn_in, gain_attn, unit_three, scale_three)
    grad_two = grad_three + d_attn_h

    near_grad = grad_two.astype(BF16)
    far_grad = far_half(near_grad)
    near_grad = near_blocks(near_grad)
    kept_one, near_out = ffn_backward(near_grad, terms_one, ffn_one, hidden, 0, None)
    far_grad, near_out = tie(far_grad, near_out)
    far_grad = near_blocks(far_grad)
    kept_one, far_out = ffn_backward(far_grad, terms_one, ffn_one, hidden, 1, kept_one)
    kept_one, far_out = tie(kept_one, far_out)
    d_gate_up = left_dot(jnp.concatenate(blocks_two, 0), kept_one).astype(BF16)
    d_ffn_in_one, d_gate_up = seq_scatter(near_out, far_out, d_gate_up)
    owned_one = dp_scatter(jnp.concatenate([d_gate_up, *grads_attn], 1))
    d_hidden_one, d_gain_ffn_one = norm_back(d_ffn_in_one, gain_ffn_one, unit_two, scale_two)
    grad_one = grad_two + d_hidden_one

    grad_mix = grad_one.astype(BF16)
    far_mix = far_half(grad_mix)
    d_down = left_dot(
        jnp.concatenate(near_grad + far_grad, 0), terms_one[:, 2 * hidden :]
    ).astype(BF16)
    far_mix, d_down = tie(far_mix, d_down)
    mix_blocks = near_blocks(grad_mix) + near_blocks(far_mix)
    mix_blocks[-1], owned_two = tie(mix_blocks[-1], owned_two)
    d_projected, near_out, far_out, kernel_grads = conv_backward(
        place, bounds, mix_blocks, projected, mix_all, out_block, kernel
    )
    d_w_in = left_dot(normed_one, d_projected)
    d_w_out = left_dot(gated, jnp.concatenate(mix_blocks, 0))
    grads_mix = jnp.concatenate(
        [d_down, d_w_in.astype(BF16), pack_rows(d_w_out.astype(BF16), dp_count)], 1
    )
    kept_mix, sent_mix = dp_pair_parts(grads_mix)
    sent_mix, kept_two = tie(sent_mix, kept_two)
    d_normed = seq_scatter(near_out, far_out)
    unit_one, scale_one = unit_scale(x_flat)
    d_x_part, d_gain_mix = norm_back(d_normed, gain_mix, unit_one, scale_one)
    d_x = (grad_one + d_x_part).reshape(rows, length, width)

    kernel_wide = lax.dynamic_update_slice_in_dim(
        jnp.zeros((taps, width), F32), kernel_grads, seq_place * channels, 1
    )
    head_wide = jnp.pad(
        d_head_gains.reshape(2, dp_count, -1),
        ((0, 0), (0, 0), (0, slots - head // dp_count)),
    ).reshape(2, width)
    vectors = jnp.concatenate(
        [
            jnp.stack([d_gain_mix, d_gain_ffn_one, d_gain_attn, d_gain_ffn_two]),
            kernel_wide,
            head_wide,
        ],
        0,
    )
    vector_columns = jnp.pad(vectors.T, ((0, 0), (0, 128 - vectors.shape[0])))
    owned_vectors = dp_scatter_small(vector_columns.astype(BF16))

    def redeal(block):
        return pack_piece(undeal_rows(unpack_piece(block, width)), channels)

    ffn_out = right_dot(kept_two[:, 2 * hidden :], ffn_two[:, 2 * hidden :])
    hidden_four = hidden_three + seq_scatter(*halves_of(ffn_out))
    out = hidden_four.astype(BF16).reshape(rows, length, width)
    shared_two = share(owned_two)
    owned_mix, (out, d_x, *shared_two), owned_one = dp_scatter_pairs(
        kept_mix, sent_mix, (out, d_x, *shared_two), owned_one
    )
    d_wgate_two, d_wup_two, d_down_two = assemble(
        place, shared_two, [(n * hidden, hidden, 1, False) for n in range(3)]
    )
    tasks = [(n * hidden, hidden, 1, False) for n in range(2)]
    for columns in (channels, kv_width, kv_width):
        tasks.append((tasks[-1][0] + tasks[-1][1], columns, 1, False))
    d_wgate_one, d_wup_one, d_w_q, d_w_k, d_w_v = assemble(
        place, share(owned_one[:, :-channels]), tasks
    )
    (d_w_o_full,) = assemble(
        place, share(redeal(owned_one[:, -channels:])), [(0, channels, 1, True)]
    )
    shared_vectors = share(owned_vectors)
    owned_mix, d_wgate_one, d_w_o_full, d_wgate_two, *shared_vectors = tie(
        owned_mix, d_wgate_one, d_w_o_full, d_wgate_two, *shared_vectors
    )
    shared_mix = share(owned_mix[:, :-channels])
    shared_out = share(redeal(owned_mix[:, -channels:]))
    d_down_one, d_w_in_full = assemble(
        place, shared_mix, [(0, hidden, 1, False), (hidden, 3 * channels, 3, False)]
    )
    (d_w_out_full,) = assemble(place, shared_out, [(0, channels, 1, True)])
    sums = sum(block.astype(F32) for block in shared_vectors).T
    small_head = head // dp_count
    return (
        out,
        d_x,
        d_w_in_full,
        sums[4 : 4 + taps],
        d_w_out_full,
        d_wgate_one,
        d_wup_one,
        d_down_one,
        sums[0],
        sums[1],
        d_w_q,
        d_w_k,
        d_w_v,
        d_w_o_full,
        sums[4 + taps, :small_head],
        sums[5 + taps, :small_head],
        d_wgate_two,
        d_wup_two,
        d_down_two,
        sums[2],
        sums[3],
    )


def solution(mesh):
    matrix = P("dp", None)
    vector = P("dp")
    tokens = P("dp", "seq", None)
    kernel = P(None, "dp")
    in_specs = (
        (tokens, matrix, P("dp", "seq"), tokens, matrix, kernel)
        + (matrix,) * 4
        + (vector,) * 2
        + (matrix,) * 4
        + (vector,) * 2
        + (matrix,) * 3
        + (vector,) * 2
    )
    out_specs = (
        (tokens, tokens, matrix, kernel)
        + (matrix,) * 4
        + (vector,) * 2
        + (matrix,) * 4
        + (vector,) * 2
        + (matrix,) * 3
        + (vector,) * 2
    )
    return jax.shard_map(local, mesh=mesh, in_specs=in_specs, out_specs=out_specs, check_vma=False)
```

```python
import jax
import jax.numpy as jnp
from jax import lax
from jax.experimental import pallas as pl
from jax.experimental.pallas import tpu as pltpu
from jax.sharding import PartitionSpec as P

EPS = 1e-05
THETA = 1000000.0
NEG = -1e30
F32 = jnp.float32
BF16 = jnp.bfloat16
TILE = 256
LANES = 128
VMEM_LIMIT = 48 << 20


def left_dot(left, right):
    return lax.dot_general(left, right, (((0,), (0,)), ((), ())), preferred_element_type=F32)


def right_dot(left, right):
    return lax.dot_general(left, right, (((1,), (1,)), ((), ())), preferred_element_type=F32)


def plain_dot(left, right):
    return jnp.dot(left, right, preferred_element_type=F32)


def unit_scale(value):
    scale = lax.rsqrt(jnp.mean(value * value, -1, keepdims=True) + EPS)
    return (value * scale, scale)


def norm_back(grad_out, gain, unit, scale):
    weighted = grad_out * gain
    grad_in = scale * (weighted - unit * jnp.mean(weighted * unit, -1, keepdims=True))
    gain_grad = jnp.sum((grad_out * unit).reshape(-1, unit.shape[-1]), 0)
    return (grad_in, gain_grad)


def doc_starts(bounds, places):
    return jnp.max(jnp.where(bounds <= places[..., None], bounds, 0), -1)


def rope_tables(places, head):
    half = head // 2
    freqs = THETA ** (-(2.0 * jnp.arange(half, dtype=F32)) / head)
    angles = places.astype(F32)[:, None] * freqs
    cosine = jnp.cos(angles)
    sine = jnp.sin(angles)
    return (
        jnp.concatenate([cosine] * 4, 1),
        jnp.concatenate([-sine, sine, -sine, sine], 1),
    )


def seq_bits():
    size = lax.axis_size("seq")
    bits = []
    bit = 1
    while bit < size:
        bits.append(bit)
        bit = bit * 2
    return bits


def swap_seq(array, bit):
    size = lax.axis_size("seq")
    return lax.ppermute(array, "seq", [(i, i ^ bit) for i in range(size)])


def tie(*values):
    return lax.optimization_barrier(values)


def near_blocks(block):
    have = {0: block}
    for bit in reversed(seq_bits()[:-1]):
        for place in sorted(have):
            have[place | bit] = swap_seq(have[place], bit)
    return [have[place] for place in sorted(have)]


def far_half(block):
    return swap_seq(block, seq_bits()[-1])


def near_sum(half):
    size = lax.axis_size("seq") // 2
    length = half.shape[0] // size
    have = {place: half[place * length : (place + 1) * length] for place in range(size)}
    for bit in seq_bits()[:-1]:
        for place in sorted(have, reverse=True):
            if place & bit:
                got = swap_seq(have.pop(place).astype(BF16), bit).astype(F32)
                have[place ^ bit] = have[place ^ bit].astype(F32) + got
    return have[0].astype(F32)


def seq_scatter(near, far, *work):
    sent = far_half(near_sum(far).astype(BF16))
    kept = near_sum(near)
    sent, kept, *work = tie(sent, kept, *work)
    total = kept + sent.astype(F32)
    return (total, *work) if work else total


def half_lanes(shape):
    return lax.broadcasted_iota(jnp.int32, shape, 1) < LANES // 2


def head_mean(value):
    row = lax.broadcasted_iota(jnp.int32, (LANES, LANES), 0) < LANES // 2
    column = half_lanes((LANES, LANES))
    ones = jnp.where(row == column, 2.0 / LANES, 0.0).astype(BF16)
    high = value.astype(BF16)
    low = (value - high.astype(F32)).astype(BF16)
    return plain_dot(high, ones) + plain_dot(low, ones)


def swap_quarters(value):
    quarter = LANES // 4
    lane = lax.broadcasted_iota(jnp.int32, value.shape, 1)
    first = (lane // quarter) % 2 == 0
    return jnp.where(
        first, pltpu.roll(value, LANES - quarter, 1), pltpu.roll(value, quarter, 1)
    )


def head_unit(value):
    scale = lax.rsqrt(head_mean(value * value) + EPS)
    return (value * scale, scale)


def pad_pair(value, second):
    lower = half_lanes(value.shape)
    if second:
        high = jnp.where(lower, 0.0, value)
        return (pltpu.roll(high, LANES // 2, 1), high)
    low = jnp.where(lower, value, 0.0)
    return (low, pltpu.roll(low, LANES // 2, 1))


def load_heads(raw_ref, cos_ref, sin_ref, gains_ref, rows, target, length, pairs):
    cosine = cos_ref[pl.ds(target, length), :]
    sine = sin_ref[pl.ds(target, length), :]
    groups = raw_ref.shape[1] // LANES

    def turned(group, gain):
        value = head_unit(raw_ref[rows, group * LANES : (group + 1) * LANES])[0] * gain
        return value * cosine + swap_quarters(value) * sine

    scale = (LANES // 2) ** (-0.5)
    queries = [(turned(g, gains_ref[0:1, :]) * scale).astype(BF16) for g in range(pairs)]
    keys = []
    values = []
    cached = {}
    for g in range(pairs):
        place = pairs * LANES + g * (LANES // 2)
        group, second = divmod(place, LANES)
        if group not in cached:
            cached[group] = turned(group, gains_ref[1:2, :]).astype(BF16).astype(F32)
        keys.append([k.astype(BF16) for k in pad_pair(cached[group], second > 0)])
        place = place + pairs * (LANES // 2)
        group, second = divmod(place, LANES)
        value = raw_ref[rows, group * LANES : (group + 1) * LANES]
        values.append([v.astype(BF16) for v in pad_pair(value, second > 0)])
    return (queries, keys, values)


def allowed_tile(start_ref, first_key, first_query):
    query = first_query + lax.broadcasted_iota(jnp.int32, (1, TILE), 1)
    start = start_ref[0:1, pl.ds(first_query, TILE)]
    key = first_key + lax.broadcasted_iota(jnp.int32, (TILE, TILE), 0)
    return (key >= start) & (key <= query)


def block_rows(block, count, length):
    half, offset = divmod(block, count // 2)
    return (half, slice(offset * length, (offset + 1) * length))


def attention_forward_kernel(place_ref, *refs, length, pairs, tokens):
    token_refs = refs[:tokens]
    (
        qkv_ref, o_ref, cos_ref, sin_ref, start_ref, gains_ref,
        raw_ref, out_ref, wide_ref, total_ref, near_out_ref, far_out_ref,
        query_ref, key_ref, value_ref,
    ) = refs[tokens:]
    full = raw_ref.shape[0]
    count = full // length
    place = place_ref[0]

    for block in range(count):
        target = pl.multiple_of((block ^ place) * length, 8)
        source = slice(block * length, (block + 1) * length)
        raw_ref[source, :] = plain_dot(token_refs[block][...], qkv_ref[...])
        queries, keys, values = load_heads(
            raw_ref, cos_ref, sin_ref, gains_ref, source, target, length, pairs
        )
        for g in range(pairs):
            query_ref[g, pl.ds(target, length), :] = queries[g]
            for h in range(2):
                key_ref[2 * g + h, pl.ds(target, length), :] = keys[g][h]
                value_ref[2 * g + h, pl.ds(target, length), :] = values[g][h]

    half = LANES // 2

    def query_tile(i, _):
        first_query = pl.multiple_of(i * TILE, TILE)

        def key_tile(j, carry):
            first_key = pl.multiple_of(j * TILE, TILE)
            allowed = allowed_tile(start_ref, first_key, first_query)
            sums, outs = carry
            new_sums = []
            new_outs = []
            for g in range(pairs):
                query = query_ref[g, pl.ds(first_query, TILE), :]
                total = outs[g]
                for h in range(2):
                    key = key_ref[2 * g + h, pl.ds(first_key, TILE), :]
                    value = value_ref[2 * g + h, pl.ds(first_key, TILE), :]
                    weight = jnp.where(allowed, jnp.exp(right_dot(key, query)), 0.0)
                    new_sums.append(sums[2 * g + h] + jnp.sum(weight, 0, keepdims=True))
                    total = total + lax.dot_general(
                        value, weight.astype(BF16), (((0,), (0,)), ((), ())),
                        preferred_element_type=F32,
                    )
                new_outs.append(total)
            return (new_sums, new_outs)

        carry = (
            [jnp.zeros((1, TILE), F32) for _ in range(2 * pairs)],
            [jnp.zeros((LANES, TILE), F32) for _ in range(pairs)],
        )
        sums, outs = lax.fori_loop(0, i + 1, key_tile, carry)
        columns = pl.ds(first_query, TILE)
        for g in range(pairs):
            scaled = jnp.concatenate(
                [outs[g][h * half : (h + 1) * half] / sums[2 * g + h] for h in range(2)], 0
            )
            for h in range(2):
                total_ref[2 * g + h : 2 * g + h + 1, columns] = sums[2 * g + h]
            wide_ref[g * LANES : (g + 1) * LANES, columns] = scaled
            query_ref[g, columns, :] = scaled.T.astype(BF16)
        return 0

    lax.fori_loop(0, full // TILE, query_tile, 0)

    for block in range(count):
        side, rows = block_rows(block, count, length)
        source = pl.multiple_of((block ^ place) * length, 8)
        target = slice(block * length, (block + 1) * length)
        for g in range(pairs):
            out_ref[target, g * LANES : (g + 1) * LANES] = query_ref[
                g, pl.ds(source, length), :
            ]
        partial = plain_dot(out_ref[target, :], o_ref[...])
        (near_out_ref, far_out_ref)[side][rows, :] = partial.astype(BF16)


def attention_backward_kernel(place_ref, *refs, length, pairs, tokens):
    token_refs = refs[:tokens]
    (
        qkv_ref, o_ref, cos_ref, sin_ref, start_ref, gains_ref, raw_ref, wide_ref, total_ref,
        out_ref, near_out_ref, far_out_ref, gain_grad_ref,
        query_ref, key_ref, value_ref, hold_ref, dq_ref, dk_ref, dv_ref,
    ) = refs[tokens:]
    full = raw_ref.shape[0]
    count = full // length
    place = place_ref[0]
    half = LANES // 2

    for block in range(count):
        target = pl.multiple_of((block ^ place) * length, 8)
        source = slice(block * length, (block + 1) * length)
        grads = right_dot(token_refs[block][...], o_ref[...]).astype(BF16)
        queries, keys, values = load_heads(
            raw_ref, cos_ref, sin_ref, gains_ref, source, target, length, pairs
        )
        rows = pl.ds(target, length)
        for g in range(pairs):
            query_ref[g, rows, :] = queries[g]
            hold_ref[g, rows, :] = grads[:, g * LANES : (g + 1) * LANES]
            dk_ref[g, rows, :] = jnp.zeros((length, LANES), F32)
            dv_ref[g, rows, :] = jnp.zeros((length, LANES), F32)
            for h in range(2):
                key_ref[2 * g + h, rows, :] = keys[g][h]
                value_ref[2 * g + h, rows, :] = values[g][h]

    lower = half_lanes((TILE, LANES))

    def query_tile(i, _):
        first_query = pl.multiple_of(i * TILE, TILE)
        columns = pl.ds(first_query, TILE)
        inverse = [1.0 / total_ref[n : n + 1, columns] for n in range(2 * pairs)]
        inner = []
        for g in range(pairs):
            grad = hold_ref[g, columns, :].astype(F32).T
            both = grad * wide_ref[g * LANES : (g + 1) * LANES, columns]
            for h in range(2):
                inner.append(jnp.sum(both[h * half : (h + 1) * half], 0, keepdims=True))

        def key_tile(j, outs):
            first_key = pl.multiple_of(j * TILE, TILE)
            rows = pl.ds(first_key, TILE)
            allowed = allowed_tile(start_ref, first_key, first_query)
            new_outs = []
            for g in range(pairs):
                query = query_ref[g, columns, :]
                grad = hold_ref[g, columns, :]
                zero = jnp.zeros_like(query)
                total = outs[g]
                d_key = dk_ref[g, rows, :]
                d_value = dv_ref[g, rows, :]
                for h in range(2):
                    keep = lower if h == 0 else jnp.logical_not(lower)
                    key = key_ref[2 * g + h, rows, :]
                    value = value_ref[2 * g + h, rows, :]
                    weight = jnp.exp(right_dot(key, query)) * inverse[2 * g + h]
                    weight = jnp.where(allowed, weight, 0.0)
                    d_weight = right_dot(value, grad)
                    d_score = (weight * (d_weight - inner[2 * g + h])).astype(BF16)
                    d_value = d_value + plain_dot(
                        weight.astype(BF16), jnp.where(keep, grad, zero)
                    )
                    d_key = d_key + plain_dot(d_score, jnp.where(keep, query, zero))
                    total = total + lax.dot_general(
                        key, d_score, (((0,), (0,)), ((), ())), preferred_element_type=F32
                    )
                dk_ref[g, rows, :] = d_key
                dv_ref[g, rows, :] = d_value
                new_outs.append(total)
            return new_outs

        outs = lax.fori_loop(
            0, i + 1, key_tile, [jnp.zeros((LANES, TILE), F32) for _ in range(pairs)]
        )
        for g in range(pairs):
            dq_ref[g, columns, :] = outs[g].T
        return 0

    lax.fori_loop(0, full // TILE, query_tile, 0)
    scale = half ** (-0.5)

    low = half_lanes((length, LANES))
    query_gain = jnp.zeros((1, LANES), F32)
    key_gain = jnp.zeros((1, LANES), F32)
    for block in range(count):
        side, side_rows = block_rows(block, count, length)
        rows = pl.ds(pl.multiple_of((block ^ place) * length, 8), length)
        target = slice(block * length, (block + 1) * length)
        cosine = cos_ref[rows, :]
        sine = sin_ref[rows, :]

        def back(grad, group, gain):
            grad = grad.astype(BF16).astype(F32)
            unit, inverse = head_unit(raw_ref[target, group * LANES : (group + 1) * LANES])
            d_rot = grad * cosine + swap_quarters(grad * sine)
            weighted = d_rot * gain
            d_raw = inverse * (weighted - unit * head_mean(weighted * unit))
            return (d_raw, d_rot * unit)

        for g in range(pairs):
            d_raw, terms = back(dq_ref[g, rows, :] * scale, g, gains_ref[0:1, :])
            query_gain = query_gain + jnp.sum(terms, 0, keepdims=True)
            out_ref[target, g * LANES : (g + 1) * LANES] = d_raw.astype(BF16)
        groups = {}
        for kind, held in ((0, dk_ref), (1, dv_ref)):
            for g in range(pairs):
                place_of = pairs * LANES + kind * pairs * half + g * half
                group, second = divmod(place_of, LANES)
                value = held[g, rows, :]
                value = value + pltpu.roll(value, half, 1)
                groups.setdefault(group, {})[second // half] = (kind, value)
        for group, parts in groups.items():
            merged = jnp.where(low, parts[0][1], parts[1][1])
            is_key = [parts[n][0] == 0 for n in range(2)]
            result = merged
            if any(is_key):
                d_raw, terms = back(merged, group, gains_ref[1:2, :])
                if not is_key[1]:
                    d_raw = jnp.where(low, d_raw, merged)
                    terms = jnp.where(low, terms, 0.0)
                result = d_raw
                key_gain = key_gain + jnp.sum(terms, 0, keepdims=True)
            out_ref[target, group * LANES : (group + 1) * LANES] = result.astype(BF16)
        partial = right_dot(out_ref[target, :], qkv_ref[...])
        (near_out_ref, far_out_ref)[side][side_rows, :] = partial.astype(BF16)
    gain_grad_ref[0:1, :] = query_gain
    gain_grad_ref[1:2, :] = key_gain


def whole(count):
    return [pl.BlockSpec(memory_space=pltpu.VMEM)] * count


def attention_forward(place, tokens, qkv, o, cosine, sine, start, gains):
    length = tokens[0].shape[0]
    full = len(tokens) * length
    width, columns = qkv.shape
    pairs = columns // (2 * LANES)
    return pl.pallas_call(
        lambda *refs: attention_forward_kernel(
            *refs, length=length, pairs=pairs, tokens=len(tokens)
        ),
        in_specs=[pl.BlockSpec(memory_space=pltpu.SMEM)] + whole(6 + len(tokens)),
        out_specs=tuple(whole(6)),
        out_shape=(
            jax.ShapeDtypeStruct((full, columns), F32),
            jax.ShapeDtypeStruct((full, pairs * LANES), BF16),
            jax.ShapeDtypeStruct((pairs * LANES, full), F32),
            jax.ShapeDtypeStruct((8, full), F32),
            jax.ShapeDtypeStruct((full // 2, width), BF16),
            jax.ShapeDtypeStruct((full // 2, width), BF16),
        ),
        scratch_shapes=[
            pltpu.VMEM((pairs, full, LANES), BF16),
            pltpu.VMEM((2 * pairs, full, LANES), BF16),
            pltpu.VMEM((2 * pairs, full, LANES), BF16),
        ],
        cost_estimate=pl.CostEstimate(
            flops=20_000_000_000, transcendentals=6_000_000, bytes_accessed=20_000_000
        ),
        compiler_params=pltpu.CompilerParams(vmem_limit_bytes=VMEM_LIMIT),
        name="attention_forward",
    )(place, *tokens, qkv, o, cosine, sine, start, gains)


def attention_backward(place, tokens, qkv, o, cosine, sine, start, gains, raw, wide, totals):
    length = tokens[0].shape[0]
    full = len(tokens) * length
    width, columns = qkv.shape
    pairs = columns // (2 * LANES)
    return pl.pallas_call(
        lambda *refs: attention_backward_kernel(
            *refs, length=length, pairs=pairs, tokens=len(tokens)
        ),
        in_specs=[pl.BlockSpec(memory_space=pltpu.SMEM)] + whole(9 + len(tokens)),
        out_specs=tuple(whole(4)),
        out_shape=(
            jax.ShapeDtypeStruct((full, columns), BF16),
            jax.ShapeDtypeStruct((full // 2, width), BF16),
            jax.ShapeDtypeStruct((full // 2, width), BF16),
            jax.ShapeDtypeStruct((2, LANES), F32),
        ),
        scratch_shapes=[
            pltpu.VMEM((pairs, full, LANES), BF16),
            pltpu.VMEM((2 * pairs, full, LANES), BF16),
            pltpu.VMEM((2 * pairs, full, LANES), BF16),
            pltpu.VMEM((pairs, full, LANES), BF16),
            pltpu.VMEM((pairs, full, LANES), F32),
            pltpu.VMEM((pairs, full, LANES), F32),
            pltpu.VMEM((pairs, full, LANES), F32),
        ],
        cost_estimate=pl.CostEstimate(
            flops=20_000_000_000, transcendentals=6_000_000, bytes_accessed=20_000_000
        ),
        compiler_params=pltpu.CompilerParams(vmem_limit_bytes=VMEM_LIMIT),
        name="attention_backward",
    )(place, *tokens, qkv, o, cosine, sine, start, gains, raw, wide, totals)


def column_block(weight, parts):
    size = lax.axis_size("seq")
    place = lax.axis_index("seq")
    rows, columns = weight.shape
    block = columns // parts // size
    split = weight.reshape(rows, parts, size * block)
    return lax.dynamic_slice_in_dim(split, place * block, block, 2).reshape(rows, parts * block)


def deal_pairs():
    size = lax.axis_size("seq")
    count = lax.axis_size("dp")
    pairs = []
    for place in range(size):
        for owner in range(count):
            source = (owner % size) * count + place * (count // size) + owner // size
            pairs.append((source, place * count + owner))
    return pairs


def deal_rows(*weights):
    size = lax.axis_size("seq")
    place = lax.axis_index("seq")
    piece = weights[0].shape[0] // size
    parts = [lax.dynamic_slice_in_dim(w, place * piece, piece, 0) for w in weights]
    dealt = lax.ppermute(jnp.concatenate(parts, 0), ("seq", "dp"), deal_pairs())
    return [dealt[n * piece : (n + 1) * piece] for n in range(len(weights))]


def pack_piece(piece, columns):
    count = piece.shape[1] // columns
    return jnp.concatenate(
        [piece[:, n * columns : (n + 1) * columns] for n in range(count)], 0
    )


def unpack_piece(block, width):
    count = width // block.shape[1]
    rows = block.shape[0] // count
    return jnp.concatenate([block[n * rows : (n + 1) * rows] for n in range(count)], 1)


def pack_rows(rows_block, parts):
    rows, width = rows_block.shape
    piece = rows // parts
    split = rows_block.reshape(parts, piece, width // rows, rows)
    return jnp.swapaxes(split, 1, 2).reshape(width, rows)


def unpack_rows(block, parts):
    width, rows = block.shape
    split = block.reshape(parts, width // rows, rows // parts, rows)
    return jnp.swapaxes(split, 1, 2).reshape(rows, width)


def undeal_rows(part):
    return lax.ppermute(part, ("seq", "dp"), [(b, a) for a, b in deal_pairs()])


def dp_gather(block):
    return lax.all_gather(block, "dp", axis=0, tiled=True)


def dp_scatter(grads):
    return lax.psum_scatter(grads, "dp", scatter_dimension=0, tiled=True)


def swap_dp(array, bit):
    size = lax.axis_size("dp")
    return lax.ppermute(array, "dp", [(i, i ^ bit) for i in range(size)])


def dp_bits():
    return [1, 2, 4] if lax.axis_size("dp") == 8 else []


def dp_gather_small(block, later):
    if not dp_bits():
        return (dp_gather(block), later)
    size = lax.axis_size("dp")
    place = lax.axis_index("dp")
    rows = block.shape[0]
    near, middle, far = dp_bits()
    have = {0: block, far: swap_dp(block, far), middle: swap_dp(block, middle)}
    have[near] = swap_dp(block, near)
    have[far], later = tie(have[far], later)
    have[far | middle] = swap_dp(have[far], middle)
    for turn in (middle, far, far | middle):
        have[turn | near] = swap_dp(have[turn], near)
    result = jnp.zeros((size * rows, block.shape[1]), block.dtype)
    for turn in range(size):
        result = lax.dynamic_update_slice_in_dim(result, have[turn], (place ^ turn) * rows, 0)
    return (result, later)


def dp_scatter_small(grads):
    if not dp_bits():
        return dp_scatter(grads)
    size = lax.axis_size("dp")
    place = lax.axis_index("dp")
    sums = grads.reshape(size, -1, grads.shape[1]).astype(F32)
    for bit in dp_bits():
        split = sums.reshape(-1, 2, *sums.shape[1:])
        side = (place // bit) % 2
        kept = lax.dynamic_index_in_dim(split, side, 1, False)
        sent = lax.dynamic_index_in_dim(split, 1 - side, 1, False).astype(BF16)
        sums = kept + swap_dp(sent, bit).astype(F32)
    return sums[0].astype(BF16)


def dp_pair_parts(grads):
    if not dp_bits():
        return (grads, grads[:8])
    size = lax.axis_size("dp")
    side = lax.axis_index("dp") % 2
    columns = grads.shape[1]
    blocks = grads.reshape(size // 2, 2, -1, columns)
    kept = lax.dynamic_index_in_dim(blocks, side, 1, False).reshape(-1, columns)
    sent = lax.dynamic_index_in_dim(blocks, 1 - side, 1, False).reshape(-1, columns)
    return (kept, sent)


def dp_scatter_pairs(kept, sent, work, later):
    if not dp_bits():
        kept, later, *work = tie(kept, later, *work)
        return (dp_scatter(kept), work, later)
    size = lax.axis_size("dp")
    got, *work = tie(swap_dp(sent, 1), *work)
    sums = (kept.astype(F32) + got.astype(F32)).astype(BF16)
    sums, later = tie(sums, later)
    groups = [list(range(n, size, 2)) for n in range(2)]
    owned = lax.psum_scatter(
        sums, "dp", scatter_dimension=0, tiled=True, axis_index_groups=groups
    )
    return (owned, work, later)


def share(owned):
    return near_blocks(owned) + near_blocks(far_half(owned))


def assemble_kernel(place_ref, *refs, count, tasks):
    blocks = refs[:count]
    outs = refs[count:]
    place = place_ref[0]
    for turn in range(count):
        for target in range(count):

            @pl.when((place ^ turn) == target)
            def _():
                for (start, columns, split, by_rows), out_ref in zip(tasks, outs):
                    if by_rows:
                        rows = blocks[turn].shape[0] // count
                        for part in range(count):
                            out_ref[
                                target * rows : (target + 1) * rows,
                                part * columns : (part + 1) * columns,
                            ] = blocks[turn][
                                part * rows : (part + 1) * rows, start : start + columns
                            ].astype(F32)
                    else:
                        step = columns // split
                        for part in range(split):
                            first = (part * count + target) * step
                            out_ref[:, first : first + step] = blocks[turn][
                                :, start + part * step : start + (part + 1) * step
                            ].astype(F32)


def assemble(place, blocks, tasks):
    count = len(blocks)
    rows = blocks[0].shape[0]
    if all(columns // split % LANES == 0 for _, columns, split, _ in tasks):
        return pl.pallas_call(
            lambda *refs: assemble_kernel(*refs, count=count, tasks=tasks),
            in_specs=[pl.BlockSpec(memory_space=pltpu.SMEM)] + whole(count),
            out_specs=tuple(whole(len(tasks))),
            out_shape=tuple(
                jax.ShapeDtypeStruct((rows, count * columns), F32) for _, columns, _, _ in tasks
            ),
            compiler_params=pltpu.CompilerParams(vmem_limit_bytes=VMEM_LIMIT),
            name="assemble",
        )(place, *blocks)
    stacked = jnp.stack(blocks, 0)
    ordered = [
        lax.dynamic_index_in_dim(stacked, place[0] ^ i, 0, False) for i in range(count)
    ]
    results = []
    for start, columns, split, by_rows in tasks:
        parts = [block[:, start : start + columns] for block in ordered]
        if by_rows:
            joined = jnp.concatenate([unpack_piece(p, count * columns) for p in parts], 0)
        else:
            step = columns // split
            joined = jnp.concatenate(
                [p[:, n * step : (n + 1) * step] for n in range(split) for p in parts], 1
            )
        results.append(joined.astype(F32))
    return results


def gate_terms(normed, w_gate, w_up):
    gate = plain_dot(normed, w_gate)
    upper = plain_dot(normed, w_up)
    sigma = jax.nn.sigmoid(gate)
    swish = gate * sigma
    return (upper * (sigma + swish * (1.0 - sigma)), swish, swish * upper)


def block_here(refs):
    value = refs[0][...]
    for number, ref in enumerate(refs[1:]):
        value = jnp.where(pl.program_id(0) == number + 1, ref[...], value)
    return value


def ffn_forward_kernel(*refs, count):
    normed_refs = refs[:count]
    gate_ref, up_ref, down_ref = refs[count : count + 3]
    kept_ref, partial_ref = refs[-2:]
    hidden = gate_ref.shape[1]
    slope, swish, act = gate_terms(block_here(normed_refs), gate_ref[...], up_ref[...])
    act = act.astype(BF16)
    kept_ref[:, :hidden] = slope.astype(BF16)
    kept_ref[:, hidden : 2 * hidden] = swish.astype(BF16)
    kept_ref[:, 2 * hidden :] = act
    partial_ref[...] = right_dot(act, down_ref[...]).astype(BF16)


def ffn_turn_kernel(*refs, count):
    normed_refs = refs[:count]
    grad_refs = refs[count : 2 * count]
    gate_ref, up_ref, down_ref = refs[2 * count : 2 * count + 3]
    kept_ref, partial_ref = refs[-2:]
    hidden = gate_ref.shape[1]
    slope, swish, act = gate_terms(block_here(normed_refs), gate_ref[...], up_ref[...])
    d_act = plain_dot(block_here(grad_refs), down_ref[...])
    d_gate = (d_act * slope).astype(BF16)
    d_up = (d_act * swish).astype(BF16)
    kept_ref[:, :hidden] = d_gate
    kept_ref[:, hidden : 2 * hidden] = d_up
    kept_ref[:, 2 * hidden :] = act.astype(BF16)
    partial = right_dot(d_gate, gate_ref[...]) + right_dot(d_up, up_ref[...])
    partial_ref[...] = partial.astype(BF16)


def ffn_backward_kernel(*refs, count):
    grad_refs = refs[:count]
    terms_ref, gate_ref, up_ref, down_ref = refs[count : count + 4]
    kept_ref, partial_ref = refs[-2:]
    hidden = gate_ref.shape[1]
    d_act = plain_dot(block_here(grad_refs), down_ref[...])
    d_gate = (d_act * terms_ref[:, :hidden].astype(F32)).astype(BF16)
    d_up = (d_act * terms_ref[:, hidden:].astype(F32)).astype(BF16)
    kept_ref[:, :hidden] = d_gate
    kept_ref[:, hidden:] = d_up
    partial = right_dot(d_gate, gate_ref[...]) + right_dot(d_up, up_ref[...])
    partial_ref[...] = partial.astype(BF16)


def ffn_call(kernel, name, tokens, terms, weights, hidden, first, full, kept_width, kept):
    width = weights.shape[0]
    count = len(tokens[0])
    length = tokens[0][0].shape[0]
    operands = [block for blocks in tokens for block in blocks]
    in_specs = [
        pl.BlockSpec((length, width), lambda i: (0, 0), pipeline_mode=pl.Buffered(1))
        for _ in operands
    ]
    if terms is not None:
        in_specs.append(pl.BlockSpec((length, 2 * hidden), lambda i: (i + first, 0)))
        operands.append(terms)
    for place in range(3):
        in_specs.append(
            pl.BlockSpec(
                (width, hidden), lambda i, place=place: (0, place), pipeline_mode=pl.Buffered(1)
            )
        )
        operands.append(weights)
    aliases = {}
    if kept is not None:
        aliases = {len(operands): 0}
        in_specs.append(pl.BlockSpec(memory_space=pl.ANY))
        operands.append(kept)
    return pl.pallas_call(
        lambda *refs: kernel(*refs, count=count),
        grid=(count,),
        in_specs=in_specs,
        out_specs=(
            pl.BlockSpec((length, kept_width), lambda i: (i + first, 0)),
            pl.BlockSpec((length, width), lambda i: (i, 0)),
        ),
        out_shape=(
            jax.ShapeDtypeStruct((full, kept_width), BF16),
            jax.ShapeDtypeStruct((count * length, width), BF16),
        ),
        input_output_aliases=aliases,
        cost_estimate=pl.CostEstimate(
            flops=6_000_000_000, transcendentals=1_000_000, bytes_accessed=20_000_000
        ),
        compiler_params=pltpu.CompilerParams(vmem_limit_bytes=VMEM_LIMIT),
        name=name,
    )(*operands)


def split_weights(weights, hidden):
    return [weights[:, n * hidden : (n + 1) * hidden] for n in range(3)]


def halves_of(array):
    half = array.shape[0] // 2
    return (array[:half], array[half:])


def place_rows(kept, part, number):
    if kept is None:
        kept = jnp.zeros((2 * part.shape[0], part.shape[1]), part.dtype)
    return lax.dynamic_update_slice_in_dim(kept, part, number * part.shape[0], 0)


def ffn_forward(normed, weights, hidden):
    if hidden % LANES:
        w_gate, w_up, w_down = split_weights(weights, hidden)
        terms = gate_terms(jnp.concatenate(normed, 0), w_gate, w_up)
        terms = jnp.concatenate(terms, 1).astype(BF16)
        return (terms, right_dot(terms[:, 2 * hidden :], w_down).astype(BF16))
    return ffn_call(
        ffn_forward_kernel, "ffn_forward", [normed], None, weights, hidden,
        0, len(normed) * normed[0].shape[0], 3 * hidden, None,
    )


def ffn_turn(normed, grads, weights, hidden, number, kept):
    if hidden % LANES:
        w_gate, w_up, w_down = split_weights(weights, hidden)
        slope, swish, act = gate_terms(jnp.concatenate(normed, 0), w_gate, w_up)
        d_act = plain_dot(jnp.concatenate(grads, 0), w_down)
        part = jnp.concatenate([d_act * slope, d_act * swish, act], 1).astype(BF16)
        partial = right_dot(part[:, : 2 * hidden], weights[:, : 2 * hidden]).astype(BF16)
        return (place_rows(kept, part, number), partial)
    count = len(normed)
    return ffn_call(
        ffn_turn_kernel, "ffn_turn", [normed, grads], None, weights, hidden,
        number * count, 2 * count * normed[0].shape[0], 3 * hidden, kept,
    )


def ffn_backward(grads, terms, weights, hidden, number, kept):
    count = len(grads)
    length = grads[0].shape[0]
    if hidden % LANES:
        w_gate, w_up, w_down = split_weights(weights, hidden)
        rows = slice(number * count * length, (number + 1) * count * length)
        d_act = plain_dot(jnp.concatenate(grads, 0), w_down)
        slope = terms[rows, :hidden].astype(F32)
        swish = terms[rows, hidden : 2 * hidden].astype(F32)
        part = jnp.concatenate([d_act * slope, d_act * swish], 1).astype(BF16)
        partial = right_dot(part, weights[:, : 2 * hidden]).astype(BF16)
        return (place_rows(kept, part, number), partial)
    return ffn_call(
        ffn_backward_kernel, "ffn_backward", [grads], terms, weights, hidden,
        number * count, 2 * count * length, 2 * hidden, kept,
    )


def row_starts(bounds_ref, token):
    start = jnp.zeros(token.shape, jnp.int32)
    for number in range(1, bounds_ref.shape[0]):
        bound = bounds_ref[number]
        start = jnp.where(bound <= token, jnp.maximum(start, bound), start)
    return start


def conv_backward_kernel(*refs, length, tokens, taps):
    place_ref, bounds_ref = refs[:2]
    grad_refs = refs[2 : 2 + tokens]
    (
        projected_ref, in_ref, out_w_ref, tap_ref,
        d_projected_ref, near_out_ref, far_out_ref, tap_grad_ref,
        product_ref, d_gated_ref, d_conv_ref,
    ) = refs[2 + tokens :]
    place = place_ref[0]
    channels = out_w_ref.shape[0]
    full = tokens * length
    product_ref[0:8, :] = jnp.zeros((8, channels), F32)
    d_conv_ref[full : full + 8, :] = jnp.zeros((8, channels), F32)
    for block in range(tokens):
        rows = slice(block * length, (block + 1) * length)
        first = pl.multiple_of((block ^ place) * length, 8)
        d_gated_ref[rows, :] = right_dot(grad_refs[block][...], out_w_ref[...])
        product = projected_ref[rows, :channels] * projected_ref[rows, 2 * channels :]
        product_ref[pl.ds(pl.multiple_of(8 + first, 8), length), :] = product.astype(BF16).astype(F32)
    tap_grads = [jnp.zeros((1, channels), F32) for _ in range(taps)]
    for block in range(tokens):
        rows = slice(block * length, (block + 1) * length)
        first = pl.multiple_of((block ^ place) * length, 8)
        window = product_ref[pl.ds(first, length + 8), :]
        token = first + lax.broadcasted_iota(jnp.int32, (length, channels), 0)
        start = row_starts(bounds_ref, token)
        d_gated = d_gated_ref[rows, :]
        d_conv = d_gated * projected_ref[rows, channels : 2 * channels]
        conv = jnp.zeros((length, channels), F32)
        for tap in range(taps):
            moved = window[8 - tap : 8 - tap + length, :]
            moved = jnp.where(token - tap >= start, moved, 0.0)
            conv = conv + tap_ref[tap : tap + 1, :] * moved
            tap_grads[tap] = tap_grads[tap] + jnp.sum(d_conv * moved, 0, keepdims=True)
        d_projected_ref[rows, channels : 2 * channels] = (d_gated * conv).astype(BF16)
        d_conv_ref[pl.ds(first, length), :] = d_conv
    for tap in range(taps):
        tap_grad_ref[tap : tap + 1, :] = tap_grads[tap]
    for block in range(tokens):
        side, side_rows = block_rows(block, tokens, length)
        rows = slice(block * length, (block + 1) * length)
        first = pl.multiple_of((block ^ place) * length, 8)
        window = d_conv_ref[pl.ds(first, length + 8), :]
        token = first + lax.broadcasted_iota(jnp.int32, (length, channels), 0)
        total = tap_ref[0:1, :] * window[:length, :]
        for tap in range(1, taps):
            same = token >= row_starts(bounds_ref, token + tap)
            total = total + tap_ref[tap : tap + 1, :] * jnp.where(
                same, window[tap : tap + length, :], 0.0
            )
        d_product = total.astype(BF16).astype(F32)
        d_projected_ref[rows, :channels] = (
            d_product * projected_ref[rows, 2 * channels :]
        ).astype(BF16)
        d_projected_ref[rows, 2 * channels :] = (
            d_product * projected_ref[rows, :channels]
        ).astype(BF16)
        partial = right_dot(d_projected_ref[rows, :], in_ref[:, : 3 * channels])
        (near_out_ref, far_out_ref)[side][side_rows, :] = partial.astype(BF16)


def conv_backward(place, bounds, grads, projected, in_weights, out_weights, kernel):
    length, width = grads[0].shape
    full = len(grads) * length
    channels = out_weights.shape[0]
    taps = kernel.shape[0]
    scalar = pl.BlockSpec(memory_space=pltpu.SMEM)
    return pl.pallas_call(
        lambda *refs: conv_backward_kernel(*refs, length=length, tokens=len(grads), taps=taps),
        in_specs=[scalar, scalar] + whole(len(grads) + 4),
        out_specs=tuple(whole(4)),
        out_shape=(
            jax.ShapeDtypeStruct((full, 3 * channels), BF16),
            jax.ShapeDtypeStruct((full // 2, width), BF16),
            jax.ShapeDtypeStruct((full // 2, width), BF16),
            jax.ShapeDtypeStruct((taps, channels), F32),
        ),
        scratch_shapes=[
            pltpu.VMEM((full + 8, channels), F32),
            pltpu.VMEM((full, channels), F32),
            pltpu.VMEM((full + 8, channels), F32),
        ],
        cost_estimate=pl.CostEstimate(flops=0, transcendentals=0, bytes_accessed=100_000),
        compiler_params=pltpu.CompilerParams(vmem_limit_bytes=VMEM_LIMIT),
        name="conv_backward",
    )(place, bounds, *grads, projected, in_weights, out_weights, kernel)


def conv_forward_kernel(*refs, length, tokens, taps):
    place_ref, bounds_ref = refs[:2]
    token_refs = refs[2 : 2 + tokens]
    (
        in_ref, out_w_ref, tap_ref, gain_ref,
        normed_ref, projected_ref, gated_ref, near_out_ref, far_out_ref, product_ref,
    ) = refs[2 + tokens :]
    place = place_ref[0]
    channels = gated_ref.shape[1]
    product_ref[0:8, :] = jnp.zeros((8, channels), F32)
    for block in range(tokens):
        rows = slice(block * length, (block + 1) * length)
        value = token_refs[block][...].astype(F32)
        scale = lax.rsqrt(jnp.mean(value * value, -1, keepdims=True) + EPS)
        normed = (value * scale * gain_ref[...]).astype(BF16)
        normed_ref[rows, :] = normed
        projected = plain_dot(normed, in_ref[:, : 3 * channels])
        projected_ref[rows, :] = projected
        product = (projected[:, :channels] * projected[:, 2 * channels :]).astype(BF16)
        target = pl.multiple_of(8 + (block ^ place) * length, 8)
        product_ref[pl.ds(target, length), :] = product.astype(F32)
    for block in range(tokens):
        side, side_rows = block_rows(block, tokens, length)
        rows = slice(block * length, (block + 1) * length)
        first = pl.multiple_of((block ^ place) * length, 8)
        window = product_ref[pl.ds(first, length + 8), :]
        token = first + lax.broadcasted_iota(jnp.int32, (length, channels), 0)
        start = row_starts(bounds_ref, token)
        conv = tap_ref[0:1, :] * window[8:, :]
        for tap in range(1, taps):
            moved = window[8 - tap : 8 - tap + length, :]
            moved = jnp.where(token - tap >= start, moved, 0.0)
            conv = conv + tap_ref[tap : tap + 1, :] * moved
        gated = (projected_ref[rows, channels : 2 * channels] * conv).astype(BF16)
        gated_ref[rows, :] = gated
        partial = plain_dot(gated, out_w_ref[...]).astype(BF16)
        (near_out_ref, far_out_ref)[side][side_rows, :] = partial


def conv_forward(place, bounds, tokens, in_weights, out_weights, kernel, gain):
    length, width = tokens[0].shape
    full = len(tokens) * length
    channels = out_weights.shape[0]
    taps = kernel.shape[0]
    scalar = pl.BlockSpec(memory_space=pltpu.SMEM)
    return pl.pallas_call(
        lambda *refs: conv_forward_kernel(*refs, length=length, tokens=len(tokens), taps=taps),
        in_specs=[scalar, scalar] + whole(len(tokens) + 4),
        out_specs=tuple(whole(5)),
        out_shape=(
            jax.ShapeDtypeStruct((full, width), BF16),
            jax.ShapeDtypeStruct((full, 3 * channels), F32),
            jax.ShapeDtypeStruct((full, channels), BF16),
            jax.ShapeDtypeStruct((full // 2, width), BF16),
            jax.ShapeDtypeStruct((full // 2, width), BF16),
        ),
        scratch_shapes=[pltpu.VMEM((full + 8, channels), F32)],
        cost_estimate=pl.CostEstimate(
            flops=4_000_000_000, transcendentals=2_000, bytes_accessed=20_000_000
        ),
        compiler_params=pltpu.CompilerParams(vmem_limit_bytes=VMEM_LIMIT),
        name="conv_forward",
    )(place, bounds, *tokens, in_weights, out_weights, kernel, gain)


def local(
    x_in,
    cu_seqlens,
    positions,
    cotangent,
    w_in,
    conv_w,
    w_out,
    w_gate1,
    w_up1,
    w_down1,
    g_mix1,
    g_ffn1,
    w_q,
    key_projection_weight,
    value_projection_weight,
    w_o,
    g_q,
    g_k,
    w_gate2,
    w_up2,
    w_down2,
    g_attn2,
    g_ffn2,
):
    rows, length, width = x_in.shape
    assert rows == 1
    seq_count = lax.axis_size("seq")
    dp_count = lax.axis_size("dp")
    seq_place = lax.axis_index("seq")
    full = length * seq_count
    channels = width // seq_count
    slots = width // dp_count
    head = g_q.shape[0] * dp_count
    taps = conv_w.shape[0]

    dealt_out, dealt_o = deal_rows(w_out, w_o)
    x_low, dealt_out, dealt_o = tie(x_in.reshape(length, width), dealt_out, dealt_o)
    x_far = far_half(x_low)
    cotangent_low, x_far = tie(cotangent.reshape(length, width), x_far)
    x_blocks = near_blocks(x_low) + near_blocks(x_far)
    cotangent_blocks = near_blocks(cotangent_low) + near_blocks(far_half(cotangent_low))
    head_gains = jnp.pad(jnp.stack([g_q, g_k], 1), ((0, slots - head // dp_count), (0, 0)))
    small = jnp.concatenate(
        [conv_w.T, jnp.stack([g_mix1, g_ffn1, g_attn2, g_ffn2], 1), head_gains], 1
    )
    small = jnp.pad(small, ((0, 0), (0, 128 - small.shape[1])))
    out_piece = pack_piece(dealt_out, channels)
    o_piece = pack_piece(dealt_o, channels)
    mix_block = jnp.concatenate([column_block(w_in, 3), small], 1)
    mix_block, w_gate1, w_up1, w_down1, w_q, key_projection_weight, value_projection_weight = tie(
        mix_block, w_gate1, w_up1, w_down1, w_q, key_projection_weight, value_projection_weight
    )
    hidden = w_gate1.shape[1] // seq_count
    ffn_one = jnp.concatenate(
        [
            column_block(w, 1)
            for w in (
                w_gate1, w_up1, w_down1, w_q, key_projection_weight, value_projection_weight
            )
        ]
        + [o_piece],
        1,
    )
    mix_all, ffn_one = dp_gather_small(mix_block, ffn_one)
    out_all, ffn_one = dp_gather_small(out_piece, ffn_one)
    ffn_one = dp_gather(ffn_one)
    attn_all = ffn_one[:, 3 * hidden :]
    ffn_two = dp_gather(
        jnp.concatenate([column_block(w, 1) for w in (w_gate2, w_up2, w_down2)], 1)
    )
    qkv_width = attn_all.shape[1] - channels
    qkv_block = attn_all[:, :qkv_width]
    o_block = unpack_rows(attn_all[:, qkv_width:], dp_count)
    bounds = cu_seqlens[0]
    place = seq_place.reshape(1).astype(jnp.int32)
    out_block = unpack_rows(out_all, dp_count)
    small_all = mix_all[:, 3 * channels : 3 * channels + 128].astype(F32).T
    kernel = lax.dynamic_slice_in_dim(small_all[:taps], seq_place * channels, channels, 1)
    gain_mix, gain_ffn_one, gain_attn, gain_ffn_two = (small_all[taps + i] for i in range(4))
    head_gains = small_all[taps + 4 : taps + 6].reshape(2, dp_count, slots)
    head_gains = jnp.tile(head_gains[:, :, : head // dp_count].reshape(2, head), (1, 2))

    x_flat = x_in.reshape(length, width).astype(F32)
    normed_one, projected, gated, near_out, far_out = conv_forward(
        place, bounds, x_blocks, mix_all, out_block, kernel, gain_mix[None, :]
    )
    near_out, late_bounds, *cotangent_blocks = tie(near_out, bounds, *cotangent_blocks)
    order = jnp.arange(full, dtype=jnp.int32)
    starts = doc_starts(late_bounds, order)
    cosine, sine = rope_tables(order - starts, head)
    mixed, cosine, sine = seq_scatter(near_out, far_out, cosine, sine)
    hidden_one = x_flat + mixed
    starts = starts[None, :]

    unit_two, scale_two = unit_scale(hidden_one)
    near_two = (unit_two * gain_ffn_one).astype(BF16)
    far_two = far_half(near_two)
    blocks_two = near_blocks(near_two) + near_blocks(far_two)
    terms_one, partial_one = ffn_forward(blocks_two, ffn_one, hidden)
    mixed, qkv_block, o_block = seq_scatter(*halves_of(partial_one), qkv_block, o_block)
    hidden_two = hidden_one + mixed

    unit_three, scale_three = unit_scale(hidden_two)
    near_three = (unit_three * gain_attn).astype(BF16)
    blocks_three = near_blocks(near_three) + near_blocks(far_half(near_three))
    kv_width = (qkv_width - channels) // 2
    raw, attended_low, wide, totals, near_out, far_out = attention_forward(
        place, blocks_three, qkv_block, o_block, cosine, sine, starts, head_gains
    )
    hidden_three = hidden_two + seq_scatter(near_out, far_out)

    unit_four, scale_four = unit_scale(hidden_three)
    near_four = (unit_four * gain_ffn_two).astype(BF16)
    far_four = far_half(near_four)
    near_four = near_blocks(near_four)
    half = len(near_four)
    kept_two, near_out = ffn_turn(
        near_four, cotangent_blocks[:half], ffn_two, hidden, 0, None
    )
    far_four, near_out = tie(far_four, near_out)
    far_four = near_blocks(far_four)
    kept_two, far_out = ffn_turn(
        far_four, cotangent_blocks[half:], ffn_two, hidden, 1, kept_two
    )

    grad_four = cotangent.reshape(length, width).astype(F32)
    kept_two, far_out = tie(kept_two, far_out)
    normed_four = jnp.concatenate(near_four + far_four, 0)
    d_gate_up = left_dot(normed_four, kept_two[:, : 2 * hidden]).astype(BF16)
    d_ffn_in, d_gate_up = seq_scatter(near_out, far_out, d_gate_up)
    d_hidden, d_gain_ffn_two = norm_back(d_ffn_in, gain_ffn_two, unit_four, scale_four)
    grad_three = grad_four + d_hidden

    grad_attn = grad_three.astype(BF16)
    far_attn = far_half(grad_attn)
    d_down = left_dot(jnp.concatenate(cotangent_blocks, 0), kept_two[:, 2 * hidden :])
    grads_two = jnp.concatenate([d_gate_up, d_down.astype(BF16)], 1)
    far_attn, grads_two = tie(far_attn, grads_two)
    owned_two = dp_scatter(grads_two)
    grad_blocks = near_blocks(grad_attn) + near_blocks(far_attn)
    d_raw, near_out, far_out, d_head_gains = attention_backward(
        place, grad_blocks, qkv_block, o_block, cosine, sine, starts, head_gains,
        raw, wide, totals,
    )
    d_head_gains = d_head_gains[:, :head] + d_head_gains[:, head:]
    d_qkv = left_dot(jnp.concatenate(blocks_three, 0), d_raw)
    d_w_o = left_dot(attended_low, jnp.concatenate(grad_blocks, 0))
    d_w_o = pack_rows(d_w_o.astype(BF16), dp_count)
    d_attn_in, *grads_attn = seq_scatter(near_out, far_out, d_qkv.astype(BF16), d_w_o)
    d_attn_h, d_gain_attn = norm_back(d_attn_in, gain_attn, unit_three, scale_three)
    grad_two = grad_three + d_attn_h

    near_grad = grad_two.astype(BF16)
    far_grad = far_half(near_grad)
    near_grad = near_blocks(near_grad)
    kept_one, near_out = ffn_backward(near_grad, terms_one, ffn_one, hidden, 0, None)
    far_grad, near_out = tie(far_grad, near_out)
    far_grad = near_blocks(far_grad)
    kept_one, far_out = ffn_backward(far_grad, terms_one, ffn_one, hidden, 1, kept_one)
    kept_one, far_out = tie(kept_one, far_out)
    d_gate_up = left_dot(jnp.concatenate(blocks_two, 0), kept_one).astype(BF16)
    d_ffn_in_one, d_gate_up = seq_scatter(near_out, far_out, d_gate_up)
    owned_one = dp_scatter(jnp.concatenate([d_gate_up, *grads_attn], 1))
    d_hidden_one, d_gain_ffn_one = norm_back(d_ffn_in_one, gain_ffn_one, unit_two, scale_two)
    grad_one = grad_two + d_hidden_one

    grad_mix = grad_one.astype(BF16)
    far_mix = far_half(grad_mix)
    d_down = left_dot(
        jnp.concatenate(near_grad + far_grad, 0), terms_one[:, 2 * hidden :]
    ).astype(BF16)
    far_mix, d_down = tie(far_mix, d_down)
    mix_blocks = near_blocks(grad_mix) + near_blocks(far_mix)
    mix_blocks[-1], owned_two = tie(mix_blocks[-1], owned_two)
    d_projected, near_out, far_out, kernel_grads = conv_backward(
        place, bounds, mix_blocks, projected, mix_all, out_block, kernel
    )
    d_w_in = left_dot(normed_one, d_projected)
    d_w_out = left_dot(gated, jnp.concatenate(mix_blocks, 0))
    grads_mix = jnp.concatenate(
        [d_down, d_w_in.astype(BF16), pack_rows(d_w_out.astype(BF16), dp_count)], 1
    )
    kept_mix, sent_mix = dp_pair_parts(grads_mix)
    sent_mix, kept_two = tie(sent_mix, kept_two)
    d_normed = seq_scatter(near_out, far_out)
    unit_one, scale_one = unit_scale(x_flat)
    d_x_part, d_gain_mix = norm_back(d_normed, gain_mix, unit_one, scale_one)
    d_x = (grad_one + d_x_part).reshape(rows, length, width)

    kernel_wide = lax.dynamic_update_slice_in_dim(
        jnp.zeros((taps, width), F32), kernel_grads, seq_place * channels, 1
    )
    head_wide = jnp.pad(
        d_head_gains.reshape(2, dp_count, -1),
        ((0, 0), (0, 0), (0, slots - head // dp_count)),
    ).reshape(2, width)
    vectors = jnp.concatenate(
        [
            jnp.stack([d_gain_mix, d_gain_ffn_one, d_gain_attn, d_gain_ffn_two]),
            kernel_wide,
            head_wide,
        ],
        0,
    )
    vector_columns = jnp.pad(vectors.T, ((0, 0), (0, 128 - vectors.shape[0])))
    owned_vectors = dp_scatter_small(vector_columns.astype(BF16))

    def redeal(block):
        return pack_piece(undeal_rows(unpack_piece(block, width)), channels)

    ffn_out = right_dot(kept_two[:, 2 * hidden :], ffn_two[:, 2 * hidden :])
    hidden_four = hidden_three + seq_scatter(*halves_of(ffn_out))
    out = hidden_four.astype(BF16).reshape(rows, length, width)
    shared_two = share(owned_two)
    owned_mix, (out, d_x, *shared_two), owned_one = dp_scatter_pairs(
        kept_mix, sent_mix, (out, d_x, *shared_two), owned_one
    )
    d_wgate_two, d_wup_two, d_down_two = assemble(
        place, shared_two, [(n * hidden, hidden, 1, False) for n in range(3)]
    )
    tasks = [(n * hidden, hidden, 1, False) for n in range(2)]
    for columns in (channels, kv_width, kv_width):
        tasks.append((tasks[-1][0] + tasks[-1][1], columns, 1, False))
    d_wgate_one, d_wup_one, d_w_q, d_w_k, d_w_v = assemble(
        place, share(owned_one[:, :-channels]), tasks
    )
    (d_w_o_full,) = assemble(
        place, share(redeal(owned_one[:, -channels:])), [(0, channels, 1, True)]
    )
    shared_vectors = share(owned_vectors)
    owned_mix, d_wgate_one, d_w_o_full, d_wgate_two, *shared_vectors = tie(
        owned_mix, d_wgate_one, d_w_o_full, d_wgate_two, *shared_vectors
    )
    shared_mix = share(owned_mix[:, :-channels])
    shared_out = share(redeal(owned_mix[:, -channels:]))
    d_down_one, d_w_in_full = assemble(
        place, shared_mix, [(0, hidden, 1, False), (hidden, 3 * channels, 3, False)]
    )
    (d_w_out_full,) = assemble(place, shared_out, [(0, channels, 1, True)])
    sums = sum(block.astype(F32) for block in shared_vectors).T
    small_head = head // dp_count
    return (
        out,
        d_x,
        d_w_in_full,
        sums[4 : 4 + taps],
        d_w_out_full,
        d_wgate_one,
        d_wup_one,
        d_down_one,
        sums[0],
        sums[1],
        d_w_q,
        d_w_k,
        d_w_v,
        d_w_o_full,
        sums[4 + taps, :small_head],
        sums[5 + taps, :small_head],
        d_wgate_two,
        d_wup_two,
        d_down_two,
        sums[2],
        sums[3],
    )


def solution(mesh):
    matrix = P("dp", None)
    vector = P("dp")
    tokens = P("dp", "seq", None)
    kernel = P(None, "dp")
    in_specs = (
        (tokens, matrix, P("dp", "seq"), tokens, matrix, kernel)
        + (matrix,) * 4
        + (vector,) * 2
        + (matrix,) * 4
        + (vector,) * 2
        + (matrix,) * 3
        + (vector,) * 2
    )
    out_specs = (
        (tokens, tokens, matrix, kernel)
        + (matrix,) * 4
        + (vector,) * 2
        + (matrix,) * 4
        + (vector,) * 2
        + (matrix,) * 3
        + (vector,) * 2
    )
    return jax.shard_map(local, mesh=mesh, in_specs=in_specs, out_specs=out_specs, check_vma=False)
```
